32 devices in a mesh: seq: 4 (over z), shard: 8 (over y, x, core).
Axes of the slice: x: 2, y: 2, z: 4, core: 2. Of those that a mesh axis runs over, the one named last changes fastest.
Arguments:
- hidden_in: bfloat16 [8192, 512], P(('shard', 'seq')), may hold values from -6 to 6
- encoder: bfloat16 [2048, 512], P(('shard', 'seq')), may hold values from -6 to 6
- segment_ids: int32 [8192], replicated, may hold values from 0 to 1, never falling along the last dimension, each value on 1 to 5120 neighbouring positions
- timestep: int32 [2], replicated, may hold values from 0 to 49
- out_grad: bfloat16 [8192, 512], P(('shard', 'seq')), may hold values from -6 to 6
- time_table: bfloat16 [50, 512], P(None, 'shard'), may hold values from -6 to 6
- norm_gain: bfloat16 [3, 512], P(None, 'shard'), may hold values from 0.5 to 1.5
- norm_bias: bfloat16 [3, 512], P(None, 'shard'), may hold values from -1.5 to 1.5
- self_proj: bfloat16 [512, 1536], P('shard'), may hold values from -0.25 to 0.25
- self_out: bfloat16 [512, 512], P('shard'), may hold values from -1 to 1
- cross_query: bfloat16 [512, 512], P('shard'), may hold values from -0.25 to 0.25
- cross_memory: bfloat16 [512, 1024], P('shard'), may hold values from -0.25 to 0.25
- cross_out: bfloat16 [512, 512], P('shard'), may hold values from -1 to 1
- up_weight: bfloat16 [512, 2048], P('shard'), may hold values from -0.25 to 0.25
- up_bias: bfloat16 [2048], P('shard'), may hold values from -2.5 to 2.5
- down_weight: bfloat16 [2048, 512], P('shard'), may hold values from -0.125 to 0.125
- down_bias: bfloat16 [512], P('shard'), may hold values from -1.5 to 1.5
Outputs:
- layer_out: bfloat16 [8192, 512], P(('shard', 'seq'))
- hidden_grad: float32 [8192, 512], P(('shard', 'seq'))
- encoder_grad: float32 [2048, 512], P(('shard', 'seq'))
- time_grad: float32 [50, 512], P(None, 'shard')
- gain_grad: float32 [3, 512], P(None, 'shard')
- bias_grad: float32 [3, 512], P(None, 'shard')
- proj_grad: float32 [512, 1536], P('shard')
- self_out_grad: float32 [512, 512], P('shard')
- query_grad: float32 [512, 512], P('shard')
- memory_grad: float32 [512, 1024], P('shard')
- cross_out_grad: float32 [512, 512], P('shard')
- up_weight_grad: float32 [512, 2048], P('shard')
- up_bias_grad: float32 [2048], P('shard')
- down_weight_grad: float32 [2048, 512], P('shard')
- down_bias_grad: float32 [512], P('shard')
The draws below stay inside these ranges and needn't reach their ends.
Inputs may be any that keep to these rules, and one draw needn't show every extreme that they name: `segment_ids`: never falling; 2 sequences of 1 to 5120 tokens each.
All inputs are finite; a program needn't handle non-finite values.
Results may differ from the reference program's by a relative error of at most 0.023.
Values may be sent and summed in bfloat16 or wider, within the bound.
A program may use at most 256 MiB of HBM per device.

```python
import math
import jax
import jax.numpy as jnp
import numpy as np
from jax import lax

D = 512
H = 8
FF = 2048
HD = 64
DOCS = 2
ENC = 1024
STEPS = 50
TOKENS = 8192
MOST = 5120
ENCTOK = 2048


def raised(values, key, source, target, blocks, factor):
    def block_of(dim):
        return (jnp.arange(values.shape[dim]) // (values.shape[dim] // blocks)).reshape((-1,) + (1,) * (values.ndim - 1 - dim))

    first = jax.random.permutation(key, blocks)[block_of(target)]
    second = (block_of(target) + blocks // 2) % blocks
    return jnp.where((block_of(source) == first) | (block_of(source) == second), factor * values, values)


def steps_of(key, shape, cuts, least, high):
    def one(position, shards_of):
        steps = jax.random.uniform(jax.random.fold_in(jax.random.fold_in(key, 6), position), (shards_of,), jnp.float32, least / len(cuts), high / len(cuts))
        return jnp.repeat(jnp.exp(steps), shape[position] // shards_of).reshape((-1,) + (1,) * (len(shape) - position - 1))

    factor_of = one(*cuts[0])
    for cut in cuts[1:]:
        factor_of = factor_of * one(*cut)
    return factor_of


def profile(amount, total, bound, skew):
    portions = [(1 << 20) // math.isqrt(rank ** skew) + 1 for rank in range(2, amount + 1)]
    surplus, holding = total - bound - (amount - 1), [1] * (amount - 1)
    while surplus > 0:
        free = [i for i in range(amount - 1) if holding[i] < bound]
        pool, budget = sum([portions[i] for i in free]), surplus
        for i in free:
            more = min(bound - holding[i], max(1, budget * portions[i] // pool), surplus)
            holding[i] = holding[i] + more
            surplus = surplus - more
    return np.array([bound] + holding)


def ragged_sizes(key, number_of, total, limit, slope):
    if number_of == 2:
        one = jax.random.randint(key, (), max(1, total - limit), min(limit, total - 1) + 1)
        return jnp.stack([one, total - one])
    sizes = jnp.asarray(profile(number_of, total, limit, slope), jnp.int32)
    twos = (number_of - 1) // 2
    giver, sink = sizes[1:1 + 2 * twos:2], sizes[2:2 + 2 * twos:2]
    slack = jnp.minimum(giver - 1, limit - sink)
    moved = jax.random.randint(jax.random.fold_in(key, 1), (twos,), 0, 1 << 20) % (slack + 1)
    sizes = sizes.at[1:1 + 2 * twos:2].set(giver - moved).at[2:2 + 2 * twos:2].set(sink + moved)
    return sizes[jax.random.permutation(jax.random.fold_in(key, 2), number_of)]


def centred(own_key, shape, width, bound, shards=(), kind=jnp.bfloat16):
    array = width * jax.random.normal(own_key, shape, jnp.float32)
    if shards:
        array = array * steps_of(own_key, shape, shards, -0.22, 0.18)
    return jnp.clip(array, -bound, bound).astype(kind)


def gaussian_with(rng, dims, scale, limit, split, heavy, held_as=jnp.bfloat16):
    array = scale * jax.random.normal(rng, dims, jnp.float32)
    if split:
        array = array * steps_of(rng, dims, split, -0.22, 0.18)
    return jnp.clip(raised(array, jax.random.fold_in(rng, 3), *heavy), -limit, limit).astype(held_as)


def setup_inputs(seed: int = 0) -> dict:
    arg_keys = jax.random.split(jax.random.key(seed), 18)
    return {
        "hidden_in": gaussian_with(arg_keys[0], (TOKENS, D), 1.0, 6.0, ((0, 32),), (0, 1, 32, 2.75)),
        "encoder": centred(arg_keys[1], (ENCTOK, D), 1.0, 6.0, ((0, 32),)),
        "segment_ids": jnp.searchsorted(jnp.cumsum(ragged_sizes(arg_keys[2], DOCS, TOKENS, MOST, 0)), jnp.arange(TOKENS), side="right").astype(jnp.int32),
        "timestep": jax.random.randint(arg_keys[3], (DOCS,), 0, STEPS).astype(jnp.int32),
        "out_grad": gaussian_with(arg_keys[4], (TOKENS, D), 1.0, 6.0, ((0, 32),), (0, 1, 32, 2.75)),
        "time_table": centred(arg_keys[5], (STEPS, D), 1.0, 6.0, ((1, 8),)),
        "norm_gain": jnp.clip(1.0 + 0.1 * jax.random.normal(arg_keys[6], (3, D), jnp.float32), 0.5, 1.5).astype(jnp.bfloat16),
        "norm_bias": centred(arg_keys[7], (3, D), 0.3, 1.5, ((1, 8),)),
        "self_proj": centred(arg_keys[8], (D, 3 * D), D ** -0.5, 0.25, ((0, 8),)),
        "self_out": centred(arg_keys[9], (D, D), (D // 16) ** -0.5, 1.0, ((0, 8),)),
        "cross_query": centred(arg_keys[10], (D, D), D ** -0.5, 0.25, ((0, 8),)),
        "cross_memory": centred(arg_keys[11], (D, 2 * D), D ** -0.5, 0.25, ((0, 8),)),
        "cross_out": centred(arg_keys[12], (D, D), (D // 16) ** -0.5, 1.0, ((0, 8),)),
        "up_weight": centred(arg_keys[13], (D, FF), D ** -0.5, 0.25, ((0, 8),)),
        "up_bias": centred(arg_keys[14], (FF,), 0.5, 2.5, ((0, 8),)),
        "down_weight": centred(arg_keys[15], (FF, D), FF ** -0.5, 0.125, ((0, 8),)),
        "down_bias": centred(arg_keys[16], (D,), 0.3, 1.5, ((0, 8),)),
    }


@jax.custom_vjp
def low(v):
    return lax.optimization_barrier(v.astype(jnp.bfloat16)).astype(jnp.float32)

@jax.custom_vjp
def low_back(v):
    return v

def low_keep(v):
    return (low(v), None)

def low_pass(kept, grad):
    return (grad,)

def back_keep(v):
    return (v, None)

def back_low(kept, grad):
    return (low(grad),)
low.defvjp(low_keep, low_pass)
low_back.defvjp(back_keep, back_low)
highest = lax.Precision.HIGHEST
norm_eps = 1e-05
masked_score = -1e+30

def product(left, right):
    return jnp.dot(left, right, precision=highest, preferred_element_type=jnp.float32)

def layer_norm(value, gain, shift):
    center = lax.optimization_barrier(jnp.mean(value, axis=-1, keepdims=True))
    offset = value - center
    spread = lax.optimization_barrier(jnp.mean(offset * offset, axis=-1, keepdims=True))
    return offset * lax.rsqrt(spread + norm_eps) * gain + shift

def softmax_rows(scores):
    shifted = scores - lax.optimization_barrier(jnp.max(scores, axis=-1, keepdims=True))
    powers = jnp.exp(shifted)
    return powers / lax.optimization_barrier(jnp.sum(powers, axis=-1, keepdims=True))

def self_attention(queries, key_rows, value_rows, segment_ids):
    total_rows = queries.shape[0]
    block_rows = min(1024, total_rows)
    window = min(total_rows, MOST + block_rows)

    def one_block(block_index):
        first_row = block_index * block_rows
        begin_row = jnp.clip(first_row + block_rows - window, 0, total_rows - window).astype(jnp.int32)
        query_block = lax.dynamic_slice_in_dim(queries, first_row, block_rows, 0)
        key_block = lax.dynamic_slice_in_dim(key_rows, begin_row, window, 0)
        value_block = lax.dynamic_slice_in_dim(value_rows, begin_row, window, 0)
        query_seg = lax.dynamic_slice_in_dim(segment_ids, first_row, block_rows, 0)
        key_seg = lax.dynamic_slice_in_dim(segment_ids, begin_row, window, 0)
        query_pos = first_row + jnp.arange(block_rows, dtype=jnp.int32)
        key_pos = begin_row + jnp.arange(window, dtype=jnp.int32)
        allowed = (query_seg[:, None] == key_seg[None, :]) & (key_pos[None, :] <= query_pos[:, None])
        raw_scores = jnp.einsum('qhd,khd->hqk', query_block, key_block, precision=highest)
        scores = jnp.where(allowed[None], HD ** (-0.5) * low_back(raw_scores), masked_score)
        attn_probs = low(softmax_rows(scores))
        return jnp.einsum('hqk,khd->qhd', attn_probs, value_block, precision=highest)
    blocks = lax.map(jax.checkpoint(one_block), jnp.arange(total_rows // block_rows, dtype=jnp.int32))
    return blocks.reshape(total_rows, H * HD)

def cross_attention(queries, key_rows, value_rows, segment_ids):
    total_rows = queries.shape[0]
    block_rows = min(1024, total_rows)
    key_doc = jnp.arange(key_rows.shape[0], dtype=jnp.int32) // ENC

    def one_block(block_index):
        first_row = block_index * block_rows
        query_block = lax.dynamic_slice_in_dim(queries, first_row, block_rows, 0)
        query_seg = lax.dynamic_slice_in_dim(segment_ids, first_row, block_rows, 0)
        allowed = query_seg[:, None] == key_doc[None, :]
        raw_scores = jnp.einsum('qhd,khd->hqk', query_block, key_rows, precision=highest)
        scores = jnp.where(allowed[None], HD ** (-0.5) * low_back(raw_scores), masked_score)
        attn_probs = low(softmax_rows(scores))
        return jnp.einsum('hqk,khd->qhd', attn_probs, value_rows, precision=highest)
    blocks = lax.map(jax.checkpoint(one_block), jnp.arange(total_rows // block_rows, dtype=jnp.int32))
    return blocks.reshape(total_rows, H * HD)

def forward(hidden_in, encoder, time_table, norm_gain, norm_bias, self_proj, self_out, cross_query, cross_memory, cross_out, up_weight, up_bias, down_weight, down_bias, segment_ids, timestep):
    total_rows = hidden_in.shape[0]
    embedded = hidden_in + time_table[timestep][segment_ids]
    normed_one = low(layer_norm(embedded, norm_gain[0], norm_bias[0]))
    qkv = low(low_back(product(normed_one, self_proj))).reshape(total_rows, 3, H, HD)
    attn = low(low_back(self_attention(qkv[:, 0], qkv[:, 1], qkv[:, 2], segment_ids)))
    after = embedded + low_back(product(attn, self_out))
    normed_two = low(layer_norm(after, norm_gain[1], norm_bias[1]))
    cross_q = low(low_back(product(normed_two, cross_query))).reshape(total_rows, H, HD)
    memory = low(low_back(product(encoder, cross_memory))).reshape(encoder.shape[0], 2, H, HD)
    cross = low(low_back(cross_attention(cross_q, memory[:, 0], memory[:, 1], segment_ids)))
    after_two = after + low_back(product(cross, cross_out))
    normed_three = low(layer_norm(after_two, norm_gain[2], norm_bias[2]))
    pre_act = low_back(product(normed_three, up_weight) + up_bias)
    middle = low(jax.nn.gelu(pre_act, approximate=False))
    return after_two + low_back(product(middle, down_weight) + down_bias)

def reference(hidden_in, encoder, segment_ids, timestep, out_grad, time_table, norm_gain, norm_bias, self_proj, self_out, cross_query, cross_memory, cross_out, up_weight, up_bias, down_weight, down_bias):
    floats = [value.astype(jnp.float32) for value in (hidden_in, encoder, time_table, norm_gain, norm_bias, self_proj, self_out, cross_query, cross_memory, cross_out, up_weight, up_bias, down_weight, down_bias)]

    def closed(*params):
        return forward(*params, segment_ids, timestep)
    result, pullback = jax.vjp(closed, *floats)
    grads = pullback(out_grad.astype(jnp.float32))
    return (result.astype(jnp.bfloat16), grads[0], grads[1], grads[2], grads[3], grads[4], grads[5], grads[6], grads[7], grads[8], grads[9], grads[10], grads[11], grads[12], grads[13])
```

```python
import functools

import jax
import jax.numpy as jnp
from jax import lax
from jax.experimental import pallas as pl
from jax.experimental.pallas import tpu as pltpu
from jax.sharding import PartitionSpec as P

H = 8
HD = 64
DOCS = 2
ENC = 1024
EPS = 1e-05
MASKED = -1e30
SCALE = HD**-0.5
MESH = pl.DeviceIdType.MESH
BF = jnp.bfloat16
F32 = jnp.float32
DMA = pltpu.SemaphoreType.DMA
ORDER = (0, 1, 2, 4, 3, 6, 5, 7)


def mm(a, b, ca=1, cb=0):
    return lax.dot_general(a, b, (((ca,), (cb,)), ((), ())), preferred_element_type=F32)


def flip(j, bits):
    low, mid, high = j % 2, (j // 2) % 2, (j // 4) % 2
    out = j
    if bits & 1:
        out = out + 1 - 2 * low
    if bits & 2:
        out = out + 2 - 4 * mid
    if bits & 4:
        out = out + 4 - 8 * high
    return out


def rcopy(src, dst, send_sem, recv_sem, device_id):
    return pltpu.make_async_remote_copy(
        src_ref=src,
        dst_ref=dst,
        send_sem=send_sem,
        recv_sem=recv_sem,
        device_id=device_id,
        device_id_type=MESH,
    )


def place():
    shard, seq = lax.axis_index("shard"), lax.axis_index("seq")
    return shard, seq, shard % 8, shard // 8


def greet(peers):
    barrier = pltpu.get_barrier_semaphore()
    count = 0
    for condition, device in peers:
        if condition is None:
            pl.semaphore_signal(barrier, inc=1, device_id=device, device_id_type=MESH)
            count = count + 1
        else:

            @pl.when(condition)
            def _(device=device):
                pl.semaphore_signal(barrier, inc=1, device_id=device, device_id_type=MESH)

            count = count + jnp.where(condition, 1, 0)
    pl.semaphore_wait(barrier, count)


def norm_stats(value):
    center = jnp.mean(value, axis=1, keepdims=True)
    offset = value - center
    spread = jnp.mean(offset * offset, axis=1, keepdims=True)
    scale = lax.rsqrt(spread + EPS)
    return offset * scale, scale


def norm_back(d_out, hat, scale, gain):
    d_hat = d_out * gain
    first = jnp.mean(d_hat, axis=1, keepdims=True)
    second = jnp.mean(d_hat * hat, axis=1, keepdims=True)
    d_in = scale * (d_hat - first - hat * second)
    return d_in, jnp.sum(d_out * hat, axis=0, keepdims=True), jnp.sum(d_out, axis=0, keepdims=True)


def embed(hid_ref, bound, vecs_ref, block):
    rows = hid_ref.shape[0]
    pos = block * rows + lax.broadcasted_iota(jnp.int32, (rows, 1), 0)
    picked = jnp.where(pos < bound, vecs_ref[0:1, :], vecs_ref[1:2, :])
    return hid_ref[...].astype(F32) + picked


def gather_kernel(
    S, Z, G, bnd, hid, small, wproj, wmem, enc, *rest
):
    W = 5
    weights = (wproj, wmem) + rest[:W]
    rest = rest[W:]
    x_all, kv, qt, mkv, enc_all, small_all, vecs = rest[:7]
    full = rest[7:14]
    (wsend, msend, w_all, m_all, sm_s, sm_r, w_s, w_r, mw_s, mw_r, x_s, x_r, e_s, e_r, z_s, z_r,
     mb_s, mb_r, g_s, g_f, g_r, l_s) = rest[14:]
    s, z, j, m = place()
    R = wproj.shape[0]
    T = hid.shape[0]
    bound = bnd[0]
    chips = S // 2
    core, chip = s % 2, s // 2
    sib = s + 1 - 2 * core

    greet(
        [(None, {"shard": (s + d) % S}) for d in range(1, S)]
        + [(z > 0, {"seq": z - 1}), (z < Z - 1, {"seq": z + 1})]
    )

    small_all[s] = small[...]
    small_copies = []
    for d in range(1, S):
        c = rcopy(small, small_all.at[s], sm_s.at[d], sm_r.at[s], {"shard": (s + d) % S})
        c.start()
        small_copies.append(c)
    for h in range(H):
        k = wproj[:, 512 + HD * h : 512 + HD * (h + 1)]
        v = wproj[:, 1024 + HD * h : 1024 + HD * (h + 1)]
        q = wproj[:, HD * h : HD * (h + 1)]
        wsend[h] = jnp.concatenate([k, v, q, jnp.zeros_like(q)], axis=1)
        msend[h] = jnp.concatenate(
            [wmem[:, HD * h : HD * (h + 1)], wmem[:, 512 + HD * h : 512 + HD * (h + 1)]], axis=1
        )
    w_all[s] = wsend[j]
    m_all[s] = msend[j]
    w_copies = []
    for d in range(1, S):
        p = (s + d) % S
        c = rcopy(wsend.at[p % 8], w_all.at[s], w_s.at[d], w_r.at[s], {"shard": p})
        c.start()
        w_copies.append(c)
        c = rcopy(msend.at[p % 8], m_all.at[s], mw_s.at[d], mw_r.at[s], {"shard": p})
        c.start()
        w_copies.append(c)
    for d in range(1, S):
        p = (s + d) % S
        rcopy(small, small_all.at[p], sm_s.at[d], sm_r.at[p], {"shard": p}).wait_recv()
    rows = jnp.zeros((16, 512), F32)
    for p in range(S):
        lane = lax.broadcasted_iota(jnp.int32, (256, 512), 0)
        col = lax.broadcasted_iota(jnp.int32, (256, 512), 1)
        pick = ((col - p * R) == lane) & (lane < R)
        rows = rows + mm(small_all[p], jnp.where(pick, 1.0, 0.0).astype(BF))
    vecs[...] = rows

    hat, _ = norm_stats(embed(hid, bound, vecs, s * Z + z))
    x_all[j] = (hat * vecs[2:3, :] + vecs[5:6, :]).astype(BF)
    enc_all[j] = enc[...]
    copies = []

    def send_block(ref, bits_source, bits_target, send, recv):
        source = flip(j, bits_source)
        c = rcopy(ref.at[source], ref.at[source], send, recv.at[source], {"shard": flip(s, bits_target)})
        c.start()
        copies.append(c)

    def wait_block(ref, bits, recv):
        source = flip(j, bits)
        rcopy(ref.at[source], ref.at[source], x_s.at[0], recv.at[source], {"shard": sib}).wait_recv()

    for n, bits in enumerate((1, 2, 4, 6)):
        send_block(x_all, 0, bits, x_s.at[n], x_r)
    for n, bits in enumerate((1, 2, 4, 6)):
        send_block(enc_all, 0, bits, e_s.at[n], e_r)
    for d in range(1, S):
        p = (s + d) % S
        rcopy(wsend.at[0], w_all.at[p], w_s.at[d], w_r.at[p], {"shard": p}).wait_recv()
        rcopy(msend.at[0], m_all.at[p], mw_s.at[d], mw_r.at[p], {"shard": p}).wait_recv()
    w_head = w_all[...].reshape(S * R, 256)
    m_head = m_all[...].reshape(S * R, 128)

    def z_copy(ref, block, plane, step, hop, slot):
        return rcopy(
            ref.at[:, block, plane] if block is not None else ref.at[:, :, plane],
            ref.at[:, block, plane] if block is not None else ref.at[:, :, plane],
            z_s.at[(step + 1) // 2, hop, slot],
            z_r.at[(step + 1) // 2, hop, slot],
            {"seq": z + step},
        )

    def z_send(ref, block, hop, slot):
        for step in (-1, 1):
            origin = z - step * hop
            ok = (z + step >= 0) & (z + step < Z) & (origin >= 0) & (origin < Z)

            @pl.when(ok)
            def _(step=step, origin=origin):
                z_copy(ref, block, origin, step, hop, slot).start()

    def z_recv(ref, block, hop, slot):
        for step in (-1, 1):
            origin = z - step * hop
            ok = (origin >= 0) & (origin < Z)

            @pl.when(ok)
            def _(step=step, origin=origin):
                z_copy(ref, block, origin, step, hop - 1, slot).wait_recv()

    def z_drain(ref, block, hop, slot):
        for step in (-1, 1):
            origin = z - step * hop
            ok = (z + step >= 0) & (z + step < Z) & (origin >= 0) & (origin < Z)

            @pl.when(ok)
            def _(step=step, origin=origin):
                z_copy(ref, block, origin, step, hop, slot).wait_send()

    def member_copy(ref, block, d, slot, mine):
        other = (m + d) % G
        at = m if mine else other
        view = ref.at[at, block, z] if block is not None else ref.at[at, :, z]
        return rcopy(view, view, mb_s.at[d, slot], mb_r.at[at, slot], {"shard": other * 8 + j})

    def spread(ref, block, slot):
        for d in range(1, G):
            member_copy(ref, block, d, slot, True).start()
        for d in range(1, G):
            member_copy(ref, block, d, slot, False).wait_recv()
        z_send(ref, block, 0, slot)

    for n, bits in enumerate(ORDER):
        block = flip(j, bits)
        if bits:
            wait_block(x_all, bits, x_r)
            if bits in (2, 4, 6):
                send_block(x_all, bits, 1, x_s.at[3 + bits // 2], x_r)
        kvq = mm(x_all[block], w_head)
        kv[m, block, z] = kvq[:, :128].astype(BF)
        spread(kv, block, n)
        qt[block] = (SCALE * kvq[:, 128:256].T[:HD]).astype(BF)

    for bits in (2, 4, 6):
        wait_block(enc_all, bits, e_r)
        send_block(enc_all, bits, 1, e_s.at[3 + bits // 2], e_r)
    for bits in (1, 3, 5, 7):
        wait_block(enc_all, bits, e_r)
    E = enc.shape[0]
    for b in range(8):
        mkv[m, b, z] = mm(enc_all[b], m_head).astype(BF)
    spread(mkv, None, 8)

    for a, (shard, whole) in enumerate(zip(weights, full)):
        pltpu.make_async_copy(shard, whole.at[s], l_s.at[a]).start()
        for d in range(1, chips):
            p = ((chip + d) % chips) * 2 + core
            rcopy(shard, whole.at[s], g_s.at[a, d], g_r.at[a, s], {"shard": p}).start()
        rcopy(shard, whole.at[s], g_s.at[a, 0], g_r.at[a, s], {"shard": sib}).start()

    for hop in range(1, Z):
        for n, bits in enumerate(ORDER):
            z_recv(kv, flip(j, bits), hop, n)
            z_send(kv, flip(j, bits), hop, n)
        z_recv(mkv, None, hop, 8)
        z_send(mkv, None, hop, 8)

    for a, (shard, whole) in enumerate(zip(weights, full)):
        for d in range(1, chips):
            q = ((chip + chips - d) % chips) * 2 + core
            rcopy(shard, whole.at[q], g_s.at[a, d], g_r.at[a, q], {"shard": sib}).wait_recv()
            rcopy(whole.at[q], whole.at[q], g_f.at[a, d], g_r.at[a, q], {"shard": sib}).start()
    for a, (shard, whole) in enumerate(zip(weights, full)):
        rcopy(shard, whole.at[sib], g_s.at[a, 0], g_r.at[a, sib], {"shard": sib}).wait_recv()
        for d in range(1, chips):
            q = ((chip + chips - d) % chips) * 2 + 1 - core
            rcopy(shard, whole.at[q], g_s.at[a, d], g_r.at[a, q], {"shard": sib}).wait_recv()
        pltpu.make_async_copy(shard, whole.at[s], l_s.at[a]).wait()
        for d in range(chips):
            rcopy(shard, whole.at[s], g_s.at[a, d], g_r.at[a, s], {"shard": sib}).wait_send()
        for d in range(1, chips):
            q = ((chip + chips - d) % chips) * 2 + core
            rcopy(whole.at[q], whole.at[q], g_f.at[a, d], g_r.at[a, q], {"shard": sib}).wait_send()
    for c in small_copies + w_copies + copies:
        c.wait_send()
    for n, bits in enumerate(ORDER):
        for d in range(1, G):
            member_copy(kv, flip(j, bits), d, n, True).wait_send()
        for hop in range(Z - 1):
            z_drain(kv, flip(j, bits), hop, n)
    for d in range(1, G):
        member_copy(mkv, None, d, 8, True).wait_send()
    for hop in range(Z - 1):
        z_drain(mkv, None, hop, 8)


def gather_call(S, Z, bnd, hid, small, wproj, wmem, enc, wout, wcq, wco, wup, wdn):
    G = S // 8
    T, R, E = hid.shape[0], wproj.shape[0], enc.shape[0]
    weights = (wproj, wmem, wout, wcq, wco, wup, wdn)
    vmem = pl.BlockSpec(memory_space=pltpu.VMEM)
    hbm = pl.BlockSpec(memory_space=pl.ANY)
    sds = jax.ShapeDtypeStruct
    outs = [
        sds((8, T, 512), BF),
        sds((G, 8, Z, T, 128), BF),
        sds((8, HD, T), BF),
        sds((G, 8, Z, E, 128), BF),
        sds((8, E, 512), BF),
        sds((S, 16, 256), BF),
        sds((16, 512), F32),
    ] + [sds((S,) + w.shape, BF) for w in weights]
    return pl.pallas_call(
        functools.partial(gather_kernel, S, Z, G),
        out_shape=outs,
        in_specs=[pl.BlockSpec(memory_space=pltpu.SMEM)] + [vmem] * 10,
        out_specs=[vmem] * 7 + [hbm] * 7,
        scratch_shapes=[
            pltpu.VMEM((8, R, 256), BF),
            pltpu.VMEM((8, R, 128), BF),
            pltpu.VMEM((S, R, 256), BF),
            pltpu.VMEM((S, R, 128), BF),
            DMA((S,)), DMA((S,)), DMA((S,)), DMA((S,)), DMA((S,)), DMA((S,)),
            DMA((8,)), DMA((8,)), DMA((8,)), DMA((8,)),
            DMA((2, Z, 9)), DMA((2, Z, 9)),
            DMA((G, 9)), DMA((G, 9)),
            DMA((7, S // 2)), DMA((7, S // 2)), DMA((7, S)), DMA((7,)),
        ],
        compiler_params=pltpu.CompilerParams(
            collective_id=0, has_side_effects=True, vmem_limit_bytes=60 << 20
        ),
        name="gather_qkv",
    )(bnd, hid, small, wproj, wmem, enc, wout, wcq, wco, wup, wdn)


def block_scores(kv_block, queries, key_first, bound, query_first, causal, masked):
    scores = mm(kv_block, queries)
    if not masked:
        return scores
    keys, count = kv_block.shape[0], queries.shape[1]
    query_pos = query_first + lax.broadcasted_iota(jnp.int32, (1, count), 1)
    key_pos = key_first + lax.broadcasted_iota(jnp.int32, (keys, 1), 0)
    if causal:
        least = jnp.where(query_pos < bound, 0, bound)
        allowed = (key_pos <= query_pos) & (key_pos >= least)
    else:
        allowed = jnp.where(query_pos < bound, 0, 1) == key_pos // ENC
    return jnp.where(allowed, scores, MASKED)


def attend_kernel(Z, causal, info, qt, kv, ot, of, lse, vt):
    bound, m, z = info[0], info[1], info[2]
    count, T = kv.shape[0], kv.shape[1]
    per_doc = ENC // T

    def first_block(pos):
        if causal:
            return jnp.where(pos < bound, 0, bound) // T
        return jnp.where(pos < bound, 0, per_doc)

    def last_block(block):
        if causal:
            return block
        return jnp.where(block * T + T - 1 < bound, per_doc, 2 * per_doc) - 1

    def turn_values(kb, carry):
        vt[kb] = kv[kb].astype(F32).T[HD:].astype(BF)
        return carry

    low = 8 * m * Z + z
    lax.fori_loop(first_block(low * T), last_block((8 * m + 7) * Z + z) + 1, turn_values, 0)

    def one_block(i, carry):
        bq = (8 * m + i) * Z + z
        q0 = bq * T
        queries = jnp.concatenate([qt[i], jnp.zeros((HD, T), BF)], axis=0)

        def step(masked, kb, state):
            top, total, acc = state
            scores = block_scores(kv[kb], queries, kb * T, bound, q0, causal, masked)
            new_top = jnp.maximum(top, jnp.max(scores, axis=0, keepdims=True))
            powers = jnp.exp(scores - new_top)
            fade = jnp.exp(top - new_top)
            total = total * fade + jnp.sum(powers, axis=0, keepdims=True)
            acc = acc * fade + mm(vt[kb], powers.astype(BF))
            return new_top, total, acc

        state = (
            jnp.full((1, T), MASKED, F32),
            jnp.zeros((1, T), F32),
            jnp.zeros((HD, T), F32),
        )
        begin, end = first_block(q0), last_block(bq) + 1
        if causal:
            tail = jnp.where(q0 + T - 1 < bound, 0, bound)
            plain = jnp.minimum(jnp.maximum((tail + T - 1) // T, begin), end - 1)
            state = lax.fori_loop(begin, plain, functools.partial(step, True), state)
            state = lax.fori_loop(plain, end - 1, functools.partial(step, False), state)
            state = step(True, end - 1, state)
        else:
            mixed = (q0 < bound) & (q0 + T - 1 >= bound)
            cut = jnp.where(mixed, end, begin)
            state = lax.fori_loop(begin, cut, functools.partial(step, True), state)
            state = lax.fori_loop(cut, end, functools.partial(step, False), state)
        top, total, acc = state
        result = acc / total
        ot[i] = result.astype(BF)
        of[i] = result
        lse[i] = top + jnp.log(total)
        return carry

    lax.fori_loop(0, 8, one_block, 0)


def attend(Z, causal, info, qt, kv):
    T = qt.shape[2]
    sds = jax.ShapeDtypeStruct
    vmem = pl.BlockSpec(memory_space=pltpu.VMEM)
    return pl.pallas_call(
        functools.partial(attend_kernel, Z, causal),
        out_shape=[sds((8, HD, T), BF), sds((8, HD, T), F32), sds((8, 1, T), F32)],
        in_specs=[pl.BlockSpec(memory_space=pltpu.SMEM), vmem, vmem],
        out_specs=[vmem] * 3,
        scratch_shapes=[pltpu.VMEM((kv.shape[0], HD, T), BF)],
        compiler_params=pltpu.CompilerParams(vmem_limit_bytes=60 << 20),
        name="attend_self" if causal else "attend_cross",
    )(info, qt, kv)


def attend_back_kernel(Z, causal, info, qt, kv, dt, of, lse, dq, dkv, qd, rows, delta, dqf):
    bound, m, z = info[0], info[1], info[2]
    count, T = kv.shape[0], kv.shape[1]
    per_doc = ENC // T

    def prepare(i, carry):
        zero = jnp.zeros((HD, T), BF)
        qd[i, :HD, :T] = qt[i]
        qd[i, HD:, :T] = zero
        qd[i, :HD, T:] = zero
        qd[i, HD:, T:] = dt[i]
        both = jnp.concatenate([qt[i].astype(F32), dt[i].astype(F32)], axis=0).T
        lane = lax.broadcasted_iota(jnp.int32, both.shape, 1)
        rows[i, :T] = jnp.where(lane < HD, 0.0, both).astype(BF)
        rows[i, T:] = jnp.where(lane < HD, both, 0.0).astype(BF)
        delta[i] = jnp.sum(dt[i].astype(F32) * of[i], axis=0, keepdims=True)
        dqf[i] = jnp.zeros((HD, T), F32)
        return carry

    lax.fori_loop(0, 8, prepare, 0)
    base = 8 * m * Z + z

    def clear(kb, carry):
        dkv[kb] = jnp.zeros(dkv.shape[1:], BF)
        return carry

    lax.fori_loop(0, count, clear, 0)

    def key_block(kb, carry):
        block = kv[kb]
        turned = block.astype(F32).T[:HD].astype(BF)
        k0 = kb * T

        def step(masked, i, acc):
            q0 = (base + i * Z) * T
            both = mm(block, qd[i])
            scores, d_probs = both[:, :T], both[:, T:]
            if masked:
                query_pos = q0 + lax.broadcasted_iota(jnp.int32, (1, T), 1)
                key_pos = k0 + lax.broadcasted_iota(jnp.int32, (T, 1), 0)
                if causal:
                    least = jnp.where(query_pos < bound, 0, bound)
                    allowed = (key_pos <= query_pos) & (key_pos >= least)
                else:
                    allowed = jnp.where(query_pos < bound, 0, 1) == key_pos // ENC
                scores = jnp.where(allowed, scores, MASKED)
            probs = jnp.exp(scores - lse[i])
            d_raw = (probs * (d_probs - delta[i])).astype(BF)
            dqf[i] += mm(turned, d_raw)
            return acc + mm(jnp.concatenate([probs.astype(BF), d_raw], axis=1), rows[i])

        def chosen(i, acc):
            q0 = (base + i * Z) * T
            if causal:
                tail = jnp.where(q0 + T - 1 < bound, 0, bound)
                masked = (base + i * Z == kb) | (k0 < tail)
            else:
                masked = (q0 < bound) & (q0 + T - 1 >= bound)
            return lax.cond(
                masked, functools.partial(step, True), functools.partial(step, False), i, acc
            )

        if causal:
            begin = jnp.maximum(kb - base + Z - 1, 0) // Z
            reach = jnp.minimum(8, jnp.maximum((bound + T - 1) // T - base + Z - 1, 0) // Z)
            end = jnp.where(k0 + T - 1 < bound, reach, 8)
        else:
            firsts = jnp.minimum(8, jnp.maximum((bound + T - 1) // T - base + Z - 1, 0) // Z)
            wholes = jnp.minimum(8, jnp.maximum(bound // T - base + Z - 1, 0) // Z)
            begin = jnp.where(kb < per_doc, 0, wholes)
            end = jnp.where(kb < per_doc, firsts, 8)
        acc = lax.fori_loop(begin, end, chosen, jnp.zeros((T, 128), F32))
        dkv[kb] = acc.astype(BF)
        return carry

    if causal:
        start = jnp.where(base * T < bound, 0, bound) // T
        lax.fori_loop(start, base + 7 * Z + 1, key_block, 0)
    else:
        lax.fori_loop(0, count, key_block, 0)

    def finish(i, carry):
        dq[i] = (SCALE * dqf[i]).astype(BF)
        return carry

    lax.fori_loop(0, 8, finish, 0)


def attend_back(Z, causal, info, qt, kv, dt, of, lse):
    T = qt.shape[2]
    sds = jax.ShapeDtypeStruct
    vmem = pl.BlockSpec(memory_space=pltpu.VMEM)
    return pl.pallas_call(
        functools.partial(attend_back_kernel, Z, causal),
        out_shape=[sds((8, HD, T), BF), sds(kv.shape, BF)],
        in_specs=[pl.BlockSpec(memory_space=pltpu.SMEM)] + [vmem] * 5,
        out_specs=[vmem] * 2,
        scratch_shapes=[
            pltpu.VMEM((8, 128, 2 * T), BF),
            pltpu.VMEM((8, 2 * T, 128), BF),
            pltpu.VMEM((8, 1, T), F32),
            pltpu.VMEM((8, HD, T), F32),
        ],
        compiler_params=pltpu.CompilerParams(vmem_limit_bytes=60 << 20),
        name="attend_self_back" if causal else "attend_cross_back",
    )(info, qt, kv, dt, of, lse)


def greet_group():
    s, z, j, m = place()
    greet([(None, {"shard": m * 8 + (j + d) % 8}) for d in range(1, 8)])


def exchange_copies(src, dst, send, recv):
    s, z, j, m = place()
    out = []
    for d in (1, 2, 3, 4, 5, 6, 7):
        p = flip(j, d)
        out.append(rcopy(src.at[p], dst.at[j], send.at[d], recv.at[j], {"shard": m * 8 + p}))
    return out


def exchange_start(src, dst, send, recv):
    s, z, j, m = place()
    for c in exchange_copies(src, dst, send, recv):
        c.start()
    dst[j] = src[j]


def exchange_recv(src, dst, send, recv):
    s, z, j, m = place()
    for d in (1, 2, 3, 4, 5, 6, 7):
        p = flip(j, d)
        rcopy(src.at[p], dst.at[p], send.at[d], recv.at[p], {"shard": m * 8 + p}).wait_recv()


def exchange_sent(src, dst, send, recv):
    for c in exchange_copies(src, dst, send, recv):
        c.wait_send()


def remote_call(kernel, name, ident, ins, outs, scratch, smem=1, far=()):
    vmem = pl.BlockSpec(memory_space=pltpu.VMEM)
    in_specs = [pl.BlockSpec(memory_space=pltpu.SMEM)] * smem + [vmem] * (len(ins) - smem)
    for n in far:
        in_specs[n] = pl.BlockSpec(memory_space=pl.ANY)
    return pl.pallas_call(
        kernel,
        out_shape=outs,
        in_specs=in_specs,
        out_specs=[vmem] * len(outs),
        scratch_shapes=scratch,
        compiler_params=pltpu.CompilerParams(
            collective_id=ident, has_side_effects=True, vmem_limit_bytes=60 << 20
        ),
        name=name,
    )(*ins)


def middle_kernel(Z, bnd, ot, hid, vecs, wout, wcq, at, after, n2, cqt, cq_send, s1, r1, s2, r2):
    s, z, j, m = place()
    T = hid.shape[0]
    greet_group()
    exchange_start(ot, at, s1, r1)
    base = embed(hid, bnd[0], vecs, s * Z + z)
    exchange_recv(ot, at, s1, r1)
    attn = at[...].reshape(512, T).astype(F32).T.astype(BF)
    value = base + mm(attn, wout[...])
    after[...] = value
    hat, _ = norm_stats(value)
    normed = (hat * vecs[3:4, :] + vecs[6:7, :]).astype(BF)
    n2[...] = normed
    cq = mm(normed, wcq[...])
    cq_send[...] = (SCALE * cq.T).astype(BF).reshape(8, HD, T)
    exchange_start(cq_send, cqt, s2, r2)
    exchange_recv(cq_send, cqt, s2, r2)
    exchange_sent(ot, at, s1, r1)
    exchange_sent(cq_send, cqt, s2, r2)


def middle(Z, bnd, ot, hid, vecs, wout, wcq):
    T = hid.shape[0]
    sds = jax.ShapeDtypeStruct
    return remote_call(
        functools.partial(middle_kernel, Z),
        "middle",
        1,
        (bnd, ot, hid, vecs, wout, wcq),
        [sds((8, HD, T), BF), sds((T, 512), F32), sds((T, 512), BF), sds((8, HD, T), BF)],
        [pltpu.VMEM((8, HD, T), BF), DMA((8,)), DMA((8,)), DMA((8,)), DMA((8,))],
    )


def erf(x):
    return lax.erf(x)


def feed_kernel(
    crt, after, vecs, upb, wco, wup, wdn, grad,
    layer_out, d_after, co_grad, up_grad, dn_grad, smalls, upb_grad, dct,
    ct, send, n3t, out_acc, dn_acc, s1, r1, s2, r2,
):
    T = after.shape[0]
    FF = wup.shape[1]
    greet_group()
    exchange_start(crt, ct, s1, r1)
    g = grad[...]
    gf = g.astype(F32)
    gt = gf.T.astype(BF)
    exchange_recv(crt, ct, s1, r1)
    cross_t = ct[...].reshape(512, T)
    value = after[...] + mm(cross_t.astype(F32).T.astype(BF), wco[...])
    hat, scale = norm_stats(value)
    normed = hat * vecs[4:5, :] + vecs[7:8, :]
    n3 = normed.astype(BF)
    n3t[...] = n3.astype(F32).T.astype(BF)
    out_acc[...] = value + vecs[9:10, :]
    dn_acc[...] = jnp.zeros_like(dn_acc)
    width = 512
    for c in range(FF // width):
        lo, hi = c * width, (c + 1) * width
        pre = mm(n3, wup[:, lo:hi]) + upb[0:1, lo:hi].astype(F32)
        half = 0.5 * (1.0 + erf(pre * (0.5**0.5)))
        middle_c = (pre * half).astype(BF)
        out_acc[...] += mm(middle_c, wdn[lo:hi, :])
        slope = half + pre * (jnp.exp(-0.5 * pre * pre) * ((0.5 / jnp.pi) ** 0.5))
        d_pre = mm(g, wdn[lo:hi, :], 1, 1) * slope
        d_pre_b = d_pre.astype(BF)
        upb_grad[0:1, lo:hi] = jnp.sum(d_pre_b.astype(F32), axis=0, keepdims=True)
        dn_grad[lo:hi, :] = mm(middle_c.astype(F32).T.astype(BF), g).astype(BF)
        up_grad[:, lo:hi] = mm(n3t[...], d_pre_b).astype(BF)
        dn_acc[...] += mm(d_pre_b, wup[:, lo:hi], 1, 1)
    layer_out[...] = out_acc[...].astype(BF)
    d_value, d_gain, d_shift = norm_back(dn_acc[...], hat, scale, vecs[4:5, :])
    total = gf + d_value
    d_after[...] = total
    smalls[0:1, :] = d_gain
    smalls[1:2, :] = d_shift
    smalls[2:3, :] = jnp.sum(gf, axis=0, keepdims=True)
    dc = total.astype(BF)
    d_cross = mm(wco[...], dc, 1, 1)
    send[...] = d_cross.astype(BF).reshape(8, HD, T)
    exchange_start(send, dct, s2, r2)
    co_grad[...] = mm(cross_t, dc).astype(BF)
    exchange_recv(send, dct, s2, r2)
    exchange_sent(crt, ct, s1, r1)
    exchange_sent(send, dct, s2, r2)


def feed(crt, after, vecs, upb, wco, wup, wdn, grad):
    T, FF = after.shape[0], wup.shape[1]
    sds = jax.ShapeDtypeStruct
    return remote_call(
        feed_kernel,
        "feed_forward",
        2,
        (crt, after, vecs, upb, wco, wup, wdn, grad),
        [
            sds((T, 512), BF),
            sds((T, 512), F32),
            sds((512, 512), BF),
            sds((512, FF), BF),
            sds((FF, 512), BF),
            sds((8, 512), F32),
            sds((1, FF), F32),
            sds((8, HD, T), BF),
        ],
        [
            pltpu.VMEM((8, HD, T), BF),
            pltpu.VMEM((8, HD, T), BF),
            pltpu.VMEM((512, T), BF),
            pltpu.VMEM((T, 512), F32),
            pltpu.VMEM((T, 512), F32),
            DMA((8,)), DMA((8,)), DMA((8,)), DMA((8,)),
        ],
        smem=0,
    )


def middle_back_kernel(
    dcqt, after, d_after2, n2, at, vecs, wcq, wout,
    d_after, cq_grad, out_grad, smalls, dat,
    home, send, s1, r1, s2, r2,
):
    T = after.shape[0]
    greet_group()
    exchange_start(dcqt, home, s1, r1)
    hat, scale = norm_stats(after[...])
    n2t = n2[...].astype(F32).T.astype(BF)
    exchange_recv(dcqt, home, s1, r1)
    dcq = home[...].reshape(512, T).astype(F32).T.astype(BF)
    d_value, d_gain, d_shift = norm_back(mm(dcq, wcq[...], 1, 1), hat, scale, vecs[3:4, :])
    total = d_after2[...] + d_value
    d_after[...] = total
    smalls[0:1, :] = d_gain
    smalls[1:2, :] = d_shift
    da = total.astype(BF)
    send[...] = mm(wout[...], da, 1, 1).astype(BF).reshape(8, HD, T)
    exchange_start(send, dat, s2, r2)
    cq_grad[...] = mm(n2t, dcq).astype(BF)
    out_grad[...] = mm(at[...].reshape(512, T), da).astype(BF)
    exchange_recv(send, dat, s2, r2)
    exchange_sent(dcqt, home, s1, r1)
    exchange_sent(send, dat, s2, r2)


def middle_back(dcqt, after, d_after2, n2, at, vecs, wcq, wout):
    T = after.shape[0]
    sds = jax.ShapeDtypeStruct
    return remote_call(
        middle_back_kernel,
        "middle_back",
        3,
        (dcqt, after, d_after2, n2, at, vecs, wcq, wout),
        [
            sds((T, 512), F32),
            sds((512, 512), BF),
            sds((512, 512), BF),
            sds((8, 512), F32),
            sds((8, HD, T), BF),
        ],
        [
            pltpu.VMEM((8, HD, T), BF),
            pltpu.VMEM((8, HD, T), BF),
            DMA((8,)), DMA((8,)), DMA((8,)), DMA((8,)),
        ],
        smem=0,
    )


NC = 16


def last_kernel(
    S, Z, G,
    info, hid, vecs, d_after, x_all, enc_all, dqt, dkv, dmkv, wproj, wmem,
    out_g, cq_g, co_g, up_g, dn_g, smalls_in,
    hidden_grad, encoder_grad, proj_o, out_o, cq_o, mem_o, co_o, up_o, dn_o, smalls_o,
    sib_out, sib_cq, sib_co, sib_up, sib_dn, got_out, got_cq, got_co, got_up, got_dn,
    rk, rm, fin, finm, mbuf, mbufm, hkv, hq, hm, dall, psend, pgot, msend, mgot,
    wz, zin, zfin, sm_all, sm_z, sm_plane, sm_mine,
    a_s, a_r, b_s, b_r, k_s, k_r, mb_s, mb_r, hq_s, hq_r, hk_s, hk_r, hm_s, hm_r,
    p_s, p_r, pm_s, pm_r, c_s, c_r, f_s, f_r, sm_s, sm_r, sz_s, sz_r,
):
    s, z, j, m = place()
    T, E = hid.shape[0], enc_all.shape[1]
    R = 512 // S
    F = dn_g.shape[0] // S
    bound = info[0]
    chips = S // 2
    core, chip = s % 2, s // 2
    sib = s + 1 - 2 * core
    greet(
        [(None, {"shard": (s + d) % S}) for d in range(1, S)]
        + [(None, {"seq": (z + d) % Z}) for d in range(1, Z)]
    )
    grads = ((out_g, R), (cq_g, R), (co_g, R), (up_g, R), (dn_g, F))
    sibs = (sib_out, sib_cq, sib_co, sib_up, sib_dn)
    gots = (got_out, got_cq, got_co, got_up, got_dn)

    def piece(a, p):
        ref, rows = grads[a]
        return ref.at[pl.ds(pl.multiple_of(p * rows, rows), rows), :]

    def sib_copy(a, q):
        return rcopy(piece(a, 2 * q + 1 - core), sibs[a].at[q], a_s.at[a, q], a_r.at[a, q], {"shard": sib})

    for q in range(chips):
        for a in range(5):
            sib_copy(a, q).start()
    exchange_start(dqt, hq, hq_s, hq_r)

    if G > 1:
        for d in range(1, G):
            o = (m + d) % G
            rcopy(dkv.at[o], mbuf.at[m], mb_s.at[d, 0], mb_r.at[m, 0], {"shard": o * 8 + j}).start()
            rcopy(dmkv.at[o], mbufm.at[m], mb_s.at[d, 1], mb_r.at[m, 1], {"shard": o * 8 + j}).start()
        own_part = pltpu.make_async_copy(dkv.at[m], mbuf.at[m], mb_s.at[0, 0])
        own_part.start()
        own_part.wait()
        for d in range(1, G):
            o = (m + d) % G
            rcopy(dkv.at[o], mbuf.at[o], mb_s.at[d, 0], mb_r.at[o, 0], {"shard": o * 8 + j}).wait_recv()
            rcopy(dmkv.at[o], mbufm.at[o], mb_s.at[d, 1], mb_r.at[o, 1], {"shard": o * 8 + j}).wait_recv()
        for b in range(8):
            acc = mbuf[m, b].astype(F32)
            accm = dmkv[m, b].astype(F32)
            for d in range(1, G):
                acc = acc + mbuf[(m + d) % G, b].astype(F32)
                accm = accm + mbufm[(m + d) % G, b].astype(F32)
            mbuf[m, b] = acc.astype(BF)
            mbufm[m, b] = accm.astype(BF)
        part, partm = mbuf.at[m], mbufm.at[m]
    else:
        part, partm = dkv.at[0], dmkv.at[0]

    def z_view(slot, t):
        return part.at[slot, t] if slot < 8 else partm.at[:, t]

    def z_buffer(way, t, slot):
        return rk.at[way, t, slot] if slot < 8 else rm.at[way, t]

    def z_copy(way, t, slot, source):
        step = 2 * way - 1
        return rcopy(
            source, z_buffer(way, t, slot), k_s.at[way, t, slot], k_r.at[way, t, slot], {"seq": z + step}
        )

    ends = (Z - 1, 0)
    for far in range(Z - 1, 0, -1):
        for slot in range(9):
            for way in (0, 1):
                t = z + (2 * way - 1) * far

                @pl.when((z == ends[way]) & (t >= 0) & (t < Z))
                def _(way=way, t=t, slot=slot):
                    z_copy(way, t, slot, z_view(slot, t)).start()

    def own_copy(a, q):
        return rcopy(
            sibs[a].at[q], gots[a].at[chip], b_s.at[a, q], b_r.at[a, chip], {"shard": 2 * q + core}
        )

    for d in range(chips):
        q = (chip + d + 1) % chips
        for a in range(5):
            sib_copy(a, q).wait_recv()
            sibs[a][q] = (
                sibs[a][q].astype(F32) + piece(a, 2 * q + core)[...].astype(F32)
            ).astype(BF)
            if d < chips - 1:
                own_copy(a, q).start()

    turned = x_all[...].reshape(8 * T, 512).astype(F32).T.astype(BF)
    for b in range(8):
        dq_b = dqt[b].astype(F32)
        dall[b * T : (b + 1) * T, 128:] = jnp.concatenate([dq_b, jnp.zeros_like(dq_b)], axis=0).T.astype(BF)

    for far in range(Z - 1, 0, -1):
        for slot in range(9):
            for way in (0, 1):
                t = z + (2 * way - 1) * far

                @pl.when((z != ends[way]) & (t >= 0) & (t < Z))
                def _(way=way, t=t, slot=slot):
                    z_copy(way, t, slot, z_view(slot, t)).wait_recv()
                    buf = z_buffer(way, t, slot)
                    buf[...] = (
                        buf[...].astype(F32) + z_view(slot, t)[...].astype(F32)
                    ).astype(BF)
                    z_copy(way, t, slot, buf).start()

    for slot in range(9):
        for way in (0, 1):

            @pl.when(z != ends[way])
            def _(way=way, slot=slot):
                z_copy(way, z, slot, z_view(slot, z)).wait_recv()

        low = jnp.where(z == ends[0], 0.0, z_buffer(0, z, slot)[...].astype(F32))
        high = jnp.where(z == ends[1], 0.0, z_buffer(1, z, slot)[...].astype(F32))
        total = (low + high + z_view(slot, z)[...].astype(F32)).astype(BF)
        if slot < 8:
            fin[slot] = total
        else:
            finm[...] = total

    mine, minem = fin, finm
    exchange_start(mine, hkv, hk_s, hk_r)
    exchange_start(minem, hm, hm_s, hm_r)

    for b in range(8):
        dall[b * T : (b + 1) * T, :128] = mine[b]
    psend[...] = mm(turned, dall[...]).astype(BF).reshape(S, R, 256)
    enc_turned = enc_all[...].reshape(8 * E, 512).astype(F32).T.astype(BF)
    msend[...] = mm(enc_turned, minem[...].reshape(8 * E, 128)).astype(BF).reshape(S, R, 128)
    pgot[s] = psend[s]
    mgot[s] = msend[s]
    for d in range(1, S):
        p = (s + d) % S
        rcopy(psend.at[p], pgot.at[s], p_s.at[d], p_r.at[s], {"shard": p}).start()
        rcopy(msend.at[p], mgot.at[s], pm_s.at[d], pm_r.at[s], {"shard": p}).start()

    for a in range(5):
        for d in range(1, chips):
            q = (chip + d) % chips
            rcopy(sibs[a].at[q], gots[a].at[q], b_s.at[a, q], b_r.at[a, q], {"shard": 2 * q + core}).wait_recv()
        total = sibs[a][chip].astype(F32)
        for d in range(1, chips):
            total = total + gots[a][(chip + d) % chips].astype(F32)
        total = total.astype(BF)
        if a < 3:
            wz[a] = total
        elif a == 3:
            for c in range(4):
                wz[3 + c] = total[:, 512 * c : 512 * (c + 1)]
        else:
            for c in range(4):
                wz[7 + c] = total[c * R : (c + 1) * R]

    block = s * Z + z
    value = embed(hid, bound, vecs, block)
    hat, scale = norm_stats(value)
    exchange_recv(dqt, hq, hq_s, hq_r)
    exchange_recv(mine, hkv, hk_s, hk_r)
    exchange_recv(minem, hm, hm_s, hm_r)
    d_query = hq[...].reshape(512, T).astype(F32).T.astype(BF)
    d_keys = jnp.concatenate([hkv[h][:, :HD] for h in range(H)], axis=1)
    d_values = jnp.concatenate([hkv[h][:, HD:] for h in range(H)], axis=1)
    d_norm = (
        mm(d_query, wproj[:, :512], 1, 1)
        + mm(d_keys, wproj[:, 512:1024], 1, 1)
        + mm(d_values, wproj[:, 1024:], 1, 1)
    )
    d_value, d_gain, d_shift = norm_back(d_norm, hat, scale, vecs[2:3, :])
    total = d_after[...] + d_value
    hidden_grad[...] = total
    pos = block * T + lax.broadcasted_iota(jnp.int32, (T, 1), 0)
    first = jnp.sum(jnp.where(pos < bound, total, 0.0), axis=0, keepdims=True)
    second = jnp.sum(jnp.where(pos < bound, 0.0, total), axis=0, keepdims=True)
    sm_mine[...] = smalls_in[...]
    sm_mine[0:1, :] = d_gain
    sm_mine[3:4, :] = d_shift
    sm_mine[6:7, :] = first
    sm_mine[7:8, :] = second
    for d in range(1, S):
        rcopy(sm_mine, sm_all.at[s], sm_s.at[d], sm_r.at[s], {"shard": (s + d) % S}).start()
    sm_all[s] = sm_mine[...]
    e_keys = jnp.concatenate([hm[h][:, :HD] for h in range(H)], axis=1)
    e_values = jnp.concatenate([hm[h][:, HD:] for h in range(H)], axis=1)
    encoder_grad[...] = mm(e_keys, wmem[:, :512], 1, 1) + mm(e_values, wmem[:, 512:], 1, 1)

    for d in range(1, S):
        p = (s + d) % S
        rcopy(psend.at[p], pgot.at[p], p_s.at[d], p_r.at[p], {"shard": p}).wait_recv()
        rcopy(msend.at[p], mgot.at[p], pm_s.at[d], pm_r.at[p], {"shard": p}).wait_recv()
    heads, mheads = [], []
    for h in range(H):
        acc, accm = pgot[h].astype(F32), mgot[h].astype(F32)
        for g in range(1, G):
            acc = acc + pgot[8 * g + h].astype(F32)
            accm = accm + mgot[8 * g + h].astype(F32)
        heads.append(acc)
        mheads.append(accm)
    wz[11] = jnp.concatenate([v[:, 128 : 128 + HD] for v in heads], axis=1).astype(BF)
    wz[12] = jnp.concatenate([v[:, :HD] for v in heads], axis=1).astype(BF)
    wz[13] = jnp.concatenate([v[:, HD:128] for v in heads], axis=1).astype(BF)
    wz[14] = jnp.concatenate([v[:, :HD] for v in mheads], axis=1).astype(BF)
    wz[15] = jnp.concatenate([v[:, HD:] for v in mheads], axis=1).astype(BF)

    def inward(k, step):
        way = (step + 1) // 2
        return rcopy(wz.at[k], zin.at[way, k], c_s.at[way, k], c_r.at[way, k], {"seq": z + step})

    def outward(k, step):
        return rcopy(zfin.at[k], zfin.at[k], f_s.at[(step + 1) // 2, k], f_r.at[k], {"seq": z + step})

    def reduce_in(k, r):
        for step, beyond in ((-1, z > r), (1, z < r)):
            tip = ends[0] if step < 0 else ends[1]
            way = (step + 1) // 2

            @pl.when(beyond)
            def _(step=step, tip=tip, way=way):
                @pl.when(z != tip)
                def _():
                    inward(k, step).wait_recv()
                    wz[k] = (wz[k].astype(F32) + zin[way, k].astype(F32)).astype(BF)

                inward(k, step).start()

        @pl.when(z == r)
        def _():
            total = wz[k].astype(F32)
            if r < Z - 1:
                inward(k, -1).wait_recv()
                total = total + zin[0, k].astype(F32)
            if r > 0:
                inward(k, 1).wait_recv()
                total = total + zin[1, k].astype(F32)
            zfin[k] = total.astype(BF)
            if r < Z - 1:
                outward(k, 1).start()
            if r > 0:
                outward(k, -1).start()

    def send_out(k, r):
        for step, beyond in ((1, z > r), (-1, z < r)):
            tip = Z - 1 if step > 0 else 0

            @pl.when(beyond)
            def _(step=step, tip=tip):
                outward(k, step).wait_recv()

                @pl.when(z != tip)
                def _():
                    outward(k, step).start()

        value = zfin[k].astype(F32)
        if k == 0:
            out_o[...] = value
        elif k == 1:
            cq_o[...] = value
        elif k == 2:
            co_o[...] = value
        elif k < 7:
            up_o[:, 512 * (k - 3) : 512 * (k - 2)] = value
        elif k < 11:
            dn_o[(k - 7) * R : (k - 6) * R, :] = value
        elif k < 14:
            proj_o[:, 512 * (k - 11) : 512 * (k - 10)] = value
        else:
            mem_o[:, 512 * (k - 14) : 512 * (k - 13)] = value

    def root(k):
        return max(Z // 2 - 1 + k % 2, 0) if Z > 1 else 0

    lag = 3
    for k in range(NC + lag):
        if k < NC:
            reduce_in(k, root(k))
        if k >= lag:
            send_out(k - lag, root(k - lag))
        if k == 4:
            for d in range(1, S):
                p = (s + d) % S
                rcopy(sm_mine, sm_all.at[p], sm_s.at[d], sm_r.at[p], {"shard": p}).wait_recv()
            acc = sm_all[0]
            for p in range(1, S):
                acc = acc + sm_all[p]
            sm_plane[...] = acc
            for d in range(1, Z):
                rcopy(sm_plane, sm_z.at[z], sz_s.at[d], sz_r.at[z], {"seq": (z + d) % Z}).start()
            sm_z[z] = acc
    for d in range(1, Z):
        o = (z + d) % Z
        rcopy(sm_plane, sm_z.at[o], sz_s.at[d], sz_r.at[o], {"seq": o}).wait_recv()
    acc = sm_z[0]
    for o in range(1, Z):
        acc = acc + sm_z[o]
    smalls_o[...] = acc

    for a in range(5):
        for q in range(chips):
            sib_copy(a, q).wait_send()
        for d in range(1, chips):
            own_copy(a, (chip + d) % chips).wait_send()
    for d in range(1, G):
        o = (m + d) % G
        rcopy(dkv.at[o], mbuf.at[m], mb_s.at[d, 0], mb_r.at[m, 0], {"shard": o * 8 + j}).wait_send()
        rcopy(dmkv.at[o], mbufm.at[m], mb_s.at[d, 1], mb_r.at[m, 1], {"shard": o * 8 + j}).wait_send()
    exchange_sent(dqt, hq, hq_s, hq_r)
    exchange_sent(mine, hkv, hk_s, hk_r)
    exchange_sent(minem, hm, hm_s, hm_r)
    for far in range(Z - 1, 0, -1):
        for slot in range(9):
            for way in (0, 1):
                t = z + (2 * way - 1) * far

                @pl.when((t >= 0) & (t < Z))
                def _(way=way, t=t, slot=slot):
                    z_copy(way, t, slot, z_view(slot, t)).wait_send()

    for d in range(1, S):
        p = (s + d) % S
        rcopy(psend.at[p], pgot.at[s], p_s.at[d], p_r.at[s], {"shard": p}).wait_send()
        rcopy(msend.at[p], mgot.at[s], pm_s.at[d], pm_r.at[s], {"shard": p}).wait_send()
        rcopy(sm_mine, sm_all.at[s], sm_s.at[d], sm_r.at[s], {"shard": p}).wait_send()
    for d in range(1, Z):
        rcopy(sm_plane, sm_z.at[z], sz_s.at[d], sz_r.at[z], {"seq": (z + d) % Z}).wait_send()
    for k in range(NC):
        r = root(k)
        for step, beyond in ((-1, z > r), (1, z < r)):

            @pl.when(beyond)
            def _(step=step):
                inward(k, step).wait_send()

        for step in (-1, 1):
            sends = (z >= r) & (z < Z - 1) if step > 0 else (z <= r) & (z > 0)

            @pl.when(sends)
            def _(step=step):
                outward(k, step).wait_send()


def last(v):
    S, Z, G = v["S"], v["Z"], v["G"]
    T, R, F, E = v["T"], v["R"], v["F"], v["encoder"].shape[0]
    s = v["s"]
    FF = v["wup"].shape[1]
    chips = S // 2
    smalls = jnp.concatenate(
        [
            jnp.zeros((1, 512), F32), v["small2"][0:1], v["small3"][0:1],
            jnp.zeros((1, 512), F32), v["small2"][1:2], v["small3"][1:2],
            jnp.zeros((2, 512), F32), v["small3"][2:3], v["upb_grad"].reshape(FF // 512, 512),
            jnp.zeros((7 - FF // 512, 512), F32),
        ],
        axis=0,
    )
    sds = jax.ShapeDtypeStruct
    V = pltpu.VMEM
    res = remote_call(
        functools.partial(last_kernel, S, Z, G),
        "gradients_home",
        4,
        (
            v["info"], v["hidden_in"], v["vecs"], v["d_after"], v["x_all"], v["enc_all"], v["dqt"],
            v["dkv"].reshape(G, 8, Z, T, 128), v["dmkv"].reshape(G, 8, Z, E, 128), v["wproj"], v["wmem"],
            v["wout_grad"], v["cq_grad"], v["co_grad"], v["up_grad"], v["dn_grad"], smalls,
        ),
        [
            sds((T, 512), F32), sds((E, 512), F32), sds((R, 1536), F32), sds((R, 512), F32),
            sds((R, 512), F32), sds((R, 1024), F32), sds((R, 512), F32), sds((R, FF), F32),
            sds((F, 512), F32), sds((16, 512), F32),
        ],
        [V((chips, R, 512), BF)] * 3 + [V((chips, R, FF), BF), V((chips, F, 512), BF)]
        + [V((chips, R, 512), BF)] * 3 + [V((chips, R, FF), BF), V((chips, F, 512), BF)]
        + [
            V((2, Z, 8, T, 128), BF), V((2, Z, 8, E, 128), BF),
            V((8, T, 128), BF), V((8, E, 128), BF),
            V((G if G > 1 else 1, 8, Z if G > 1 else 1, T, 128), BF),
            V((G if G > 1 else 1, 8, Z if G > 1 else 1, E, 128), BF),
            V((8, T, 128), BF), V((8, HD, T), BF), V((8, E, 128), BF),
            V((8 * T, 256), BF),
            V((S, R, 256), BF), V((S, R, 256), BF), V((S, R, 128), BF), V((S, R, 128), BF),
            V((NC, R, 512), BF), V((2, NC, R, 512), BF), V((NC, R, 512), BF),
            V((S, 16, 512), F32), V((Z, 16, 512), F32), V((16, 512), F32), V((16, 512), F32),
            DMA((5, chips)), DMA((5, chips)), DMA((5, chips)), DMA((5, chips)),
            DMA((2, Z, 9)), DMA((2, Z, 9)), DMA((G, 2)), DMA((G, 2)),
            DMA((8,)), DMA((8,)), DMA((8,)), DMA((8,)), DMA((8,)), DMA((8,)),
            DMA((S,)), DMA((S,)), DMA((S,)), DMA((S,)),
            DMA((2, NC)), DMA((2, NC)), DMA((2, NC)), DMA((NC,)),
            DMA((S,)), DMA((S,)), DMA((Z,)), DMA((Z,)),
        ],
        far=(7,) if G > 1 else (),
    )
    hidden_grad, encoder_grad, proj_o, out_o, cq_o, mem_o, co_o, up_o, dn_o, sums = res

    def own(rows, width):
        return lax.dynamic_slice(rows, (0, s * width), (rows.shape[0], width))

    step_hot = v["step_hot"].astype(F32)
    time_rows = own(sums[6:8], R)
    time_grad = jnp.sum(step_hot[:, :, None] * time_rows[:, None, :], axis=0)
    upb = own(sums[9 : 9 + FF // 512].reshape(1, FF), F)[0]
    return (
        v["layer_out"], hidden_grad, encoder_grad, time_grad, own(sums[0:3], R), own(sums[3:6], R),
        proj_o, out_o, cq_o, mem_o, co_o, up_o, upb, dn_o, own(sums[8:9], R)[0],
    )


def shards(
    hidden_in, encoder, segment_ids, timestep, out_grad, time_table, norm_gain, norm_bias,
    self_proj, self_out, cross_query, cross_memory, cross_out, up_weight, up_bias, down_weight, down_bias,
):
    S, Z = lax.axis_size("shard"), lax.axis_size("seq")
    s, z = lax.axis_index("shard"), lax.axis_index("seq")
    T, R, F = hidden_in.shape[0], self_proj.shape[0], up_bias.shape[0]
    G = S // 8
    NB = S * Z
    bound = jnp.sum((segment_ids == 0).astype(jnp.int32))
    info = jnp.stack([bound, s // 8, z]).astype(jnp.int32)
    step_hot = timestep[:, None] == jnp.arange(time_table.shape[0], dtype=jnp.int32)[None, :]
    steps = jnp.sum(jnp.where(step_hot[:, :, None], time_table[None], 0), axis=1)
    small = jnp.concatenate(
        [
            jnp.pad(jnp.concatenate([steps, norm_gain, norm_bias], axis=0), ((0, 0), (0, 256 - R))),
            jnp.pad(up_bias[None], ((0, 0), (0, 256 - F))),
            jnp.pad(down_bias[None], ((0, 6), (0, 256 - R))),
        ],
        axis=0,
    ).astype(BF)
    (
        x_all, kv, qt, mkv, enc_all, small_all, vecs, gproj, gmem, gout, gcq, gco, gup, gdn,
    ) = gather_call(
        S, Z, info, hidden_in, small, self_proj, cross_memory, encoder,
        self_out, cross_query, cross_out, up_weight, down_weight,
    )
    wproj, wmem = gproj.reshape(512, 1536), gmem.reshape(512, 1024)
    wout, wcq, wco = gout.reshape(512, 512), gcq.reshape(512, 512), gco.reshape(512, 512)
    wup, wdn = gup.reshape(512, -1), gdn.reshape(-1, 512)
    upb = small_all[:, 8, :F].reshape(1, S * F)
    kv = kv.reshape(NB, T, 128)
    mkv = mkv.reshape(DOCS * ENC // T, T, 128)

    ot, of, lse = attend(Z, True, info, qt, kv)
    at, after, n2, cqt = middle(Z, info, ot, hidden_in, vecs, wout, wcq)
    crt, crf, clse = attend(Z, False, info, cqt, mkv)
    layer_out, d_after2, co_grad, up_grad, dn_grad, small3, upb_grad, dct = feed(
        crt, after, vecs, upb, wco, wup, wdn, out_grad
    )
    dcqt, dmkv = attend_back(Z, False, info, cqt, mkv, dct, crf, clse)
    d_after, cq_grad, wout_grad, small2, dat = middle_back(
        dcqt, after, d_after2, n2, at, vecs, wcq, wout
    )
    dqt, dkv = attend_back(Z, True, info, qt, kv, dat, of, lse)
    return last(locals())


def solution(mesh):
    return jax.shard_map(
        shards,
        mesh=mesh,
        in_specs=(
            P(("shard", "seq"), None),
            P(("shard", "seq"), None),
            P(),
            P(),
            P(("shard", "seq"), None),
            P(None, "shard"),
            P(None, "shard"),
            P(None, "shard"),
            P("shard", None),
            P("shard", None),
            P("shard", None),
            P("shard", None),
            P("shard", None),
            P("shard", None),
            P("shard"),
            P("shard", None),
            P("shard"),
        ),
        out_specs=(
            P(("shard", "seq"), None),
            P(("shard", "seq"), None),
            P(("shard", "seq"), None),
            P(None, "shard"),
            P(None, "shard"),
            P(None, "shard"),
            P("shard", None),
            P("shard", None),
            P("shard", None),
            P("shard", None),
            P("shard", None),
            P("shard", None),
            P("shard"),
            P("shard", None),
            P("shard"),
        ),
        check_vma=False,
    )
```

```python
import functools

import jax
import jax.numpy as jnp
from jax import lax
from jax.experimental import pallas as pl
from jax.experimental.pallas import tpu as pltpu
from jax.sharding import PartitionSpec as P

H = 8
HD = 64
DOCS = 2
ENC = 1024
EPS = 1e-05
MASKED = -1e30
SCALE = HD**-0.5
MESH = pl.DeviceIdType.MESH
BF = jnp.bfloat16
F32 = jnp.float32
DMA = pltpu.SemaphoreType.DMA
LIMIT = 62 << 20
ORDER = (0, 1, 2, 4, 3, 6, 5, 7)


def mm(a, b, ca=1, cb=0):
    return lax.dot_general(a, b, (((ca,), (cb,)), ((), ())), preferred_element_type=F32)


def flip(j, bits):
    low, mid, high = j % 2, (j // 2) % 2, (j // 4) % 2
    out = j
    if bits & 1:
        out = out + 1 - 2 * low
    if bits & 2:
        out = out + 2 - 4 * mid
    if bits & 4:
        out = out + 4 - 8 * high
    return out


def rcopy(src, dst, send_sem, recv_sem, device_id):
    return pltpu.make_async_remote_copy(
        src_ref=src,
        dst_ref=dst,
        send_sem=send_sem,
        recv_sem=recv_sem,
        device_id=device_id,
        device_id_type=MESH,
    )


def place():
    shard, seq = lax.axis_index("shard"), lax.axis_index("seq")
    return shard, seq, shard % 8, shard // 8


def greet(peers):
    barrier = pltpu.get_barrier_semaphore()
    count = 0
    for condition, device in peers:
        if condition is None:
            pl.semaphore_signal(barrier, inc=1, device_id=device, device_id_type=MESH)
            count = count + 1
        else:

            @pl.when(condition)
            def _(device=device):
                pl.semaphore_signal(barrier, inc=1, device_id=device, device_id_type=MESH)

            count = count + jnp.where(condition, 1, 0)
    pl.semaphore_wait(barrier, count)


def norm_stats(value):
    center = jnp.mean(value, axis=1, keepdims=True)
    offset = value - center
    spread = jnp.mean(offset * offset, axis=1, keepdims=True)
    scale = lax.rsqrt(spread + EPS)
    return offset * scale, scale


def norm_back(d_out, hat, scale, gain):
    d_hat = d_out * gain
    first = jnp.mean(d_hat, axis=1, keepdims=True)
    second = jnp.mean(d_hat * hat, axis=1, keepdims=True)
    d_in = scale * (d_hat - first - hat * second)
    return d_in, jnp.sum(d_out * hat, axis=0, keepdims=True), jnp.sum(d_out, axis=0, keepdims=True)


def embed(hid_ref, bound, vecs_ref, block):
    rows = hid_ref.shape[0]
    pos = block * rows + lax.broadcasted_iota(jnp.int32, (rows, 1), 0)
    picked = jnp.where(pos < bound, vecs_ref[0:1, :], vecs_ref[1:2, :])
    return hid_ref[...].astype(F32) + picked


class Whole:
    def __init__(self, pairs, S, sems):
        self.pairs, self.S = pairs, S
        self.local, self.send, self.recv, self.half, self.pass_on = sems
        self.s = lax.axis_index("shard")
        self.core, self.chip = self.s % 2, self.s // 2
        self.sib = flip(self.s, 1)
        self.near = S == 8
        self.flow = []

    @staticmethod
    def scratch(count, S):
        return [DMA((count,)), DMA((count, max(8, S // 2))), DMA((count, S)), DMA((count, 2)), DMA((count, S // 2))]

    def copy(self, a, source, n, to, half=None):
        shard, whole = self.pairs[a]
        target = whole.at[source]
        if half is not None:
            rows = shard.shape[0] // 2
            target = whole.at[source, pl.ds(half * rows, rows)]
            recv = self.half.at[a, half]
        else:
            recv = self.recv.at[a, source]
        origin = shard if n < 0 else target
        send = self.send.at[a, -n - 1 if n < 0 else n]
        return rcopy(origin, target, send, recv, {"shard": to})

    def go(self, *args):
        c = self.copy(*args)
        c.start()
        self.flow.append(c)

    def arrived(self, a, source, half=None):
        self.copy(a, source, 7, self.sib, half).wait_recv()

    def same_core(self, d):
        return ((self.chip + d) % (self.S // 2)) * 2 + self.core

    def start(self, a):
        shard, whole = self.pairs[a]
        pltpu.make_async_copy(shard, whole.at[self.s], self.local.at[a]).start()
        s = self.s
        if self.near:
            self.go(a, s, -1, flip(s, 2))
            self.go(a, s, -2, flip(s, 4))
            self.go(a, s, -3, self.sib)
            return
        for d in range(1, self.S // 2):
            c = rcopy(shard, whole.at[s], self.send.at[a, d], self.recv.at[a, s], {"shard": self.same_core(d)})
            c.start()
            self.flow.append(c)
        c = rcopy(shard, whole.at[s], self.send.at[a, 0], self.recv.at[a, s], {"shard": self.sib})
        c.start()
        self.flow.append(c)

    def relay(self, a):
        if not self.near:
            return
        x, y = flip(self.s, 2), flip(self.s, 4)
        self.arrived(a, x)
        self.go(a, x, 3, y, 0)
        self.go(a, x, 5, self.sib)
        self.arrived(a, y)
        self.go(a, y, 4, x, 1)
        self.go(a, y, 6, self.sib)

    def finish(self, a):
        if self.near:
            far = flip(self.s, 6)
            self.arrived(a, far, 0)
            self.arrived(a, far, 1)
            self.go(a, far, 7, self.sib)
            return
        _, whole = self.pairs[a]
        for d in range(1, self.S // 2):
            q = self.same_core(self.S // 2 - d)
            self.arrived(a, q)
            c = rcopy(whole.at[q], whole.at[q], self.pass_on.at[a, d], self.recv.at[a, q], {"shard": self.sib})
            c.start()
            self.flow.append(c)

    def wait(self, a):
        shard, whole = self.pairs[a]
        self.arrived(a, self.sib)
        for d in range(1, self.S // 2):
            self.arrived(a, flip(self.same_core(d), 1))
        pltpu.make_async_copy(shard, whole.at[self.s], self.local.at[a]).wait()

    def drain(self):
        for c in self.flow:
            c.wait_send()


def gather_kernel(
    S, Z, G,
    timestep, seg, hid, table, gain, shift, upb, dnb, wproj, wmem, enc, wout, wcq, wco, wup, wdn,
    info, x_all, kv, qt, mkv, enc_all, vecs, upb_row, gout, gcq, gco, gup, gdn,
    rows_f, small, small_all, wsend, msend, w_all, m_all, sm_s, sm_r, w_s, w_r, mw_s, mw_r,
    x_s, x_r, e_s, e_r, z_s, z_r, mb_s, mb_r, *whole_sems
):
    s, z, j, m = place()
    R, F = wproj.shape[0], upb.shape[1]
    T, E = hid.shape[0], enc.shape[0]
    sib = flip(s, 1)

    step = lax.broadcasted_iota(jnp.int32, table.shape, 0)
    rows_f[...] = jnp.zeros((16, 256), F32)
    for d in range(DOCS):
        picked = jnp.where(step == timestep[d], table[...].astype(F32), 0.0)
        rows_f[d : d + 1, :R] = jnp.sum(picked, axis=0, keepdims=True)
    rows_f[2:5, :R] = gain[...].astype(F32)
    rows_f[5:8, :R] = shift[...].astype(F32)
    rows_f[8:9, :F] = upb[...].astype(F32)
    rows_f[9:10, :R] = dnb[...].astype(F32)
    small[...] = rows_f[...].astype(BF)
    small_all[s] = small[...]
    bound = jnp.sum(jnp.where(seg[...] == 0, 1.0, 0.0)).astype(jnp.int32)
    info[0] = bound
    info[1] = m
    info[2] = z
    info[3] = s

    greet(
        [(None, {"shard": (s + d) % S}) for d in range(1, S)]
        + [(z > 0, {"seq": z - 1}), (z < Z - 1, {"seq": z + 1})]
    )
    small_copies = []
    for d in range(1, S):
        c = rcopy(small, small_all.at[s], sm_s.at[d], sm_r.at[s], {"shard": (s + d) % S})
        c.start()
        small_copies.append(c)
    for h in range(H):
        k = wproj[:, 512 + HD * h : 512 + HD * (h + 1)]
        v = wproj[:, 1024 + HD * h : 1024 + HD * (h + 1)]
        q = wproj[:, HD * h : HD * (h + 1)]
        wsend[h] = jnp.concatenate([k, v, q, jnp.zeros_like(q)], axis=1)
        msend[h] = jnp.concatenate(
            [wmem[:, HD * h : HD * (h + 1)], wmem[:, 512 + HD * h : 512 + HD * (h + 1)]], axis=1
        )
    w_all[s] = wsend[j]
    m_all[s] = msend[j]
    w_copies = []
    for d in range(1, S):
        p = (s + d) % S
        c = rcopy(wsend.at[p % 8], w_all.at[s], w_s.at[d], w_r.at[s], {"shard": p})
        c.start()
        w_copies.append(c)
        c = rcopy(msend.at[p % 8], m_all.at[s], mw_s.at[d], mw_r.at[s], {"shard": p})
        c.start()
        w_copies.append(c)
    for d in range(1, S):
        p = (s + d) % S
        rcopy(small, small_all.at[p], sm_s.at[d], sm_r.at[p], {"shard": p}).wait_recv()
    rows = jnp.zeros((16, 512), F32)
    lane = lax.broadcasted_iota(jnp.int32, (256, 512), 0)
    col = lax.broadcasted_iota(jnp.int32, (256, 512), 1)
    for p in range(S):
        pick = ((col - p * R) == lane) & (lane < R)
        rows = rows + mm(small_all[p], jnp.where(pick, 1.0, 0.0).astype(BF))
        upb_row[0:1, p * F : (p + 1) * F] = small_all[p].astype(F32)[8:9, :F]
    vecs[...] = rows

    hat, _ = norm_stats(embed(hid, bound, vecs, s * Z + z))
    x_all[j] = (hat * vecs[2:3, :] + vecs[5:6, :]).astype(BF)
    enc_all[j] = enc[...]
    copies = []

    def send_block(ref, bits_source, bits_target, send, recv):
        source = flip(j, bits_source)
        c = rcopy(ref.at[source], ref.at[source], send, recv.at[source], {"shard": flip(s, bits_target)})
        c.start()
        copies.append(c)

    def wait_block(ref, bits, recv):
        source = flip(j, bits)
        rcopy(ref.at[source], ref.at[source], x_s.at[0], recv.at[source], {"shard": sib}).wait_recv()

    for n, bits in enumerate((1, 2, 4, 6)):
        send_block(x_all, 0, bits, x_s.at[n], x_r)
    for n, bits in enumerate((1, 2, 4, 6)):
        send_block(enc_all, 0, bits, e_s.at[n], e_r)
    whole = Whole(
        ((wout, gout), (wcq, gcq), (wco, gco), (wup, gup), (wdn, gdn)), S, whole_sems
    )
    for a in range(3):
        whole.start(a)
    for d in range(1, S):
        p = (s + d) % S
        rcopy(wsend.at[0], w_all.at[p], w_s.at[d], w_r.at[p], {"shard": p}).wait_recv()
        rcopy(msend.at[0], m_all.at[p], mw_s.at[d], mw_r.at[p], {"shard": p}).wait_recv()
    w_head = w_all[...].reshape(S * R, 256)
    m_head = m_all[...].reshape(S * R, 128)

    def z_copy(ref, block, plane, step, hop, slot):
        view = ref.at[:, block, plane] if block is not None else ref.at[:, :, plane]
        way = (step + 1) // 2
        return rcopy(view, view, z_s.at[way, hop, slot], z_r.at[way, hop, slot], {"seq": z + step})

    def z_passes(step, hop):
        origin = z - step * hop
        return (z + step >= 0) & (z + step < Z) & (origin >= 0) & (origin < Z)

    def z_send(ref, block, hop, slot):
        for step in (-1, 1):

            @pl.when(z_passes(step, hop))
            def _(step=step):
                z_copy(ref, block, z - step * hop, step, hop, slot).start()

    def z_recv(ref, block, hop, slot):
        for step in (-1, 1):
            origin = z - step * hop

            @pl.when((origin >= 0) & (origin < Z))
            def _(step=step, origin=origin):
                z_copy(ref, block, origin, step, hop - 1, slot).wait_recv()

    def z_drain(ref, block, hop, slot):
        for step in (-1, 1):

            @pl.when(z_passes(step, hop))
            def _(step=step):
                z_copy(ref, block, z - step * hop, step, hop, slot).wait_send()

    def member_copy(ref, block, d, slot, mine):
        other = (m + d) % G
        at = m if mine else other
        view = ref.at[at, block, z] if block is not None else ref.at[at, :, z]
        return rcopy(view, view, mb_s.at[d, slot], mb_r.at[at, slot], {"shard": other * 8 + j})

    def spread(ref, block, slot):
        for d in range(1, G):
            member_copy(ref, block, d, slot, True).start()
        for d in range(1, G):
            member_copy(ref, block, d, slot, False).wait_recv()
        z_send(ref, block, 0, slot)

    for n, bits in enumerate(ORDER):
        block = flip(j, bits)
        if bits:
            wait_block(x_all, bits, x_r)
            if bits in (2, 4, 6):
                send_block(x_all, bits, 1, x_s.at[3 + bits // 2], x_r)
        kvq = mm(x_all[block], w_head)
        kv[m, block, z] = kvq[:, :128].astype(BF)
        spread(kv, block, n)
        qt[block] = (SCALE * kvq[:, 128:256].T[:HD]).astype(BF)
    for a in range(3, 5):
        whole.start(a)

    for bits in (2, 4, 6):
        wait_block(enc_all, bits, e_r)
        send_block(enc_all, bits, 1, e_s.at[3 + bits // 2], e_r)
    for bits in (1, 3, 5, 7):
        wait_block(enc_all, bits, e_r)
    for b in range(8):
        mkv[m, b, z] = mm(enc_all[b], m_head).astype(BF)
    spread(mkv, None, 8)

    for hop in range(1, Z):
        for n, bits in enumerate(ORDER):
            z_recv(kv, flip(j, bits), hop, n)
            z_send(kv, flip(j, bits), hop, n)
        z_recv(mkv, None, hop, 8)
        z_send(mkv, None, hop, 8)
        if hop == 1:
            for a in range(3):
                whole.relay(a)
        if hop == min(2, Z - 1):
            for a in range(3, 5):
                whole.relay(a)
            for a in range(3):
                whole.finish(a)
    for a in range(3, 5):
        whole.finish(a)
    for a in range(5):
        whole.wait(a)
    whole.drain()
    for c in small_copies + w_copies + copies:
        c.wait_send()
    for n, bits in enumerate(ORDER):
        for d in range(1, G):
            member_copy(kv, flip(j, bits), d, n, True).wait_send()
        for hop in range(Z - 1):
            z_drain(kv, flip(j, bits), hop, n)
    for d in range(1, G):
        member_copy(mkv, None, d, 8, True).wait_send()
    for hop in range(Z - 1):
        z_drain(mkv, None, hop, 8)


def gather_call(S, Z, args):
    G = S // 8
    (timestep, seg, hid, table, gain, shift, upb, dnb, wproj, wmem, enc, *weights) = args
    T, R, E, F = hid.shape[0], wproj.shape[0], enc.shape[0], upb.shape[1]
    vmem = pl.BlockSpec(memory_space=pltpu.VMEM)
    smem = pl.BlockSpec(memory_space=pltpu.SMEM)
    hbm = pl.BlockSpec(memory_space=pl.ANY)
    sds = jax.ShapeDtypeStruct
    outs = [
        sds((4,), jnp.int32),
        sds((8, T, 512), BF),
        sds((G, 8, Z, T, 128), BF),
        sds((8, HD, T), BF),
        sds((G, 8, Z, E, 128), BF),
        sds((8, E, 512), BF),
        sds((16, 512), F32),
        sds((1, S * F), F32),
    ] + [sds((S,) + w.shape, BF) for w in weights]
    return pl.pallas_call(
        functools.partial(gather_kernel, S, Z, G),
        out_shape=outs,
        in_specs=[smem] + [vmem] * (len(args) - 1),
        out_specs=[smem] + [vmem] * 7 + [hbm] * 5,
        scratch_shapes=[
            pltpu.VMEM((16, 256), F32),
            pltpu.VMEM((16, 256), BF),
            pltpu.VMEM((S, 16, 256), BF),
            pltpu.VMEM((8, R, 256), BF),
            pltpu.VMEM((8, R, 128), BF),
            pltpu.VMEM((S, R, 256), BF),
            pltpu.VMEM((S, R, 128), BF),
            DMA((S,)), DMA((S,)), DMA((S,)), DMA((S,)), DMA((S,)), DMA((S,)),
            DMA((8,)), DMA((8,)), DMA((8,)), DMA((8,)),
            DMA((2, Z, 9)), DMA((2, Z, 9)),
            DMA((G, 9)), DMA((G, 9)),
        ] + Whole.scratch(5, S),
        compiler_params=pltpu.CompilerParams(
            collective_id=0, has_side_effects=True, vmem_limit_bytes=LIMIT
        ),
        name="gather_qkv",
    )(*args)


GROUP = 4


class Reach:
    def __init__(self, causal, bound, block, rows):
        self.causal, self.bound, self.rows = causal, bound, rows
        self.query_first = block * rows
        last = self.query_first + rows - 1
        mixed = (self.query_first < bound) & (last >= bound)
        if causal:
            self.least = jnp.where(self.query_first < bound, 0, bound)
            begin, self.end = self.least // rows, block + 1
            self.mixed = mixed | (self.end < GROUP)
        else:
            per = ENC // rows
            self.least = 0
            begin = jnp.where(self.query_first < bound, 0, per)
            self.end = jnp.where(last < bound, per, 2 * per)
            self.mixed = mixed
        self.groups = (self.end - begin + GROUP - 1) // GROUP

    def mask(self, kind, start, limit, n, scores):
        if kind == "plain":
            return scores
        rows = self.rows
        key = (start + n) * rows + lax.broadcasted_iota(jnp.int32, (rows, 1), 0)
        query = self.query_first + lax.broadcasted_iota(jnp.int32, (1, scores.shape[1]), 1)
        if kind == "edge":
            allowed = (key >= self.least) & (key < limit)
            if n == GROUP - 1:
                allowed = allowed & (key <= query)
        elif self.causal:
            least = jnp.where(query < self.bound, 0, self.bound)
            allowed = (key < limit) & (key <= query) & (key >= least)
        else:
            allowed = jnp.where(query < self.bound, 0, 1) == key // ENC
        return jnp.where(allowed, scores, MASKED)

    def walk(self, group, state):
        def turn(kind, g, carry):
            if kind == "edge":
                g = jnp.where(g == 0, 0, self.groups - 1)
            stop = self.end - GROUP * (self.groups - 1 - g)
            return group(kind, jnp.maximum(stop - GROUP, 0), stop * self.rows, carry)

        mixed, groups = self.mixed, self.groups
        state = lax.fori_loop(
            0, jnp.where(mixed, groups, 0), functools.partial(turn, "full"), state
        )
        if not self.causal:
            return lax.fori_loop(
                0, jnp.where(mixed, 0, groups), functools.partial(turn, "plain"), state
            )
        state = lax.fori_loop(
            0,
            jnp.where(mixed, 0, jnp.minimum(groups, 2)),
            functools.partial(turn, "edge"),
            state,
        )
        return lax.fori_loop(
            1, jnp.where(mixed, 1, groups - 1), functools.partial(turn, "plain"), state
        )


def turned_keys(kv, kt, half, begin, end):
    rows = kv.shape[1]

    def turn(kb, carry):
        flat = kv[kb].astype(F32).T[HD * half : HD * (half + 1)].astype(BF)
        kt[:, pl.ds(pl.multiple_of(kb * rows, rows), rows)] = flat
        return carry

    lax.fori_loop(begin, end, turn, 0)


def key_span(causal, bound, low, Z, rows, count):
    if not causal:
        return 0, count
    return jnp.where(low * rows < bound, 0, bound) // rows, low + 7 * Z + 1


def attend_kernel(Z, causal, info, qt, kv, ot, of, lse, vt):
    bound, m, z = info[0], info[1], info[2]
    count, T = kv.shape[0], kv.shape[1]
    low = 8 * m * Z + z

    begin, end = key_span(causal, bound, low, Z, T, count)
    turned_keys(kv, vt, 1, jnp.maximum(begin - GROUP, 0), end)

    def one_block(i, carry):
        reach = Reach(causal, bound, low + i * Z, T)
        queries = jnp.concatenate([qt[i], jnp.zeros((HD, T), BF)], axis=0)

        def group(kind, start, limit, state):
            top, total, acc = state
            keys = kv[pl.ds(start, GROUP)].reshape(GROUP * T, 128)
            raw = mm(keys, queries)
            scores = [
                reach.mask(kind, start, limit, n, raw[n * T : (n + 1) * T]) for n in range(GROUP)
            ]
            new_top = top
            for piece in scores:
                new_top = jnp.maximum(new_top, jnp.max(piece, axis=0, keepdims=True))
            fade = jnp.exp(top - new_top)
            total = total * fade
            parts = []
            for piece in scores:
                powers = jnp.exp(piece - new_top)
                total = total + jnp.sum(powers, axis=0, keepdims=True)
                parts.append(powers.astype(BF))
            values = vt[:, pl.ds(pl.multiple_of(start * T, T), GROUP * T)]
            acc = acc * fade + mm(values, jnp.concatenate(parts, axis=0))
            return new_top, total, acc

        top, total, acc = reach.walk(
            group,
            (jnp.full((1, T), MASKED, F32), jnp.zeros((1, T), F32), jnp.zeros((HD, T), F32)),
        )
        result = acc / total
        ot[i] = result.astype(BF)
        of[i] = result
        lse[i] = top + jnp.log(total)
        return carry

    lax.fori_loop(0, 8, one_block, 0)


def attend(Z, causal, info, qt, kv):
    T = qt.shape[2]
    sds = jax.ShapeDtypeStruct
    vmem = pl.BlockSpec(memory_space=pltpu.VMEM)
    return pl.pallas_call(
        functools.partial(attend_kernel, Z, causal),
        out_shape=[sds((8, HD, T), BF), sds((8, HD, T), F32), sds((8, 1, T), F32)],
        in_specs=[pl.BlockSpec(memory_space=pltpu.SMEM), vmem, vmem],
        out_specs=[vmem] * 3,
        scratch_shapes=[pltpu.VMEM((HD, kv.shape[0] * T), BF)],
        compiler_params=pltpu.CompilerParams(vmem_limit_bytes=LIMIT),
        name="attend_self" if causal else "attend_cross",
    )(info, qt, kv)


def attend_back_kernel(
    Z, causal, info, qt, kv, dt, of, lse, dq, dkv, kt, dkvf, qd, rows, raw, pair, stage, sem
):
    bound, m, z = info[0], info[1], info[2]
    count, T = kv.shape[0], kv.shape[1]
    low = 8 * m * Z + z
    zero = jnp.zeros((HD, T), BF)

    def clear(kb, carry):
        dkvf[kb] = jnp.zeros((T, 128), F32)
        return carry

    lax.fori_loop(0, count, clear, 0)

    begin, end = key_span(causal, bound, low, Z, T, count)
    turned_keys(kv, kt, 0, jnp.maximum(begin - GROUP, 0), end)

    def one_block(i, carry):
        reach = Reach(causal, bound, low + i * Z, T)
        qd[:HD, :T] = qt[i]
        qd[HD:, :T] = zero
        qd[:HD, T:] = zero
        qd[HD:, T:] = dt[i]
        both = jnp.concatenate([qt[i].astype(F32), dt[i].astype(F32)], axis=0).T
        lane = lax.broadcasted_iota(jnp.int32, both.shape, 1)
        rows[:T] = jnp.where(lane < HD, 0.0, both).astype(BF)
        rows[T:] = jnp.where(lane < HD, both, 0.0).astype(BF)
        delta = jnp.sum(dt[i].astype(F32) * of[i], axis=0, keepdims=True)
        level = lse[i]

        def group(kind, start, limit, acc):
            keys = kv[pl.ds(start, GROUP)].reshape(GROUP * T, 128)
            raw[...] = mm(keys, qd[...])
            for n in range(GROUP):
                at = slice(n * T, (n + 1) * T)
                probs = jnp.exp(reach.mask(kind, start, limit, n, raw[at, :T]) - level)
                pair[at, :T] = probs.astype(BF)
                pair[at, T:] = (probs * (raw[at, T:] - delta)).astype(BF)
            grads = mm(pair[...], rows[...])
            dkvf[pl.ds(start, GROUP)] += grads.reshape(GROUP, T, 128)
            flat = kt[:, pl.ds(pl.multiple_of(start * T, T), GROUP * T)]
            return acc + mm(flat, pair[:, T:])

        acc = reach.walk(group, jnp.zeros((HD, T), F32))
        dq[i] = (SCALE * acc).astype(BF)
        return carry

    lax.fori_loop(0, 8, one_block, 0)

    def put(kb):
        return pltpu.make_async_copy(stage.at[kb % 2], dkv.at[kb], sem.at[kb % 2])

    def flush(kb, carry):
        @pl.when(kb >= 2)
        def _():
            put(kb).wait()

        stage[kb % 2] = dkvf[kb].astype(BF)
        put(kb).start()
        return carry

    lax.fori_loop(0, count, flush, 0)
    put(0).wait()
    put(1).wait()


def attend_back(Z, causal, info, qt, kv, dt, of, lse):
    T = qt.shape[2]
    count = kv.shape[0]
    sds = jax.ShapeDtypeStruct
    vmem = pl.BlockSpec(memory_space=pltpu.VMEM)
    return pl.pallas_call(
        functools.partial(attend_back_kernel, Z, causal),
        out_shape=[sds((8, HD, T), BF), sds(kv.shape, BF)],
        in_specs=[pl.BlockSpec(memory_space=pltpu.SMEM)] + [vmem] * 5,
        out_specs=[vmem, pl.BlockSpec(memory_space=pl.ANY)],
        scratch_shapes=[
            pltpu.VMEM((HD, count * T), BF),
            pltpu.VMEM((count, T, 128), F32),
            pltpu.VMEM((128, 2 * T), BF),
            pltpu.VMEM((2 * T, 128), BF),
            pltpu.VMEM((GROUP * T, 2 * T), F32),
            pltpu.VMEM((GROUP * T, 2 * T), BF),
            pltpu.VMEM((2, T, 128), BF),
            DMA((2,)),
        ],
        compiler_params=pltpu.CompilerParams(vmem_limit_bytes=LIMIT),
        name="attend_self_back" if causal else "attend_cross_back",
    )(info, qt, kv, dt, of, lse)


def greet_group():
    s, z, j, m = place()
    greet([(None, {"shard": m * 8 + (j + d) % 8}) for d in range(1, 8)])


def exchange_copies(src, dst, send, recv):
    s, z, j, m = place()
    out = []
    for d in (1, 2, 3, 4, 5, 6, 7):
        p = flip(j, d)
        out.append(rcopy(src.at[p], dst.at[j], send.at[d], recv.at[j], {"shard": m * 8 + p}))
    return out


def exchange_start(src, dst, send, recv):
    s, z, j, m = place()
    for c in exchange_copies(src, dst, send, recv):
        c.start()
    dst[j] = src[j]


def exchange_recv(src, dst, send, recv):
    s, z, j, m = place()
    for d in (1, 2, 3, 4, 5, 6, 7):
        p = flip(j, d)
        rcopy(src.at[p], dst.at[p], send.at[d], recv.at[p], {"shard": m * 8 + p}).wait_recv()


def exchange_sent(src, dst, send, recv):
    for c in exchange_copies(src, dst, send, recv):
        c.wait_send()


def remote_call(kernel, name, ident, ins, outs, scratch, smem=1, far=()):
    vmem = pl.BlockSpec(memory_space=pltpu.VMEM)
    in_specs = [pl.BlockSpec(memory_space=pltpu.SMEM)] * smem + [vmem] * (len(ins) - smem)
    for n in far:
        in_specs[n] = pl.BlockSpec(memory_space=pl.ANY)
    return pl.pallas_call(
        kernel,
        out_shape=outs,
        in_specs=in_specs,
        out_specs=[vmem] * len(outs),
        scratch_shapes=scratch,
        compiler_params=pltpu.CompilerParams(
            collective_id=ident, has_side_effects=True, vmem_limit_bytes=LIMIT
        ),
        name=name,
    )(*ins)


def middle_kernel(Z, bnd, ot, hid, vecs, wout, wcq, at, after, n2, cqt, cq_send, s1, r1, s2, r2):
    s, z, j, m = place()
    T = hid.shape[0]
    greet_group()
    exchange_start(ot, at, s1, r1)
    base = embed(hid, bnd[0], vecs, s * Z + z)
    exchange_recv(ot, at, s1, r1)
    attn = at[...].reshape(512, T).astype(F32).T.astype(BF)
    value = base + mm(attn, wout[...])
    after[...] = value
    hat, _ = norm_stats(value)
    normed = (hat * vecs[3:4, :] + vecs[6:7, :]).astype(BF)
    n2[...] = normed
    cq = mm(normed, wcq[...])
    cq_send[...] = (SCALE * cq.T).astype(BF).reshape(8, HD, T)
    exchange_start(cq_send, cqt, s2, r2)
    exchange_recv(cq_send, cqt, s2, r2)
    exchange_sent(ot, at, s1, r1)
    exchange_sent(cq_send, cqt, s2, r2)


def middle(Z, bnd, ot, hid, vecs, wout, wcq):
    T = hid.shape[0]
    sds = jax.ShapeDtypeStruct
    return remote_call(
        functools.partial(middle_kernel, Z),
        "middle",
        1,
        (bnd, ot, hid, vecs, wout, wcq),
        [sds((8, HD, T), BF), sds((T, 512), F32), sds((T, 512), BF), sds((8, HD, T), BF)],
        [pltpu.VMEM((8, HD, T), BF), DMA((8,)), DMA((8,)), DMA((8,)), DMA((8,))],
    )


def erf(x):
    return lax.erf(x)


def feed_kernel(
    crt, after, vecs, upb, wco, wup, wdn, grad,
    layer_out, d_after, co_grad, up_grad, dn_grad, smalls, upb_grad, dct,
    ct, send, n3t, out_acc, dn_acc, s1, r1, s2, r2,
):
    T = after.shape[0]
    FF = wup.shape[1]
    greet_group()
    exchange_start(crt, ct, s1, r1)
    g = grad[...]
    gf = g.astype(F32)
    gt = gf.T.astype(BF)
    exchange_recv(crt, ct, s1, r1)
    cross_t = ct[...].reshape(512, T)
    value = after[...] + mm(cross_t.astype(F32).T.astype(BF), wco[...])
    hat, scale = norm_stats(value)
    normed = hat * vecs[4:5, :] + vecs[7:8, :]
    n3 = normed.astype(BF)
    n3t[...] = n3.astype(F32).T.astype(BF)
    out_acc[...] = value + vecs[9:10, :]
    dn_acc[...] = jnp.zeros_like(dn_acc)
    width = 512
    for c in range(FF // width):
        lo, hi = c * width, (c + 1) * width
        pre = mm(n3, wup[:, lo:hi]) + upb[0:1, lo:hi]
        half = 0.5 * (1.0 + erf(pre * (0.5**0.5)))
        middle_c = (pre * half).astype(BF)
        out_acc[...] += mm(middle_c, wdn[lo:hi, :])
        slope = half + pre * (jnp.exp(-0.5 * pre * pre) * ((0.5 / jnp.pi) ** 0.5))
        d_pre = mm(g, wdn[lo:hi, :], 1, 1) * slope
        d_pre_b = d_pre.astype(BF)
        upb_grad[0:1, lo:hi] = jnp.sum(d_pre_b.astype(F32), axis=0, keepdims=True)
        dn_grad[lo:hi, :] = mm(middle_c.astype(F32).T.astype(BF), g).astype(BF)
        up_grad[:, lo:hi] = mm(n3t[...], d_pre_b).astype(BF)
        dn_acc[...] += mm(d_pre_b, wup[:, lo:hi], 1, 1)
    layer_out[...] = out_acc[...].astype(BF)
    d_value, d_gain, d_shift = norm_back(dn_acc[...], hat, scale, vecs[4:5, :])
    total = gf + d_value
    d_after[...] = total
    smalls[0:1, :] = d_gain
    smalls[1:2, :] = d_shift
    smalls[2:3, :] = jnp.sum(gf, axis=0, keepdims=True)
    dc = total.astype(BF)
    d_cross = mm(wco[...], dc, 1, 1)
    send[...] = d_cross.astype(BF).reshape(8, HD, T)
    exchange_start(send, dct, s2, r2)
    co_grad[...] = mm(cross_t, dc).astype(BF)
    exchange_recv(send, dct, s2, r2)
    exchange_sent(crt, ct, s1, r1)
    exchange_sent(send, dct, s2, r2)


def feed(crt, after, vecs, upb, wco, wup, wdn, grad):
    T, FF = after.shape[0], wup.shape[1]
    sds = jax.ShapeDtypeStruct
    return remote_call(
        feed_kernel,
        "feed_forward",
        2,
        (crt, after, vecs, upb, wco, wup, wdn, grad),
        [
            sds((T, 512), BF),
            sds((T, 512), F32),
            sds((512, 512), BF),
            sds((512, FF), BF),
            sds((FF, 512), BF),
            sds((8, 512), F32),
            sds((1, FF), F32),
            sds((8, HD, T), BF),
        ],
        [
            pltpu.VMEM((8, HD, T), BF),
            pltpu.VMEM((8, HD, T), BF),
            pltpu.VMEM((512, T), BF),
            pltpu.VMEM((T, 512), F32),
            pltpu.VMEM((T, 512), F32),
            DMA((8,)), DMA((8,)), DMA((8,)), DMA((8,)),
        ],
        smem=0,
    )


def middle_back_kernel(
    dcqt, after, d_after2, n2, at, vecs, wcq, wout,
    d_after, cq_grad, out_grad, smalls, dat,
    home, send, s1, r1, s2, r2,
):
    T = after.shape[0]
    greet_group()
    exchange_start(dcqt, home, s1, r1)
    hat, scale = norm_stats(after[...])
    n2t = n2[...].astype(F32).T.astype(BF)
    exchange_recv(dcqt, home, s1, r1)
    dcq = home[...].reshape(512, T).astype(F32).T.astype(BF)
    d_value, d_gain, d_shift = norm_back(mm(dcq, wcq[...], 1, 1), hat, scale, vecs[3:4, :])
    total = d_after2[...] + d_value
    d_after[...] = total
    smalls[0:1, :] = d_gain
    smalls[1:2, :] = d_shift
    da = total.astype(BF)
    send[...] = mm(wout[...], da, 1, 1).astype(BF).reshape(8, HD, T)
    exchange_start(send, dat, s2, r2)
    cq_grad[...] = mm(n2t, dcq).astype(BF)
    out_grad[...] = mm(at[...].reshape(512, T), da).astype(BF)
    exchange_recv(send, dat, s2, r2)
    exchange_sent(dcqt, home, s1, r1)
    exchange_sent(send, dat, s2, r2)


def middle_back(dcqt, after, d_after2, n2, at, vecs, wcq, wout):
    T = after.shape[0]
    sds = jax.ShapeDtypeStruct
    return remote_call(
        middle_back_kernel,
        "middle_back",
        3,
        (dcqt, after, d_after2, n2, at, vecs, wcq, wout),
        [
            sds((T, 512), F32),
            sds((512, 512), BF),
            sds((512, 512), BF),
            sds((8, 512), F32),
            sds((8, HD, T), BF),
        ],
        [
            pltpu.VMEM((8, HD, T), BF),
            pltpu.VMEM((8, HD, T), BF),
            DMA((8,)), DMA((8,)), DMA((8,)), DMA((8,)),
        ],
        smem=0,
    )


NC = 16


def last_kernel(
    S, Z, G,
    info, hid, vecs, d_after, x_all, enc_all, dqt, dkv, dmkv, wproj_s, wmem_s,
    out_g, cq_g, co_g, up_g, dn_g, small2, small3, upb_g,
    hidden_grad, encoder_grad, zfin, smalls_o,
    wproj_all, wmem_all,
    sib_out, sib_cq, sib_co, sib_up, sib_dn, got_out, got_cq, got_co, got_up, got_dn,
    rk, rm, fin, finm, mbuf, mbufm, hkv, hq, hm, turned, enc_turned, dall, psend, pgot, msend, mgot,
    wz, zin, sm_all, sm_z, sm_plane, sm_mine,
    a_s, a_r, b_s, b_r, k_s, k_r, mb_s, mb_r, hq_s, hq_r, hk_s, hk_r, hm_s, hm_r,
    p_s, p_r, pm_s, pm_r, c_s, c_r, f_s, f_r, sm_s, sm_r, sz_s, sz_r, *whole_sems
):
    s, z, j, m = place()
    T, E = hid.shape[0], enc_all.shape[1]
    R = 512 // S
    F = dn_g.shape[0] // S
    bound = info[0]
    chips = S // 2
    core, chip = s % 2, s // 2
    sib = flip(s, 1)
    ends = (Z - 1, 0)
    greet(
        [(None, {"shard": (s + d) % S}) for d in range(1, S)]
        + [(None, {"seq": (z + d) % Z}) for d in range(1, Z)]
    )
    grads = ((out_g, R), (cq_g, R), (co_g, R), (up_g, R), (dn_g, F))
    sibs = (sib_out, sib_cq, sib_co, sib_up, sib_dn)
    gots = (got_out, got_cq, got_co, got_up, got_dn)

    def piece(a, p):
        ref, rows = grads[a]
        return ref.at[pl.ds(pl.multiple_of(p * rows, rows), rows), :]

    if G > 1:
        for d in range(1, G):
            o = (m + d) % G
            rcopy(dkv.at[o], mbuf.at[m], mb_s.at[d, 0], mb_r.at[m, 0], {"shard": o * 8 + j}).start()
            rcopy(dmkv.at[o], mbufm.at[m], mb_s.at[d, 1], mb_r.at[m, 1], {"shard": o * 8 + j}).start()
        own_part = pltpu.make_async_copy(dkv.at[m], mbuf.at[m], mb_s.at[0, 0])
        own_part.start()
        own_part.wait()
        for d in range(1, G):
            o = (m + d) % G
            rcopy(dkv.at[o], mbuf.at[o], mb_s.at[d, 0], mb_r.at[o, 0], {"shard": o * 8 + j}).wait_recv()
            rcopy(dmkv.at[o], mbufm.at[o], mb_s.at[d, 1], mb_r.at[o, 1], {"shard": o * 8 + j}).wait_recv()
        for b in range(8):
            acc = mbuf[m, b].astype(F32)
            accm = dmkv[m, b].astype(F32)
            for d in range(1, G):
                acc = acc + mbuf[(m + d) % G, b].astype(F32)
                accm = accm + mbufm[(m + d) % G, b].astype(F32)
            mbuf[m, b] = acc.astype(BF)
            mbufm[m, b] = accm.astype(BF)
        part, partm = mbuf.at[m], mbufm.at[m]
    else:
        part, partm = dkv.at[0], dmkv.at[0]

    def z_view(slot, t):
        return part.at[slot, t] if slot < 8 else partm.at[:, t]

    def z_buffer(way, t, slot):
        return rk.at[way, t, slot] if slot < 8 else rm.at[way, t]

    def z_copy(way, t, slot, source):
        step = 2 * way - 1
        return rcopy(
            source, z_buffer(way, t, slot), k_s.at[way, t, slot], k_r.at[way, t, slot], {"seq": z + step}
        )

    for far in range(Z - 1, 0, -1):
        for slot in range(9):
            for way in (0, 1):
                t = z + (2 * way - 1) * far

                @pl.when((z == ends[way]) & (t >= 0) & (t < Z))
                def _(way=way, t=t, slot=slot):
                    z_copy(way, t, slot, z_view(slot, t)).start()

    def sib_copy(a, q):
        return rcopy(piece(a, 2 * q + 1 - core), sibs[a].at[q], a_s.at[a, q], a_r.at[a, q], {"shard": sib})

    for a in range(5):
        for q in range(chips):
            sib_copy(a, q).start()
    exchange_start(dqt, hq, hq_s, hq_r)
    whole = Whole(((wproj_s, wproj_all), (wmem_s, wmem_all)), S, whole_sems)

    def own_copy(a, q):
        return rcopy(
            sibs[a].at[q], gots[a].at[chip], b_s.at[a, q], b_r.at[a, chip], {"shard": 2 * q + core}
        )

    def chip_sum(a):
        for d in range(chips):
            q = (chip + d + 1) % chips
            sib_copy(a, q).wait_recv()
            sibs[a][q] = (
                sibs[a][q].astype(F32) + piece(a, 2 * q + core)[...].astype(F32)
            ).astype(BF)
            if d < chips - 1:
                own_copy(a, q).start()

    def turn_block(b):
        turned[:, b * T : (b + 1) * T] = x_all[b].astype(F32).T.astype(BF)

    def turn_query(b):
        dq_b = dqt[b].astype(F32)
        dall[b * T : (b + 1) * T, 128:] = (
            jnp.concatenate([dq_b, jnp.zeros_like(dq_b)], axis=0).T.astype(BF)
        )

    def turn_encoder():
        enc_turned[...] = enc_all[...].reshape(8 * E, 512).astype(F32).T.astype(BF)

    def start_whole():
        whole.start(0)
        whole.start(1)

    def relay_whole():
        whole.relay(0)
        whole.relay(1)

    def finish_whole():
        whole.finish(0)
        whole.finish(1)

    def own_sum(a):
        for d in range(1, chips):
            q = (chip + d) % chips
            rcopy(sibs[a].at[q], gots[a].at[q], b_s.at[a, q], b_r.at[a, q], {"shard": 2 * q + core}).wait_recv()
        total = sibs[a][chip].astype(F32)
        for d in range(1, chips):
            total = total + gots[a][(chip + d) % chips].astype(F32)
        total = total.astype(BF)
        if a < 3:
            wz[a] = total
        elif a == 3:
            for c in range(4):
                wz[3 + c] = total[:, 512 * c : 512 * (c + 1)]
        else:
            for c in range(4):
                wz[7 + c] = total[c * R : (c + 1) * R]

    block = s * Z + z
    work = [functools.partial(chip_sum, a) for a in range(5)] + [start_whole]
    work += [functools.partial(turn_block, b) for b in range(8)]
    work += [functools.partial(turn_query, b) for b in range(8)] + [turn_encoder]
    late = [relay_whole, finish_whole]

    for far in range(Z - 1, 0, -1):
        for slot in range(9):
            if work:
                work.pop(0)()
            for way in (0, 1):
                t = z + (2 * way - 1) * far

                @pl.when((z != ends[way]) & (t >= 0) & (t < Z))
                def _(way=way, t=t, slot=slot):
                    z_copy(way, t, slot, z_view(slot, t)).wait_recv()
                    buf = z_buffer(way, t, slot)
                    buf[...] = (
                        buf[...].astype(F32) + z_view(slot, t)[...].astype(F32)
                    ).astype(BF)
                    z_copy(way, t, slot, buf).start()

    def inward(k, step):
        way = (step + 1) // 2
        return rcopy(wz.at[k], zin.at[way, k], c_s.at[way, k], c_r.at[way, k], {"seq": z + step})

    def outward(k, step):
        return rcopy(zfin.at[k], zfin.at[k], f_s.at[(step + 1) // 2, k], f_r.at[k], {"seq": z + step})

    def root(k):
        return max(Z // 2 - 1 + k % 2, 0) if Z > 1 else 0

    def tips(k):
        r = root(k)
        for step in (-1, 1):
            tip = ends[(step + 1) // 2]
            if tip != r:

                @pl.when(z == tip)
                def _(step=step):
                    inward(k, step).start()

    def partial(k):
        r = root(k)
        for step, beyond in ((-1, z > r), (1, z < r)):
            tip = ends[(step + 1) // 2]
            way = (step + 1) // 2

            @pl.when(beyond & (z != tip))
            def _(step=step, way=way):
                inward(k, step).wait_recv()
                wz[k] = (wz[k].astype(F32) + zin[way, k].astype(F32)).astype(BF)
                inward(k, step).start()

    def total_of(k):
        r = root(k)

        @pl.when(z == r)
        def _():
            total = wz[k].astype(F32)
            if r < Z - 1:
                inward(k, -1).wait_recv()
                total = total + zin[0, k].astype(F32)
            if r > 0:
                inward(k, 1).wait_recv()
                total = total + zin[1, k].astype(F32)
            zfin[k] = total.astype(BF)
            if r < Z - 1:
                outward(k, 1).start()
            if r > 0:
                outward(k, -1).start()

    def send_out(k):
        r = root(k)
        for step, beyond in ((1, z > r), (-1, z < r)):
            tip = Z - 1 if step > 0 else 0

            @pl.when(beyond)
            def _(step=step, tip=tip):
                outward(k, step).wait_recv()

                @pl.when(z != tip)
                def _():
                    outward(k, step).start()

    for task in work:
        task()
    psend_q = mm(turned[...], dall[:, 128:])
    for a in range(5):
        own_sum(a)
        for k in ((0,), (1,), (2,), (3, 4, 5, 6), (7, 8, 9, 10))[a]:
            tips(k)
    hat, scale = norm_stats(embed(hid, bound, vecs, block))
    relay_whole()

    for slot in range(9):
        for way in (0, 1):

            @pl.when(z != ends[way])
            def _(way=way, slot=slot):
                z_copy(way, z, slot, z_view(slot, z)).wait_recv()

        low = jnp.where(z == ends[0], 0.0, z_buffer(0, z, slot)[...].astype(F32))
        high = jnp.where(z == ends[1], 0.0, z_buffer(1, z, slot)[...].astype(F32))
        total = (low + high + z_view(slot, z)[...].astype(F32)).astype(BF)
        if slot < 8:
            fin[slot] = total
            dall[slot * T : (slot + 1) * T, :128] = total
        else:
            finm[...] = total
    exchange_start(fin, hkv, hk_s, hk_r)
    exchange_start(finm, hm, hm_s, hm_r)
    for k in range(7):
        partial(k)

    psend_kv = mm(turned[...], dall[:, :128])
    psend[...] = jnp.concatenate([psend_kv, psend_q], axis=1).astype(BF).reshape(S, R, 256)
    msend[...] = mm(enc_turned[...], finm[...].reshape(8 * E, 128)).astype(BF).reshape(S, R, 128)
    pgot[s] = psend[s]
    mgot[s] = msend[s]
    for d in range(1, S):
        p = (s + d) % S
        rcopy(psend.at[p], pgot.at[s], p_s.at[d], p_r.at[s], {"shard": p}).start()
        rcopy(msend.at[p], mgot.at[s], pm_s.at[d], pm_r.at[s], {"shard": p}).start()

    finish_whole()
    for k in range(7, 11):
        partial(k)
        total_of(k - 7)

    exchange_recv(dqt, hq, hq_s, hq_r)
    exchange_recv(fin, hkv, hk_s, hk_r)
    exchange_recv(finm, hm, hm_s, hm_r)
    whole.wait(0)
    whole.wait(1)
    wproj = wproj_all[...].reshape(512, 1536)
    d_query = hq[...].reshape(512, T).astype(F32).T.astype(BF)
    d_keys = jnp.concatenate([hkv[h][:, :HD] for h in range(H)], axis=1)
    d_values = jnp.concatenate([hkv[h][:, HD:] for h in range(H)], axis=1)
    d_norm = (
        mm(d_query, wproj[:, :512], 1, 1)
        + mm(d_keys, wproj[:, 512:1024], 1, 1)
        + mm(d_values, wproj[:, 1024:], 1, 1)
    )
    d_value, d_gain, d_shift = norm_back(d_norm, hat, scale, vecs[2:3, :])
    total = d_after[...] + d_value
    hidden_grad[...] = total
    pos = block * T + lax.broadcasted_iota(jnp.int32, (T, 1), 0)
    sm_mine[...] = jnp.zeros((16, 512), F32)
    sm_mine[0:1, :] = d_gain
    sm_mine[1:2, :] = small2[0:1, :]
    sm_mine[2:3, :] = small3[0:1, :]
    sm_mine[3:4, :] = d_shift
    sm_mine[4:5, :] = small2[1:2, :]
    sm_mine[5:6, :] = small3[1:2, :]
    sm_mine[6:7, :] = jnp.sum(jnp.where(pos < bound, total, 0.0), axis=0, keepdims=True)
    sm_mine[7:8, :] = jnp.sum(jnp.where(pos < bound, 0.0, total), axis=0, keepdims=True)
    sm_mine[8:9, :] = small3[2:3, :]
    for c in range(upb_g.shape[1] // 512):
        sm_mine[9 + c : 10 + c, :] = upb_g[0:1, 512 * c : 512 * (c + 1)]
    for d in range(1, S):
        rcopy(sm_mine, sm_all.at[s], sm_s.at[d], sm_r.at[s], {"shard": (s + d) % S}).start()
    sm_all[s] = sm_mine[...]

    for k in range(4, 8):
        total_of(k)

    for d in range(1, S):
        p = (s + d) % S
        rcopy(psend.at[p], pgot.at[p], p_s.at[d], p_r.at[p], {"shard": p}).wait_recv()
        rcopy(msend.at[p], mgot.at[p], pm_s.at[d], pm_r.at[p], {"shard": p}).wait_recv()
    heads, mheads = [], []
    for h in range(H):
        acc, accm = pgot[h].astype(F32), mgot[h].astype(F32)
        for g in range(1, G):
            acc = acc + pgot[8 * g + h].astype(F32)
            accm = accm + mgot[8 * g + h].astype(F32)
        heads.append(acc)
        mheads.append(accm)
    wz[11] = jnp.concatenate([v[:, 128 : 128 + HD] for v in heads], axis=1).astype(BF)
    wz[12] = jnp.concatenate([v[:, :HD] for v in heads], axis=1).astype(BF)
    wz[13] = jnp.concatenate([v[:, HD:128] for v in heads], axis=1).astype(BF)
    wz[14] = jnp.concatenate([v[:, :HD] for v in mheads], axis=1).astype(BF)
    wz[15] = jnp.concatenate([v[:, HD:] for v in mheads], axis=1).astype(BF)
    for k in range(11, NC):
        tips(k)
    e_keys = jnp.concatenate([hm[h][:, :HD] for h in range(H)], axis=1)
    e_values = jnp.concatenate([hm[h][:, HD:] for h in range(H)], axis=1)
    wmem = wmem_all[...].reshape(512, 1024)
    encoder_grad[...] = mm(e_keys, wmem[:, :512], 1, 1) + mm(e_values, wmem[:, 512:], 1, 1)

    for d in range(1, S):
        p = (s + d) % S
        rcopy(sm_mine, sm_all.at[p], sm_s.at[d], sm_r.at[p], {"shard": p}).wait_recv()
    acc = sm_all[0]
    for p in range(1, S):
        acc = acc + sm_all[p]
    sm_plane[...] = acc
    for d in range(1, Z):
        rcopy(sm_plane, sm_z.at[z], sz_s.at[d], sz_r.at[z], {"seq": (z + d) % Z}).start()
    sm_z[z] = acc
    for k in range(NC):
        if k + 11 < NC:
            partial(k + 11)
        if k + 8 < NC:
            total_of(k + 8)
        send_out(k)
    for d in range(1, Z):
        o = (z + d) % Z
        rcopy(sm_plane, sm_z.at[o], sz_s.at[d], sz_r.at[o], {"seq": o}).wait_recv()
    acc = sm_z[0]
    for o in range(1, Z):
        acc = acc + sm_z[o]
    smalls_o[...] = acc

    whole.drain()
    for a in range(5):
        for q in range(chips):
            sib_copy(a, q).wait_send()
        for d in range(1, chips):
            own_copy(a, (chip + d) % chips).wait_send()
    for d in range(1, G):
        o = (m + d) % G
        rcopy(dkv.at[o], mbuf.at[m], mb_s.at[d, 0], mb_r.at[m, 0], {"shard": o * 8 + j}).wait_send()
        rcopy(dmkv.at[o], mbufm.at[m], mb_s.at[d, 1], mb_r.at[m, 1], {"shard": o * 8 + j}).wait_send()
    exchange_sent(dqt, hq, hq_s, hq_r)
    exchange_sent(fin, hkv, hk_s, hk_r)
    exchange_sent(finm, hm, hm_s, hm_r)
    for far in range(Z - 1, 0, -1):
        for slot in range(9):
            for way in (0, 1):
                t = z + (2 * way - 1) * far

                @pl.when((t >= 0) & (t < Z))
                def _(way=way, t=t, slot=slot):
                    z_copy(way, t, slot, z_view(slot, t)).wait_send()

    for d in range(1, S):
        p = (s + d) % S
        rcopy(psend.at[p], pgot.at[s], p_s.at[d], p_r.at[s], {"shard": p}).wait_send()
        rcopy(msend.at[p], mgot.at[s], pm_s.at[d], pm_r.at[s], {"shard": p}).wait_send()
        rcopy(sm_mine, sm_all.at[s], sm_s.at[d], sm_r.at[s], {"shard": p}).wait_send()
    for d in range(1, Z):
        rcopy(sm_plane, sm_z.at[z], sz_s.at[d], sz_r.at[z], {"seq": (z + d) % Z}).wait_send()
    for k in range(NC):
        r = root(k)
        for step, beyond in ((-1, z > r), (1, z < r)):

            @pl.when(beyond)
            def _(step=step):
                inward(k, step).wait_send()

        for step in (-1, 1):
            sends = (z >= r) & (z < Z - 1) if step > 0 else (z <= r) & (z > 0)

            @pl.when(sends)
            def _(step=step):
                outward(k, step).wait_send()


def finish_kernel(
    info, timestep, zfin, sums, hid_g, enc_g, lay,
    lay_o, hid_o, enc_o, time_o, gain_o, shift_o, proj_o, out_o, cq_o, mem_o, co_o, up_o, upb_o, dn_o, dnb_o,
):
    s = info[3]
    R, F = out_o.shape[0], upb_o.shape[1]
    lay_o[...] = lay[...]
    hid_o[...] = hid_g[...]
    enc_o[...] = enc_g[...]
    out_o[...] = zfin[0].astype(F32)
    cq_o[...] = zfin[1].astype(F32)
    co_o[...] = zfin[2].astype(F32)
    for c in range(4):
        up_o[:, 512 * c : 512 * (c + 1)] = zfin[3 + c].astype(F32)
        dn_o[c * R : (c + 1) * R, :] = zfin[7 + c].astype(F32)
    for c in range(3):
        proj_o[:, 512 * c : 512 * (c + 1)] = zfin[11 + c].astype(F32)
    for c in range(2):
        mem_o[:, 512 * c : 512 * (c + 1)] = zfin[14 + c].astype(F32)

    def own(width, first):
        row = lax.broadcasted_iota(jnp.int32, (512, width), 0)
        col = lax.broadcasted_iota(jnp.int32, (512, width), 1)
        pick = jnp.where(row == col + first, 1.0, 0.0)
        return lax.dot_general(
            sums[...], pick, (((1,), (0,)), ((), ())),
            preferred_element_type=F32, precision=lax.Precision.HIGHEST,
        )

    mine = own(R, s * R)
    gain_o[...] = mine[0:3]
    shift_o[...] = mine[3:6]
    dnb_o[...] = mine[8:9]
    step = lax.broadcasted_iota(jnp.int32, time_o.shape, 0)
    grad = jnp.zeros(time_o.shape, F32)
    for d in range(DOCS):
        grad = grad + jnp.where(step == timestep[d], mine[6 + d : 7 + d], 0.0)
    time_o[...] = grad
    wide = own(F, (s * F) % 512)
    row = lax.broadcasted_iota(jnp.int32, wide.shape, 0)
    upb_o[...] = jnp.sum(jnp.where(row == 9 + s * F // 512, wide, 0.0), axis=0, keepdims=True)


def last(v):
    S, Z, G = v["S"], v["Z"], v["G"]
    T, R, F, E = v["T"], v["R"], v["F"], v["encoder"].shape[0]
    FF = v["wup"].shape[1]
    chips = S // 2
    sds = jax.ShapeDtypeStruct
    V = pltpu.VMEM
    GM, ZM = (G, Z) if G > 1 else (1, 1)
    hidden_grad, encoder_grad, zfin, sums = remote_call(
        functools.partial(last_kernel, S, Z, G),
        "gradients_home",
        4,
        (
            v["info"], v["hidden_in"], v["vecs"], v["d_after"], v["x_all"], v["enc_all"], v["dqt"],
            v["dkv"].reshape(G, 8, Z, T, 128), v["dmkv"].reshape(G, 8, Z, E, 128),
            v["self_proj"], v["cross_memory"],
            v["wout_grad"], v["cq_grad"], v["co_grad"], v["up_grad"], v["dn_grad"],
            v["small2"], v["small3"], v["upb_grad"],
        ),
        [sds((T, 512), F32), sds((E, 512), F32), sds((NC, R, 512), BF), sds((16, 512), F32)],
        [V((S, R, 1536), BF), V((S, R, 1024), BF)]
        + [V((chips, R, 512), BF)] * 3 + [V((chips, R, FF), BF), V((chips, F, 512), BF)]
        + [V((chips, R, 512), BF)] * 3 + [V((chips, R, FF), BF), V((chips, F, 512), BF)]
        + [
            V((2, Z, 8, T, 128), BF), V((2, Z, 8, E, 128), BF),
            V((8, T, 128), BF), V((8, E, 128), BF),
            V((GM, 8, ZM, T, 128), BF), V((GM, 8, ZM, E, 128), BF),
            V((8, T, 128), BF), V((8, HD, T), BF), V((8, E, 128), BF),
            V((512, 8 * T), BF), V((512, 8 * E), BF), V((8 * T, 256), BF),
            V((S, R, 256), BF), V((S, R, 256), BF), V((S, R, 128), BF), V((S, R, 128), BF),
            V((NC, R, 512), BF), V((2, NC, R, 512), BF),
            V((S, 16, 512), F32), V((Z, 16, 512), F32), V((16, 512), F32), V((16, 512), F32),
            DMA((5, chips)), DMA((5, chips)), DMA((5, chips)), DMA((5, chips)),
            DMA((2, Z, 9)), DMA((2, Z, 9)), DMA((G, 2)), DMA((G, 2)),
            DMA((8,)), DMA((8,)), DMA((8,)), DMA((8,)), DMA((8,)), DMA((8,)),
            DMA((S,)), DMA((S,)), DMA((S,)), DMA((S,)),
            DMA((2, NC)), DMA((2, NC)), DMA((2, NC)), DMA((NC,)),
            DMA((S,)), DMA((S,)), DMA((Z,)), DMA((Z,)),
        ] + Whole.scratch(2, S),
        far=(7,) if G > 1 else (),
    )
    vmem = pl.BlockSpec(memory_space=pltpu.VMEM)
    smem = pl.BlockSpec(memory_space=pltpu.SMEM)
    steps = v["time_table"].shape[0]
    outs = [
        sds((T, 512), BF), sds((T, 512), F32), sds((E, 512), F32), sds((steps, R), F32), sds((3, R), F32),
        sds((3, R), F32), sds((R, 1536), F32), sds((R, 512), F32), sds((R, 512), F32), sds((R, 1024), F32),
        sds((R, 512), F32), sds((R, FF), F32), sds((1, F), F32), sds((F, 512), F32), sds((1, R), F32),
    ]
    res = pl.pallas_call(
        finish_kernel,
        out_shape=outs,
        in_specs=[smem, smem] + [vmem] * 5,
        out_specs=[vmem] * len(outs),
        compiler_params=pltpu.CompilerParams(vmem_limit_bytes=LIMIT),
        name="outputs",
    )(v["info"], v["timestep"], zfin, sums, hidden_grad, encoder_grad, v["layer_out"])
    res = list(res)
    res[12] = res[12].reshape(F)
    res[14] = res[14].reshape(R)
    return tuple(res)


def shards(
    hidden_in, encoder, segment_ids, timestep, out_grad, time_table, norm_gain, norm_bias,
    self_proj, self_out, cross_query, cross_memory, cross_out, up_weight, up_bias, down_weight, down_bias,
):
    S, Z = lax.axis_size("shard"), lax.axis_size("seq")
    T, R, F = hidden_in.shape[0], self_proj.shape[0], up_bias.shape[0]
    G = S // 8
    info, x_all, kv, qt, mkv, enc_all, vecs, upb, gout, gcq, gco, gup, gdn = gather_call(
        S,
        Z,
        (
            timestep, segment_ids.reshape(-1, 128), hidden_in, time_table, norm_gain, norm_bias,
            up_bias[None], down_bias[None], self_proj, cross_memory, encoder,
            self_out, cross_query, cross_out, up_weight, down_weight,
        ),
    )
    wout, wcq, wco = gout.reshape(512, 512), gcq.reshape(512, 512), gco.reshape(512, 512)
    wup, wdn = gup.reshape(512, -1), gdn.reshape(-1, 512)
    kv = kv.reshape(S * Z, T, 128)
    mkv = mkv.reshape(DOCS * ENC // T, T, 128)

    ot, of, lse = attend(Z, True, info, qt, kv)
    at, after, n2, cqt = middle(Z, info, ot, hidden_in, vecs, wout, wcq)
    crt, crf, clse = attend(Z, False, info, cqt, mkv)
    layer_out, d_after2, co_grad, up_grad, dn_grad, small3, upb_grad, dct = feed(
        crt, after, vecs, upb, wco, wup, wdn, out_grad
    )
    dcqt, dmkv = attend_back(Z, False, info, cqt, mkv, dct, crf, clse)
    d_after, cq_grad, wout_grad, small2, dat = middle_back(
        dcqt, after, d_after2, n2, at, vecs, wcq, wout
    )
    dqt, dkv = attend_back(Z, True, info, qt, kv, dat, of, lse)
    return last(locals())


def solution(mesh):
    return jax.shard_map(
        shards,
        mesh=mesh,
        in_specs=(
            P(("shard", "seq"), None),
            P(("shard", "seq"), None),
            P(),
            P(),
            P(("shard", "seq"), None),
            P(None, "shard"),
            P(None, "shard"),
            P(None, "shard"),
            P("shard", None),
            P("shard", None),
            P("shard", None),
            P("shard", None),
            P("shard", None),
            P("shard", None),
            P("shard"),
            P("shard", None),
            P("shard"),
        ),
        out_specs=(
            P(("shard", "seq"), None),
            P(("shard", "seq"), None),
            P(("shard", "seq"), None),
            P(None, "shard"),
            P(None, "shard"),
            P(None, "shard"),
            P("shard", None),
            P("shard", None),
            P("shard", None),
            P("shard", None),
            P("shard", None),
            P("shard", None),
            P("shard"),
            P("shard", None),
            P("shard"),
        ),
        check_vma=False,
    )
```

```python
import functools

import jax
import jax.numpy as jnp
from jax import lax
from jax.experimental import pallas as pl
from jax.experimental.pallas import tpu as pltpu
from jax.sharding import PartitionSpec as P

H = 8
HD = 64
DOCS = 2
ENC = 1024
EPS = 1e-05
MASKED = -1e30
SCALE = HD**-0.5
MESH = pl.DeviceIdType.MESH
BF = jnp.bfloat16
F32 = jnp.float32
DMA = pltpu.SemaphoreType.DMA


def room(small=True):
    return (ROOM << 20) if small and lax.axis_size("shard") == 8 else (63 << 20)


ROOM = 30
ORDER = (0, 1, 2, 4, 3, 6, 5, 7)


def mm(a, b, ca=1, cb=0):
    return lax.dot_general(a, b, (((ca,), (cb,)), ((), ())), preferred_element_type=F32)


def flip(j, bits):
    low, mid, high = j % 2, (j // 2) % 2, (j // 4) % 2
    out = j
    if bits & 1:
        out = out + 1 - 2 * low
    if bits & 2:
        out = out + 2 - 4 * mid
    if bits & 4:
        out = out + 4 - 8 * high
    return out


def rcopy(src, dst, send_sem, recv_sem, device_id):
    return pltpu.make_async_remote_copy(
        src_ref=src,
        dst_ref=dst,
        send_sem=send_sem,
        recv_sem=recv_sem,
        device_id=device_id,
        device_id_type=MESH,
    )


def place():
    shard, seq = lax.axis_index("shard"), lax.axis_index("seq")
    return shard, seq, shard % 8, shard // 8


def greet(peers):
    barrier = pltpu.get_barrier_semaphore()
    count = 0
    for condition, device in peers:
        if condition is None:
            pl.semaphore_signal(barrier, inc=1, device_id=device, device_id_type=MESH)
            count = count + 1
        else:

            @pl.when(condition)
            def _(device=device):
                pl.semaphore_signal(barrier, inc=1, device_id=device, device_id_type=MESH)

            count = count + jnp.where(condition, 1, 0)
    pl.semaphore_wait(barrier, count)


def norm_stats(value):
    center = jnp.mean(value, axis=1, keepdims=True)
    offset = value - center
    spread = jnp.mean(offset * offset, axis=1, keepdims=True)
    scale = lax.rsqrt(spread + EPS)
    return offset * scale, scale


def norm_back(d_out, hat, scale, gain):
    d_hat = d_out * gain
    first = jnp.mean(d_hat, axis=1, keepdims=True)
    second = jnp.mean(d_hat * hat, axis=1, keepdims=True)
    d_in = scale * (d_hat - first - hat * second)
    return d_in, jnp.sum(d_out * hat, axis=0, keepdims=True), jnp.sum(d_out, axis=0, keepdims=True)


def embed(hid_ref, bound, vecs_ref, block):
    rows = hid_ref.shape[0]
    pos = block * rows + lax.broadcasted_iota(jnp.int32, (rows, 1), 0)
    picked = jnp.where(pos < bound, vecs_ref[0:1, :], vecs_ref[1:2, :])
    return hid_ref[...].astype(F32) + picked


class Whole:
    def __init__(self, pairs, S, sems):
        self.pairs, self.S = pairs, S
        self.local, self.send, self.recv, self.half, self.pass_on = sems
        self.s = lax.axis_index("shard")
        self.core, self.chip = self.s % 2, self.s // 2
        self.sib = flip(self.s, 1)
        self.near = S == 8
        self.flow = []

    @staticmethod
    def scratch(count, S):
        return [DMA((count,)), DMA((count, max(8, S // 2))), DMA((count, S)), DMA((count, 2)), DMA((count, S // 2))]

    def copy(self, a, source, n, to, half=None):
        shard, whole = self.pairs[a]
        target = whole.at[source]
        if half is not None:
            rows = shard.shape[0] // 2
            target = whole.at[source, pl.ds(half * rows, rows)]
            recv = self.half.at[a, half]
        else:
            recv = self.recv.at[a, source]
        origin = shard if n < 0 else target
        send = self.send.at[a, -n - 1 if n < 0 else n]
        return rcopy(origin, target, send, recv, {"shard": to})

    def go(self, *args):
        c = self.copy(*args)
        c.start()
        self.flow.append(c)

    def arrived(self, a, source, half=None):
        self.copy(a, source, 7, self.sib, half).wait_recv()

    def same_core(self, d):
        return ((self.chip + d) % (self.S // 2)) * 2 + self.core

    def start(self, a):
        shard, whole = self.pairs[a]
        pltpu.make_async_copy(shard, whole.at[self.s], self.local.at[a]).start()
        s = self.s
        if self.near:
            self.go(a, s, -1, flip(s, 2))
            self.go(a, s, -2, flip(s, 4))
            self.go(a, s, -3, self.sib)
            return
        for d in range(1, self.S // 2):
            c = rcopy(shard, whole.at[s], self.send.at[a, d], self.recv.at[a, s], {"shard": self.same_core(d)})
            c.start()
            self.flow.append(c)
        c = rcopy(shard, whole.at[s], self.send.at[a, 0], self.recv.at[a, s], {"shard": self.sib})
        c.start()
        self.flow.append(c)

    def relay(self, a):
        if not self.near:
            return
        x, y = flip(self.s, 2), flip(self.s, 4)
        self.arrived(a, x)
        self.go(a, x, 3, y, 0)
        self.go(a, x, 5, self.sib)
        self.arrived(a, y)
        self.go(a, y, 4, x, 1)
        self.go(a, y, 6, self.sib)

    def finish(self, a):
        if self.near:
            far = flip(self.s, 6)
            self.arrived(a, far, 0)
            self.arrived(a, far, 1)
            self.go(a, far, 7, self.sib)
            return
        _, whole = self.pairs[a]
        for d in range(1, self.S // 2):
            q = self.same_core(self.S // 2 - d)
            self.arrived(a, q)
            c = rcopy(whole.at[q], whole.at[q], self.pass_on.at[a, d], self.recv.at[a, q], {"shard": self.sib})
            c.start()
            self.flow.append(c)

    def wait(self, a):
        shard, whole = self.pairs[a]
        self.arrived(a, self.sib)
        for d in range(1, self.S // 2):
            self.arrived(a, flip(self.same_core(d), 1))
        pltpu.make_async_copy(shard, whole.at[self.s], self.local.at[a]).wait()

    def drain(self):
        for c in self.flow:
            c.wait_send()


def gather_kernel(
    S, Z, G,
    timestep, seg_h, hid_h, table_h, gain_h, shift_h, upb_h, dnb_h, wproj_h, wmem_h, enc_h,
    wout, wcq, wco, wup, wdn,
    info, x_all, kv, qt, mkv, enc_all, vecs, upb_row, gout, gcq, gco, gup, gdn,
    seg, hid, table, gain, shift, upb, dnb, wproj, wmem, enc, in_sem,
    rows_f, small, small_all, wsend, msend, w_all, m_all, sm_s, sm_r, w_s, w_r, mw_s, mw_r,
    x_s, x_r, e_s, e_r, z_s, z_r, mb_s, mb_r, *whole_sems
):
    s, z, j, m = place()
    near = (seg, hid, table, gain, shift, upb, dnb, wproj, wmem, enc)
    far = (seg_h, hid_h, table_h, gain_h, shift_h, upb_h, dnb_h, wproj_h, wmem_h, enc_h)
    loads = [pltpu.make_async_copy(b, a, in_sem.at[n]) for n, (a, b) in enumerate(zip(near, far))]
    for c in loads:
        c.start()
    for c in loads:
        c.wait()
    R, F = wproj.shape[0], upb.shape[0]
    T, E = hid.shape[0], enc.shape[0]
    sib = flip(s, 1)

    step = lax.broadcasted_iota(jnp.int32, table.shape, 0)
    rows_f[...] = jnp.zeros((16, 256), F32)
    for d in range(DOCS):
        picked = jnp.where(step == timestep[d], table[...].astype(F32), 0.0)
        rows_f[d : d + 1, :R] = jnp.sum(picked, axis=0, keepdims=True)
    rows_f[2:5, :R] = gain[...].astype(F32)
    rows_f[5:8, :R] = shift[...].astype(F32)
    rows_f[8:9, :F] = upb[...].astype(F32).reshape(1, F)
    rows_f[9:10, :R] = dnb[...].astype(F32).reshape(1, R)
    small[...] = rows_f[...].astype(BF)
    small_all[s] = small[...]
    bound = jnp.sum(jnp.where(seg[...] == 0, 1.0, 0.0)).astype(jnp.int32)
    info[0] = bound
    info[1] = m
    info[2] = z
    info[3] = s

    greet(
        [(None, {"shard": (s + d) % S}) for d in range(1, S)]
        + [(z > 0, {"seq": z - 1}), (z < Z - 1, {"seq": z + 1})]
    )
    small_copies = []
    for d in range(1, S):
        c = rcopy(small, small_all.at[s], sm_s.at[d], sm_r.at[s], {"shard": (s + d) % S})
        c.start()
        small_copies.append(c)
    for h in range(H):
        k = wproj[:, 512 + HD * h : 512 + HD * (h + 1)]
        v = wproj[:, 1024 + HD * h : 1024 + HD * (h + 1)]
        q = wproj[:, HD * h : HD * (h + 1)]
        wsend[h] = jnp.concatenate([k, v, q, jnp.zeros_like(q)], axis=1)
        msend[h] = jnp.concatenate(
            [wmem[:, HD * h : HD * (h + 1)], wmem[:, 512 + HD * h : 512 + HD * (h + 1)]], axis=1
        )
    w_all[s] = wsend[j]
    m_all[s] = msend[j]
    w_copies = []
    for d in range(1, S):
        p = (s + d) % S
        c = rcopy(wsend.at[p % 8], w_all.at[s], w_s.at[d], w_r.at[s], {"shard": p})
        c.start()
        w_copies.append(c)
        c = rcopy(msend.at[p % 8], m_all.at[s], mw_s.at[d], mw_r.at[s], {"shard": p})
        c.start()
        w_copies.append(c)
    for d in range(1, S):
        p = (s + d) % S
        rcopy(small, small_all.at[p], sm_s.at[d], sm_r.at[p], {"shard": p}).wait_recv()
    rows = jnp.zeros((16, 512), F32)
    lane = lax.broadcasted_iota(jnp.int32, (256, 512), 0)
    col = lax.broadcasted_iota(jnp.int32, (256, 512), 1)
    for p in range(S):
        pick = ((col - p * R) == lane) & (lane < R)
        rows = rows + mm(small_all[p], jnp.where(pick, 1.0, 0.0).astype(BF))
        upb_row[0:1, p * F : (p + 1) * F] = small_all[p].astype(F32)[8:9, :F]
    vecs[...] = rows

    hat, _ = norm_stats(embed(hid, bound, vecs, s * Z + z))
    x_all[j] = (hat * vecs[2:3, :] + vecs[5:6, :]).astype(BF)
    enc_all[j] = enc[...]
    copies = []

    def send_block(ref, bits_source, bits_target, send, recv):
        source = flip(j, bits_source)
        c = rcopy(ref.at[source], ref.at[source], send, recv.at[source], {"shard": flip(s, bits_target)})
        c.start()
        copies.append(c)

    def wait_block(ref, bits, recv):
        source = flip(j, bits)
        rcopy(ref.at[source], ref.at[source], x_s.at[0], recv.at[source], {"shard": sib}).wait_recv()

    for n, bits in enumerate((1, 2, 4, 6)):
        send_block(x_all, 0, bits, x_s.at[n], x_r)
    for n, bits in enumerate((1, 2, 4, 6)):
        send_block(enc_all, 0, bits, e_s.at[n], e_r)
    whole = Whole(
        ((wout, gout), (wcq, gcq), (wco, gco), (wup, gup), (wdn, gdn)), S, whole_sems
    )
    for d in range(1, S):
        p = (s + d) % S
        rcopy(wsend.at[0], w_all.at[p], w_s.at[d], w_r.at[p], {"shard": p}).wait_recv()
        rcopy(msend.at[0], m_all.at[p], mw_s.at[d], mw_r.at[p], {"shard": p}).wait_recv()
    w_head = w_all[...].reshape(S * R, 256)
    m_head = m_all[...].reshape(S * R, 128)

    def z_copy(ref, block, plane, step, hop, slot):
        view = ref.at[:, block, plane] if block is not None else ref.at[:, :, plane]
        way = (step + 1) // 2
        return rcopy(view, view, z_s.at[way, hop, slot], z_r.at[way, hop, slot], {"seq": z + step})

    def z_passes(step, hop):
        origin = z - step * hop
        return (z + step >= 0) & (z + step < Z) & (origin >= 0) & (origin < Z)

    def z_send(ref, block, hop, slot):
        for step in (-1, 1):

            @pl.when(z_passes(step, hop))
            def _(step=step):
                z_copy(ref, block, z - step * hop, step, hop, slot).start()

    def z_recv(ref, block, hop, slot):
        for step in (-1, 1):
            origin = z - step * hop

            @pl.when((origin >= 0) & (origin < Z))
            def _(step=step, origin=origin):
                z_copy(ref, block, origin, step, hop - 1, slot).wait_recv()

    def z_drain(ref, block, hop, slot):
        for step in (-1, 1):

            @pl.when(z_passes(step, hop))
            def _(step=step):
                z_copy(ref, block, z - step * hop, step, hop, slot).wait_send()

    def member_copy(ref, block, d, slot, mine):
        other = (m + d) % G
        at = m if mine else other
        view = ref.at[at, block, z] if block is not None else ref.at[at, :, z]
        return rcopy(view, view, mb_s.at[d, slot], mb_r.at[at, slot], {"shard": other * 8 + j})

    def spread(ref, block, slot):
        for d in range(1, G):
            member_copy(ref, block, d, slot, True).start()
        for d in range(1, G):
            member_copy(ref, block, d, slot, False).wait_recv()
        z_send(ref, block, 0, slot)

    def block_step(n):
        bits = ORDER[n]
        block = flip(j, bits)
        if bits:
            wait_block(x_all, bits, x_r)
            if bits in (2, 4, 6):
                send_block(x_all, bits, 1, x_s.at[3 + bits // 2], x_r)
        kvq = mm(x_all[block], w_head)
        kv[m, block, z] = kvq[:, :128].astype(BF)
        spread(kv, block, n)
        qt[block] = (SCALE * kvq[:, 128:256].T[:HD]).astype(BF)

    def encoder_step():
        for bits in (2, 4, 6):
            wait_block(enc_all, bits, e_r)
            send_block(enc_all, bits, 1, e_s.at[3 + bits // 2], e_r)
        for bits in (1, 3, 5, 7):
            wait_block(enc_all, bits, e_r)
        for b in range(8):
            mkv[b] = mm(enc_all[b], m_head).astype(BF)

    lag = 2
    last_step = max(8, 7 + lag * (Z - 1))
    for n in range(last_step + 1):
        if n < 8:
            block_step(n)
        if n == 8:
            encoder_step()
        if n == 5:
            for a in range(5):
                whole.start(a)
        for hop in range(1, Z):
            slot = n - lag * hop
            if 0 <= slot < 8:
                z_recv(kv, flip(j, ORDER[slot]), hop, slot)
                z_send(kv, flip(j, ORDER[slot]), hop, slot)
        if n == min(10, last_step):
            for a in range(3):
                whole.relay(a)
        if n == min(12, last_step):
            for a in range(3, 5):
                whole.relay(a)
            for a in range(3):
                whole.finish(a)
    for a in range(3, 5):
        whole.finish(a)
    for a in range(5):
        whole.wait(a)
    whole.drain()
    for c in small_copies + w_copies + copies:
        c.wait_send()
    for n, bits in enumerate(ORDER):
        for d in range(1, G):
            member_copy(kv, flip(j, bits), d, n, True).wait_send()
        for hop in range(Z - 1):
            z_drain(kv, flip(j, bits), hop, n)


def gather_call(S, Z, args):
    G = S // 8
    (timestep, seg, hid, table, gain, shift, upb, dnb, wproj, wmem, enc, *weights) = args
    T, R, E, F = hid.shape[0], wproj.shape[0], enc.shape[0], upb.shape[0]
    vmem = pl.BlockSpec(memory_space=pltpu.VMEM)
    smem = pl.BlockSpec(memory_space=pltpu.SMEM)
    hbm = pl.BlockSpec(memory_space=pl.ANY)
    sds = jax.ShapeDtypeStruct
    outs = [
        sds((4,), jnp.int32),
        sds((8, T, 512), BF),
        sds((G, 8, Z, T, 128), BF),
        sds((8, HD, T), BF),
        sds((8, E, 128), BF),
        sds((8, E, 512), BF),
        sds((16, 512), F32),
        sds((1, S * F), F32),
    ] + [sds((S,) + w.shape, BF) for w in weights]
    return pl.pallas_call(
        functools.partial(gather_kernel, S, Z, G),
        out_shape=outs,
        in_specs=[smem] + [pl.BlockSpec(memory_space=pltpu.HBM)] * (len(args) - 1),
        out_specs=[smem] + [vmem] * 7 + [hbm] * 5,
        scratch_shapes=[pltpu.VMEM(a.shape, a.dtype) for a in args[1:11]]
        + [
            DMA((10,)),
            pltpu.VMEM((16, 256), F32),
            pltpu.VMEM((16, 256), BF),
            pltpu.VMEM((S, 16, 256), BF),
            pltpu.VMEM((8, R, 256), BF),
            pltpu.VMEM((8, R, 128), BF),
            pltpu.VMEM((S, R, 256), BF),
            pltpu.VMEM((S, R, 128), BF),
            DMA((S,)), DMA((S,)), DMA((S,)), DMA((S,)), DMA((S,)), DMA((S,)),
            DMA((8,)), DMA((8,)), DMA((8,)), DMA((8,)),
            DMA((2, Z, 9)), DMA((2, Z, 9)),
            DMA((G, 9)), DMA((G, 9)),
        ] + Whole.scratch(5, S),
        compiler_params=pltpu.CompilerParams(
            collective_id=0, has_side_effects=True, vmem_limit_bytes=room()
        ),
        name="gather_qkv",
    )(args[0], *[pltpu.with_memory_space_constraint(a, pltpu.HBM) for a in args[1:]])


GROUP = 4


class Reach:
    def __init__(self, causal, bound, block, rows):
        self.causal, self.bound, self.rows = causal, bound, rows
        self.query_first = block * rows
        last = self.query_first + rows - 1
        mixed = (self.query_first < bound) & (last >= bound)
        if causal:
            self.least = jnp.where(self.query_first < bound, 0, bound)
            begin, self.end = self.least // rows, block + 1
            self.mixed = mixed | (self.end < GROUP)
        else:
            per = ENC // rows
            self.least = 0
            begin = jnp.where(self.query_first < bound, 0, per)
            self.end = jnp.where(last < bound, per, 2 * per)
            self.mixed = mixed
        self.groups = (self.end - begin + GROUP - 1) // GROUP

    def mask(self, kind, start, limit, n, scores):
        if kind == "plain":
            return scores
        rows = self.rows
        key = (start + n) * rows + lax.broadcasted_iota(jnp.int32, (rows, 1), 0)
        query = self.query_first + lax.broadcasted_iota(jnp.int32, (1, scores.shape[1]), 1)
        if kind == "edge":
            allowed = (key >= self.least) & (key < limit)
            if n == GROUP - 1:
                allowed = allowed & (key <= query)
        elif self.causal:
            least = jnp.where(query < self.bound, 0, self.bound)
            allowed = (key < limit) & (key <= query) & (key >= least)
        else:
            allowed = jnp.where(query < self.bound, 0, 1) == key // ENC
        return jnp.where(allowed, scores, MASKED)

    def walk(self, group, state):
        def turn(kind, g, carry):
            if kind == "edge":
                g = jnp.where(g == 0, 0, self.groups - 1)
            stop = self.end - GROUP * (self.groups - 1 - g)
            return group(kind, jnp.maximum(stop - GROUP, 0), stop * self.rows, carry)

        mixed, groups = self.mixed, self.groups
        state = lax.fori_loop(
            0, jnp.where(mixed, groups, 0), functools.partial(turn, "full"), state
        )
        if not self.causal:
            return lax.fori_loop(
                0, jnp.where(mixed, 0, groups), functools.partial(turn, "plain"), state
            )
        state = lax.fori_loop(
            0,
            jnp.where(mixed, 0, jnp.minimum(groups, 2)),
            functools.partial(turn, "edge"),
            state,
        )
        return lax.fori_loop(
            1, jnp.where(mixed, 1, groups - 1), functools.partial(turn, "plain"), state
        )


def turned_keys(kv, kt, half, begin, end):
    rows = kv.shape[1]

    def turn(kb, carry):
        flat = kv[kb].astype(F32).T[HD * half : HD * (half + 1)].astype(BF)
        kt[:, pl.ds(pl.multiple_of(kb * rows, rows), rows)] = flat
        return carry

    lax.fori_loop(begin, end, turn, 0)


def key_span(causal, bound, low, Z, rows, count):
    if not causal:
        return 0, count
    return jnp.where(low * rows < bound, 0, bound) // rows, low + 7 * Z + 1


def attend_kernel(Z, causal, info, qt, kv, ot, of, lse, vt):
    bound, m, z = info[0], info[1], info[2]
    count, T = kv.shape[0], kv.shape[1]
    low = 8 * m * Z + z

    begin, end = key_span(causal, bound, low, Z, T, count)
    turned_keys(kv, vt, 1, jnp.maximum(begin - GROUP, 0), end)

    def one_block(i, carry):
        reach = Reach(causal, bound, low + i * Z, T)
        queries = jnp.concatenate([qt[i], jnp.zeros((HD, T), BF)], axis=0)

        def group(kind, start, limit, state):
            top, total, acc = state
            keys = kv[pl.ds(start, GROUP)].reshape(GROUP * T, 128)
            raw = mm(keys, queries)
            scores = [
                reach.mask(kind, start, limit, n, raw[n * T : (n + 1) * T]) for n in range(GROUP)
            ]
            new_top = top
            for piece in scores:
                new_top = jnp.maximum(new_top, jnp.max(piece, axis=0, keepdims=True))
            fade = jnp.exp(top - new_top)
            total = total * fade
            parts = []
            for piece in scores:
                powers = jnp.exp(piece - new_top)
                total = total + jnp.sum(powers, axis=0, keepdims=True)
                parts.append(powers.astype(BF))
            values = vt[:, pl.ds(pl.multiple_of(start * T, T), GROUP * T)]
            acc = acc * fade + mm(values, jnp.concatenate(parts, axis=0))
            return new_top, total, acc

        top, total, acc = reach.walk(
            group,
            (jnp.full((1, T), MASKED, F32), jnp.zeros((1, T), F32), jnp.zeros((HD, T), F32)),
        )
        result = acc / total
        ot[i] = result.astype(BF)
        of[i] = result
        lse[i] = top + jnp.log(total)
        return carry

    lax.fori_loop(0, 8, one_block, 0)


def attend(Z, causal, info, qt, kv):
    T = qt.shape[2]
    sds = jax.ShapeDtypeStruct
    vmem = pl.BlockSpec(memory_space=pltpu.VMEM)
    return pl.pallas_call(
        functools.partial(attend_kernel, Z, causal),
        out_shape=[sds((8, HD, T), BF), sds((8, HD, T), F32), sds((8, 1, T), F32)],
        in_specs=[pl.BlockSpec(memory_space=pltpu.SMEM), vmem, vmem],
        out_specs=[vmem] * 3,
        scratch_shapes=[pltpu.VMEM((HD, kv.shape[0] * T), BF)],
        compiler_params=pltpu.CompilerParams(vmem_limit_bytes=room()),
        name="attend_self" if causal else "attend_cross",
    )(info, qt, kv)


def attend_back_kernel(
    Z, causal, info, qt, kv, dt, of, lse, dq, dkv, kt, dkvf, qd, rows, raw, pair, stage, sem
):
    bound, m, z = info[0], info[1], info[2]
    count, T = kv.shape[0], kv.shape[1]
    low = 8 * m * Z + z
    zero = jnp.zeros((HD, T), BF)

    def clear(kb, carry):
        dkvf[kb] = jnp.zeros((T, 128), F32)
        return carry

    lax.fori_loop(0, count, clear, 0)

    begin, end = key_span(causal, bound, low, Z, T, count)
    turned_keys(kv, kt, 0, jnp.maximum(begin - GROUP, 0), end)

    def one_block(i, carry):
        reach = Reach(causal, bound, low + i * Z, T)
        qd[:HD, :T] = qt[i]
        qd[HD:, :T] = zero
        qd[:HD, T:] = zero
        qd[HD:, T:] = dt[i]
        both = jnp.concatenate([qt[i].astype(F32), dt[i].astype(F32)], axis=0).T
        lane = lax.broadcasted_iota(jnp.int32, both.shape, 1)
        rows[:T] = jnp.where(lane < HD, 0.0, both).astype(BF)
        rows[T:] = jnp.where(lane < HD, both, 0.0).astype(BF)
        delta = jnp.sum(dt[i].astype(F32) * of[i], axis=0, keepdims=True)
        level = lse[i]

        def group(kind, start, limit, acc):
            keys = kv[pl.ds(start, GROUP)].reshape(GROUP * T, 128)
            raw[...] = mm(keys, qd[...])
            for n in range(GROUP):
                at = slice(n * T, (n + 1) * T)
                probs = jnp.exp(reach.mask(kind, start, limit, n, raw[at, :T]) - level)
                pair[at, :T] = probs.astype(BF)
                pair[at, T:] = (probs * (raw[at, T:] - delta)).astype(BF)
            grads = mm(pair[...], rows[...])
            dkvf[pl.ds(start, GROUP)] += grads.reshape(GROUP, T, 128)
            flat = kt[:, pl.ds(pl.multiple_of(start * T, T), GROUP * T)]
            return acc + mm(flat, pair[:, T:])

        acc = reach.walk(group, jnp.zeros((HD, T), F32))
        dq[i] = (SCALE * acc).astype(BF)
        return carry

    lax.fori_loop(0, 8, one_block, 0)

    slots = stage.shape[0]

    def put(kb):
        return pltpu.make_async_copy(stage.at[kb % slots], dkv.at[kb], sem.at[kb % slots])

    def flush(kb, carry):
        @pl.when(kb >= slots)
        def _():
            put(kb).wait()

        stage[kb % slots] = dkvf[kb].astype(BF)
        put(kb).start()
        return carry

    def settle(kb, carry):
        put(kb).wait()
        return carry

    lax.fori_loop(0, count, flush, 0)
    lax.fori_loop(0, slots, settle, 0)


def attend_back(Z, causal, info, qt, kv, dt, of, lse):
    T = qt.shape[2]
    count = kv.shape[0]
    slots = count if count <= 32 else 2
    sds = jax.ShapeDtypeStruct
    vmem = pl.BlockSpec(memory_space=pltpu.VMEM)
    return pl.pallas_call(
        functools.partial(attend_back_kernel, Z, causal),
        out_shape=[sds((8, HD, T), BF), sds(kv.shape, BF)],
        in_specs=[pl.BlockSpec(memory_space=pltpu.SMEM)] + [vmem] * 5,
        out_specs=[vmem, pl.BlockSpec(memory_space=pl.ANY)],
        scratch_shapes=[
            pltpu.VMEM((HD, count * T), BF),
            pltpu.VMEM((count, T, 128), F32),
            pltpu.VMEM((128, 2 * T), BF),
            pltpu.VMEM((2 * T, 128), BF),
            pltpu.VMEM((GROUP * T, 2 * T), F32),
            pltpu.VMEM((GROUP * T, 2 * T), BF),
            pltpu.VMEM((slots, T, 128), BF),
            DMA((slots,)),
        ],
        compiler_params=pltpu.CompilerParams(vmem_limit_bytes=room()),
        name="attend_self_back" if causal else "attend_cross_back",
    )(info, qt, kv, dt, of, lse)


def greet_group(heads=False):
    s, z, j, m = place()
    peers = [(None, {"shard": m * 8 + (j + d) % 8}) for d in range(1, 8)]
    if heads:
        peers = peers + [(None, device) for _, _, _, device in kin()]
    greet(peers)


def kin():
    s, z, j, m = place()
    G, Z = lax.axis_size("shard") // 8, lax.axis_size("seq")
    out = []
    for dm in range(G):
        for dz in range(Z):
            if dm or dz:
                om, oz = (m + dm) % G, (z + dz) % Z
                out.append((dm * Z + dz, om, oz, {"shard": om * 8 + j, "seq": oz}))
    return out


def exchange_copies(src, dst, send, recv):
    s, z, j, m = place()
    out = []
    for d in (1, 2, 3, 4, 5, 6, 7):
        p = flip(j, d)
        out.append(rcopy(src.at[p], dst.at[j], send.at[d], recv.at[j], {"shard": m * 8 + p}))
    return out


def exchange_start(src, dst, send, recv):
    s, z, j, m = place()
    for c in exchange_copies(src, dst, send, recv):
        c.start()
    dst[j] = src[j]


def exchange_recv(src, dst, send, recv):
    s, z, j, m = place()
    for d in (1, 2, 3, 4, 5, 6, 7):
        p = flip(j, d)
        rcopy(src.at[p], dst.at[p], send.at[d], recv.at[p], {"shard": m * 8 + p}).wait_recv()


def exchange_sent(src, dst, send, recv):
    for c in exchange_copies(src, dst, send, recv):
        c.wait_send()


class ChipSums:
    def __init__(self, pairs, send, recv):
        self.pairs, self.send, self.recv = pairs, send, recv
        self.s = lax.axis_index("shard")
        self.core = self.s % 2
        self.chips = lax.axis_size("shard") // 2

    def piece(self, a, p):
        full, kept, _ = self.pairs[a]
        rows = kept.shape[1]
        return full.at[pl.ds(pl.multiple_of(p * rows, rows), rows), :]

    def copies(self):
        for a, (_, kept, buf) in enumerate(self.pairs):
            for q in range(self.chips):
                yield rcopy(
                    self.piece(a, 2 * q + 1 - self.core), buf.at[q], self.send.at[a, q], self.recv.at[a, q],
                    {"shard": flip(self.s, 1)},
                )

    def start(self):
        for c in self.copies():
            c.start()

    def finish(self):
        for c in self.copies():
            c.wait_recv()
        for a, (_, kept, buf) in enumerate(self.pairs):
            for q in range(self.chips):
                mine = self.piece(a, 2 * q + self.core)[...]
                kept[q] = (buf[q].astype(F32) + mine.astype(F32)).astype(BF)
        for c in self.copies():
            c.wait_send()


def remote_call(kernel, name, ident, ins, outs, scratch, smem=1, far=(), far_outs=()):
    vmem = pl.BlockSpec(memory_space=pltpu.VMEM)
    in_specs = [pl.BlockSpec(memory_space=pltpu.SMEM)] * smem + [vmem] * (len(ins) - smem)
    out_specs = [vmem] * len(outs)
    for n in far_outs:
        out_specs[n] = pl.BlockSpec(memory_space=pl.ANY)
    for n in far:
        in_specs[n] = pl.BlockSpec(memory_space=pl.ANY)
    return pl.pallas_call(
        kernel,
        out_shape=outs,
        in_specs=in_specs,
        out_specs=out_specs,
        scratch_shapes=scratch,
        compiler_params=pltpu.CompilerParams(
            collective_id=ident, has_side_effects=True, vmem_limit_bytes=room()
        ),
        name=name,
    )(*ins)


def middle_kernel(
    Z, bnd, ot, hid, vecs, wout, wcq, mem, at, after, n2, cqt, mkv, cq_send, s1, r1, s2, r2, s3, r3
):
    s, z, j, m = place()
    T = hid.shape[0]
    greet_group(True)
    exchange_start(ot, at, s1, r1)

    def memory_copies(mine):
        for n, om, oz, device in kin():
            c = m * Z + z if mine else om * Z + oz
            target = mkv.at[m, :, z] if mine else mkv.at[om, :, oz]
            yield rcopy(mem, target, s3.at[n], r3.at[c], device)

    for c in memory_copies(True):
        c.start()
    mkv[m, :, z] = mem[...]
    base = embed(hid, bnd[0], vecs, s * Z + z)
    exchange_recv(ot, at, s1, r1)
    attn = at[...].reshape(512, T).astype(F32).T.astype(BF)
    value = base + mm(attn, wout[...])
    after[...] = value
    hat, _ = norm_stats(value)
    normed = (hat * vecs[3:4, :] + vecs[6:7, :]).astype(BF)
    n2[...] = normed
    cq = mm(normed, wcq[...])
    cq_send[...] = (SCALE * cq.T).astype(BF).reshape(8, HD, T)
    exchange_start(cq_send, cqt, s2, r2)
    exchange_recv(cq_send, cqt, s2, r2)
    for c in memory_copies(False):
        c.wait_recv()
    exchange_sent(ot, at, s1, r1)
    exchange_sent(cq_send, cqt, s2, r2)
    for c in memory_copies(True):
        c.wait_send()


def middle(G, Z, bnd, ot, hid, vecs, wout, wcq, mem):
    T, E = hid.shape[0], mem.shape[1]
    sds = jax.ShapeDtypeStruct
    return remote_call(
        functools.partial(middle_kernel, Z),
        "middle",
        1,
        (bnd, ot, hid, vecs, wout, wcq, mem),
        [
            sds((8, HD, T), BF), sds((T, 512), F32), sds((T, 512), BF), sds((8, HD, T), BF),
            sds((G, 8, Z, E, 128), BF),
        ],
        [
            pltpu.VMEM((8, HD, T), BF), DMA((8,)), DMA((8,)), DMA((8,)), DMA((8,)),
            DMA((G * Z,)), DMA((G * Z,)),
        ],
    )


def erf(x):
    return lax.erf(x)


def feed_kernel(
    crt, after, vecs, upb, wco, wup, wdn, grad, wproj, wmem,
    layer_out, d_after, co_sum, up_sum, dn_sum, smalls, upb_grad, dct, gproj, gmem,
    ct, send, n3t, out_acc, dn_acc, co_grad, up_grad, dn_grad, co_buf, up_buf, dn_buf,
    s1, r1, s2, r2, s3, r3, *whole_sems
):
    T = after.shape[0]
    FF = wup.shape[1]
    S = lax.axis_size("shard")
    s = lax.axis_index("shard")
    greet([(None, {"shard": (s + d) % S}) for d in range(1, S)])
    exchange_start(crt, ct, s1, r1)
    whole = Whole(((wproj, gproj), (wmem, gmem)), S, whole_sems)
    for a in range(2):
        whole.start(a)
    g = grad[...]
    gf = g.astype(F32)
    gt = gf.T.astype(BF)
    exchange_recv(crt, ct, s1, r1)
    cross_t = ct[...].reshape(512, T)
    value = after[...] + mm(cross_t.astype(F32).T.astype(BF), wco[...])
    hat, scale = norm_stats(value)
    normed = hat * vecs[4:5, :] + vecs[7:8, :]
    n3 = normed.astype(BF)
    n3t[...] = n3.astype(F32).T.astype(BF)
    out_acc[...] = value + vecs[9:10, :]
    dn_acc[...] = jnp.zeros_like(dn_acc)
    width = 512
    for c in range(FF // width):
        lo, hi = c * width, (c + 1) * width
        pre = mm(n3, wup[:, lo:hi]) + upb[0:1, lo:hi]
        half = 0.5 * (1.0 + erf(pre * (0.5**0.5)))
        middle_c = (pre * half).astype(BF)
        out_acc[...] += mm(middle_c, wdn[lo:hi, :])
        slope = half + pre * (jnp.exp(-0.5 * pre * pre) * ((0.5 / jnp.pi) ** 0.5))
        d_pre = mm(g, wdn[lo:hi, :], 1, 1) * slope
        d_pre_b = d_pre.astype(BF)
        upb_grad[0:1, lo:hi] = jnp.sum(d_pre_b.astype(F32), axis=0, keepdims=True)
        dn_grad[lo:hi, :] = mm(middle_c.astype(F32).T.astype(BF), g).astype(BF)
        up_grad[:, lo:hi] = mm(n3t[...], d_pre_b).astype(BF)
        dn_acc[...] += mm(d_pre_b, wup[:, lo:hi], 1, 1)
    for a in range(2):
        whole.relay(a)
    layer_out[...] = out_acc[...].astype(BF)
    d_value, d_gain, d_shift = norm_back(dn_acc[...], hat, scale, vecs[4:5, :])
    total = gf + d_value
    d_after[...] = total
    smalls[0:1, :] = d_gain
    smalls[1:2, :] = d_shift
    smalls[2:3, :] = jnp.sum(gf, axis=0, keepdims=True)
    dc = total.astype(BF)
    d_cross = mm(wco[...], dc, 1, 1)
    send[...] = d_cross.astype(BF).reshape(8, HD, T)
    exchange_start(send, dct, s2, r2)
    co_grad[...] = mm(cross_t, dc).astype(BF)
    sums = ChipSums(
        ((co_grad, co_sum, co_buf), (up_grad, up_sum, up_buf), (dn_grad, dn_sum, dn_buf)), s3, r3
    )
    sums.start()
    for a in range(2):
        whole.finish(a)
    exchange_recv(send, dct, s2, r2)
    sums.finish()
    for a in range(2):
        whole.wait(a)
    whole.drain()
    exchange_sent(crt, ct, s1, r1)
    exchange_sent(send, dct, s2, r2)


def feed(crt, after, vecs, upb, wco, wup, wdn, grad, wproj, wmem):
    T, FF = after.shape[0], wup.shape[1]
    S = lax.axis_size("shard")
    chips, R, F = S // 2, 512 // S, FF // S
    sds = jax.ShapeDtypeStruct
    return remote_call(
        feed_kernel,
        "feed_forward",
        2,
        (crt, after, vecs, upb, wco, wup, wdn, grad, wproj, wmem),
        [
            sds((T, 512), BF),
            sds((T, 512), F32),
            sds((chips, R, 512), BF),
            sds((chips, R, FF), BF),
            sds((chips, F, 512), BF),
            sds((8, 512), F32),
            sds((1, FF), F32),
            sds((8, HD, T), BF),
            sds((S,) + wproj.shape, BF),
            sds((S,) + wmem.shape, BF),
        ],
        [
            pltpu.VMEM((8, HD, T), BF),
            pltpu.VMEM((8, HD, T), BF),
            pltpu.VMEM((512, T), BF),
            pltpu.VMEM((T, 512), F32),
            pltpu.VMEM((T, 512), F32),
            pltpu.VMEM((512, 512), BF),
            pltpu.VMEM((512, FF), BF),
            pltpu.VMEM((FF, 512), BF),
            pltpu.VMEM((chips, R, 512), BF),
            pltpu.VMEM((chips, R, FF), BF),
            pltpu.VMEM((chips, F, 512), BF),
            DMA((8,)), DMA((8,)), DMA((8,)), DMA((8,)), DMA((3, chips)), DMA((3, chips)),
        ] + Whole.scratch(2, S),
        smem=0,
        far_outs=(8, 9),
    )


def middle_back_kernel(
    dcqt, after, d_after2, n2, at, vecs, wcq, wout, dmkv,
    d_after, cq_sum, out_sum, smalls, dat, dmem,
    home, send, parts, cq_grad, out_grad, cq_buf, out_buf, s1, r1, s2, r2, s3, r3, s4, r4
):
    s, z, j, m = place()
    G, Z = dmkv.shape[0], dmkv.shape[2]
    T = after.shape[0]
    greet_group(True)
    exchange_start(dcqt, home, s1, r1)

    def memory_copies(mine):
        for n, om, oz, device in kin():
            c = m * Z + z if mine else om * Z + oz
            yield rcopy(dmkv.at[om, :, oz], parts.at[c], s3.at[n], r3.at[c], device)

    for c in memory_copies(True):
        c.start()
    parts[m * Z + z] = dmkv[m, :, z]
    hat, scale = norm_stats(after[...])
    n2t = n2[...].astype(F32).T.astype(BF)
    exchange_recv(dcqt, home, s1, r1)
    dcq = home[...].reshape(512, T).astype(F32).T.astype(BF)
    d_value, d_gain, d_shift = norm_back(mm(dcq, wcq[...], 1, 1), hat, scale, vecs[3:4, :])
    total = d_after2[...] + d_value
    d_after[...] = total
    smalls[0:1, :] = d_gain
    smalls[1:2, :] = d_shift
    da = total.astype(BF)
    send[...] = mm(wout[...], da, 1, 1).astype(BF).reshape(8, HD, T)
    exchange_start(send, dat, s2, r2)
    cq_grad[...] = mm(n2t, dcq).astype(BF)
    out_grad[...] = mm(at[...].reshape(512, T), da).astype(BF)
    sums = ChipSums(((cq_grad, cq_sum, cq_buf), (out_grad, out_sum, out_buf)), s4, r4)
    sums.start()
    for c in memory_copies(False):
        c.wait_recv()
    total_mem = parts[0].astype(F32)
    for n in range(1, G * Z):
        total_mem = total_mem + parts[n].astype(F32)
    dmem[...] = total_mem.astype(BF)
    sums.finish()
    exchange_recv(send, dat, s2, r2)
    exchange_sent(dcqt, home, s1, r1)
    exchange_sent(send, dat, s2, r2)
    for c in memory_copies(True):
        c.wait_send()


def middle_back(dcqt, after, d_after2, n2, at, vecs, wcq, wout, dmkv):
    T = after.shape[0]
    G, _, Z, E, _ = dmkv.shape
    chips, R = 4 * G, 512 // (8 * G)
    sds = jax.ShapeDtypeStruct
    return remote_call(
        middle_back_kernel,
        "middle_back",
        3,
        (dcqt, after, d_after2, n2, at, vecs, wcq, wout, dmkv),
        [
            sds((T, 512), F32),
            sds((chips, R, 512), BF),
            sds((chips, R, 512), BF),
            sds((8, 512), F32),
            sds((8, HD, T), BF),
            sds((8, E, 128), BF),
        ],
        [
            pltpu.VMEM((8, HD, T), BF),
            pltpu.VMEM((8, HD, T), BF),
            pltpu.VMEM((G * Z, 8, E, 128), BF),
            pltpu.VMEM((512, 512), BF),
            pltpu.VMEM((512, 512), BF),
            pltpu.VMEM((chips, R, 512), BF),
            pltpu.VMEM((chips, R, 512), BF),
            DMA((8,)), DMA((8,)), DMA((8,)), DMA((8,)), DMA((G * Z,)), DMA((G * Z,)),
            DMA((2, chips)), DMA((2, chips)),
        ],
        smem=0,
    )


NC = 16


def last_kernel(
    S, Z, G,
    info, hid, vecs, d_after, x_all, enc_all, dqt, dkv, finm, wproj, wmem,
    out_g, cq_g, co_g, up_g, dn_g, small2, small3, upb_g,
    hidden_grad, encoder_grad, zfin, smalls_o,
    got_out, got_cq, got_co, got_up, got_dn,
    rk, fin, mbuf, hkv, hq, hm, turned, enc_turned, dall, psend, pgot, msend, mgot,
    wz, zin, sm_all, sm_z, sm_plane, sm_mine,
    b_s, b_r, k_s, k_r, mb_s, mb_r, hq_s, hq_r, hk_s, hk_r, hm_s, hm_r,
    p_s, p_r, pm_s, pm_r, c_s, c_r, f_s, f_r, sm_s, sm_r, sz_s, sz_r,
):
    s, z, j, m = place()
    T, E = hid.shape[0], enc_all.shape[1]
    R = 512 // S
    F = dn_g.shape[1]
    bound = info[0]
    chips = S // 2
    core, chip = s % 2, s // 2
    sib = flip(s, 1)
    ends = (Z - 1, 0)
    greet(
        [(None, {"shard": (s + d) % S}) for d in range(1, S)]
        + [(None, {"seq": (z + d) % Z}) for d in range(1, Z)]
    )
    sums = (out_g, cq_g, co_g, up_g, dn_g)
    gots = (got_out, got_cq, got_co, got_up, got_dn)

    if G > 1:
        for d in range(1, G):
            o = (m + d) % G
            rcopy(dkv.at[o], mbuf.at[m], mb_s.at[d, 0], mb_r.at[m, 0], {"shard": o * 8 + j}).start()
        own_part = pltpu.make_async_copy(dkv.at[m], mbuf.at[m], mb_s.at[0, 0])
        own_part.start()
        own_part.wait()
        for d in range(1, G):
            o = (m + d) % G
            rcopy(dkv.at[o], mbuf.at[o], mb_s.at[d, 0], mb_r.at[o, 0], {"shard": o * 8 + j}).wait_recv()
        for b in range(8):
            acc = mbuf[m, b].astype(F32)
            for d in range(1, G):
                acc = acc + mbuf[(m + d) % G, b].astype(F32)
            mbuf[m, b] = acc.astype(BF)
        part = mbuf.at[m]
    else:
        part = dkv.at[0]

    def z_view(slot, t):
        return part.at[slot, t]

    def z_buffer(way, t, slot):
        return rk.at[way, t, slot]

    def z_copy(way, t, slot, source):
        step = 2 * way - 1
        return rcopy(
            source, z_buffer(way, t, slot), k_s.at[way, t, slot], k_r.at[way, t, slot], {"seq": z + step}
        )

    for far in range(Z - 1, 0, -1):
        for slot in range(8):
            for way in (0, 1):
                t = z + (2 * way - 1) * far

                @pl.when((z == ends[way]) & (t >= 0) & (t < Z))
                def _(way=way, t=t, slot=slot):
                    z_copy(way, t, slot, z_view(slot, t)).start()

    def own_copy(a, q):
        return rcopy(
            sums[a].at[q], gots[a].at[chip], b_s.at[a, q], b_r.at[a, chip], {"shard": 2 * q + core}
        )

    for a in range(5):
        for d in range(1, chips):
            own_copy(a, (chip + d) % chips).start()
    exchange_start(dqt, hq, hq_s, hq_r)
    exchange_start(finm, hm, hm_s, hm_r)

    def turn_block(b):
        turned[:, b * T : (b + 1) * T] = x_all[b].astype(F32).T.astype(BF)

    def turn_query(b):
        dq_b = dqt[b].astype(F32)
        dall[b * T : (b + 1) * T, 128:] = (
            jnp.concatenate([dq_b, jnp.zeros_like(dq_b)], axis=0).T.astype(BF)
        )

    def turn_encoder():
        enc_turned[...] = enc_all[...].reshape(8 * E, 512).astype(F32).T.astype(BF)

    def own_sum(a):
        for d in range(1, chips):
            q = (chip + d) % chips
            rcopy(sums[a].at[q], gots[a].at[q], b_s.at[a, q], b_r.at[a, q], {"shard": 2 * q + core}).wait_recv()
        total = sums[a][chip].astype(F32)
        for d in range(1, chips):
            total = total + gots[a][(chip + d) % chips].astype(F32)
        total = total.astype(BF)
        if a < 3:
            wz[a] = total
        elif a == 3:
            for c in range(4):
                wz[3 + c] = total[:, 512 * c : 512 * (c + 1)]
        else:
            for c in range(4):
                wz[7 + c] = total[c * R : (c + 1) * R]

    block = s * Z + z
    work = [functools.partial(turn_block, b) for b in range(8)]
    work += [functools.partial(turn_query, b) for b in range(8)] + [turn_encoder]

    for far in range(Z - 1, 0, -1):
        for slot in range(8):
            if work:
                work.pop(0)()
            for way in (0, 1):
                t = z + (2 * way - 1) * far

                @pl.when((z != ends[way]) & (t >= 0) & (t < Z))
                def _(way=way, t=t, slot=slot):
                    z_copy(way, t, slot, z_view(slot, t)).wait_recv()
                    buf = z_buffer(way, t, slot)
                    buf[...] = (
                        buf[...].astype(F32) + z_view(slot, t)[...].astype(F32)
                    ).astype(BF)
                    z_copy(way, t, slot, buf).start()

    def inward(k, step):
        way = (step + 1) // 2
        return rcopy(wz.at[k], zin.at[way, k], c_s.at[way, k], c_r.at[way, k], {"seq": z + step})

    def outward(k, step):
        return rcopy(zfin.at[k], zfin.at[k], f_s.at[(step + 1) // 2, k], f_r.at[k], {"seq": z + step})

    def root(k):
        return max(Z // 2 - 1 + k % 2, 0) if Z > 1 else 0

    def tips(k):
        r = root(k)
        for step in (-1, 1):
            tip = ends[(step + 1) // 2]
            if tip != r:

                @pl.when(z == tip)
                def _(step=step):
                    inward(k, step).start()

    def partial(k):
        r = root(k)
        for step, beyond in ((-1, z > r), (1, z < r)):
            tip = ends[(step + 1) // 2]
            way = (step + 1) // 2

            @pl.when(beyond & (z != tip))
            def _(step=step, way=way):
                inward(k, step).wait_recv()
                wz[k] = (wz[k].astype(F32) + zin[way, k].astype(F32)).astype(BF)
                inward(k, step).start()

    def total_of(k):
        r = root(k)

        @pl.when(z == r)
        def _():
            total = wz[k].astype(F32)
            if r < Z - 1:
                inward(k, -1).wait_recv()
                total = total + zin[0, k].astype(F32)
            if r > 0:
                inward(k, 1).wait_recv()
                total = total + zin[1, k].astype(F32)
            zfin[k] = total.astype(BF)
            if r < Z - 1:
                outward(k, 1).start()
            if r > 0:
                outward(k, -1).start()

    def send_out(k):
        r = root(k)
        for step, beyond in ((1, z > r), (-1, z < r)):
            tip = Z - 1 if step > 0 else 0

            @pl.when(beyond)
            def _(step=step, tip=tip):
                outward(k, step).wait_recv()

                @pl.when(z != tip)
                def _():
                    outward(k, step).start()

    for task in work:
        task()
    psend_q = mm(turned[...], dall[:, 128:])
    for a in range(5):
        own_sum(a)
        for k in ((0,), (1,), (2,), (3, 4, 5, 6), (7, 8, 9, 10))[a]:
            tips(k)
    hat, scale = norm_stats(embed(hid, bound, vecs, block))

    for slot in range(8):
        for way in (0, 1):

            @pl.when(z != ends[way])
            def _(way=way, slot=slot):
                z_copy(way, z, slot, z_view(slot, z)).wait_recv()

        low = jnp.where(z == ends[0], 0.0, z_buffer(0, z, slot)[...].astype(F32))
        high = jnp.where(z == ends[1], 0.0, z_buffer(1, z, slot)[...].astype(F32))
        total = (low + high + z_view(slot, z)[...].astype(F32)).astype(BF)
        fin[slot] = total
        dall[slot * T : (slot + 1) * T, :128] = total
    exchange_start(fin, hkv, hk_s, hk_r)
    for k in range(7):
        partial(k)

    psend_kv = mm(turned[...], dall[:, :128])
    psend[...] = jnp.concatenate([psend_kv, psend_q], axis=1).astype(BF).reshape(S, R, 256)
    msend[...] = mm(enc_turned[...], finm[...].reshape(8 * E, 128)).astype(BF).reshape(S, R, 128)
    pgot[s] = psend[s]
    mgot[s] = msend[s]
    for d in range(1, S):
        p = (s + d) % S
        rcopy(psend.at[p], pgot.at[s], p_s.at[d], p_r.at[s], {"shard": p}).start()
        rcopy(msend.at[p], mgot.at[s], pm_s.at[d], pm_r.at[s], {"shard": p}).start()

    for k in range(7, 11):
        partial(k)
        total_of(k - 7)

    exchange_recv(dqt, hq, hq_s, hq_r)
    exchange_recv(fin, hkv, hk_s, hk_r)
    exchange_recv(finm, hm, hm_s, hm_r)
    d_query = hq[...].reshape(512, T).astype(F32).T.astype(BF)
    d_keys = jnp.concatenate([hkv[h][:, :HD] for h in range(H)], axis=1)
    d_values = jnp.concatenate([hkv[h][:, HD:] for h in range(H)], axis=1)
    d_norm = (
        mm(d_query, wproj[:, :512], 1, 1)
        + mm(d_keys, wproj[:, 512:1024], 1, 1)
        + mm(d_values, wproj[:, 1024:], 1, 1)
    )
    d_value, d_gain, d_shift = norm_back(d_norm, hat, scale, vecs[2:3, :])
    total = d_after[...] + d_value
    hidden_grad[...] = total
    pos = block * T + lax.broadcasted_iota(jnp.int32, (T, 1), 0)
    sm_mine[...] = jnp.zeros((16, 512), F32)
    sm_mine[0:1, :] = d_gain
    sm_mine[1:2, :] = small2[0:1, :]
    sm_mine[2:3, :] = small3[0:1, :]
    sm_mine[3:4, :] = d_shift
    sm_mine[4:5, :] = small2[1:2, :]
    sm_mine[5:6, :] = small3[1:2, :]
    sm_mine[6:7, :] = jnp.sum(jnp.where(pos < bound, total, 0.0), axis=0, keepdims=True)
    sm_mine[7:8, :] = jnp.sum(jnp.where(pos < bound, 0.0, total), axis=0, keepdims=True)
    sm_mine[8:9, :] = small3[2:3, :]
    for c in range(upb_g.shape[1] // 512):
        sm_mine[9 + c : 10 + c, :] = upb_g[0:1, 512 * c : 512 * (c + 1)]
    for d in range(1, S):
        rcopy(sm_mine, sm_all.at[s], sm_s.at[d], sm_r.at[s], {"shard": (s + d) % S}).start()
    sm_all[s] = sm_mine[...]

    for k in range(4, 8):
        total_of(k)

    for d in range(1, S):
        p = (s + d) % S
        rcopy(psend.at[p], pgot.at[p], p_s.at[d], p_r.at[p], {"shard": p}).wait_recv()
        rcopy(msend.at[p], mgot.at[p], pm_s.at[d], pm_r.at[p], {"shard": p}).wait_recv()
    heads, mheads = [], []
    for h in range(H):
        acc, accm = pgot[h].astype(F32), mgot[h].astype(F32)
        for g in range(1, G):
            acc = acc + pgot[8 * g + h].astype(F32)
            accm = accm + mgot[8 * g + h].astype(F32)
        heads.append(acc)
        mheads.append(accm)
    wz[11] = jnp.concatenate([v[:, 128 : 128 + HD] for v in heads], axis=1).astype(BF)
    wz[12] = jnp.concatenate([v[:, :HD] for v in heads], axis=1).astype(BF)
    wz[13] = jnp.concatenate([v[:, HD:128] for v in heads], axis=1).astype(BF)
    wz[14] = jnp.concatenate([v[:, :HD] for v in mheads], axis=1).astype(BF)
    wz[15] = jnp.concatenate([v[:, HD:] for v in mheads], axis=1).astype(BF)
    for k in range(11, NC):
        tips(k)
    e_keys = jnp.concatenate([hm[h][:, :HD] for h in range(H)], axis=1)
    e_values = jnp.concatenate([hm[h][:, HD:] for h in range(H)], axis=1)
    encoder_grad[...] = mm(e_keys, wmem[:, :512], 1, 1) + mm(e_values, wmem[:, 512:], 1, 1)

    for d in range(1, S):
        p = (s + d) % S
        rcopy(sm_mine, sm_all.at[p], sm_s.at[d], sm_r.at[p], {"shard": p}).wait_recv()
    acc = sm_all[0]
    for p in range(1, S):
        acc = acc + sm_all[p]
    sm_plane[...] = acc
    for d in range(1, Z):
        rcopy(sm_plane, sm_z.at[z], sz_s.at[d], sz_r.at[z], {"seq": (z + d) % Z}).start()
    sm_z[z] = acc
    for k in range(NC):
        if k + 11 < NC:
            partial(k + 11)
        if k + 8 < NC:
            total_of(k + 8)
        send_out(k)
    for d in range(1, Z):
        o = (z + d) % Z
        rcopy(sm_plane, sm_z.at[o], sz_s.at[d], sz_r.at[o], {"seq": o}).wait_recv()
    acc = sm_z[0]
    for o in range(1, Z):
        acc = acc + sm_z[o]
    smalls_o[...] = acc

    for a in range(5):
        for d in range(1, chips):
            own_copy(a, (chip + d) % chips).wait_send()
    for d in range(1, G):
        o = (m + d) % G
        rcopy(dkv.at[o], mbuf.at[m], mb_s.at[d, 0], mb_r.at[m, 0], {"shard": o * 8 + j}).wait_send()
    exchange_sent(dqt, hq, hq_s, hq_r)
    exchange_sent(fin, hkv, hk_s, hk_r)
    exchange_sent(finm, hm, hm_s, hm_r)
    for far in range(Z - 1, 0, -1):
        for slot in range(8):
            for way in (0, 1):
                t = z + (2 * way - 1) * far

                @pl.when((t >= 0) & (t < Z))
                def _(way=way, t=t, slot=slot):
                    z_copy(way, t, slot, z_view(slot, t)).wait_send()

    for d in range(1, S):
        p = (s + d) % S
        rcopy(psend.at[p], pgot.at[s], p_s.at[d], p_r.at[s], {"shard": p}).wait_send()
        rcopy(msend.at[p], mgot.at[s], pm_s.at[d], pm_r.at[s], {"shard": p}).wait_send()
        rcopy(sm_mine, sm_all.at[s], sm_s.at[d], sm_r.at[s], {"shard": p}).wait_send()
    for d in range(1, Z):
        rcopy(sm_plane, sm_z.at[z], sz_s.at[d], sz_r.at[z], {"seq": (z + d) % Z}).wait_send()
    for k in range(NC):
        r = root(k)
        for step, beyond in ((-1, z > r), (1, z < r)):

            @pl.when(beyond)
            def _(step=step):
                inward(k, step).wait_send()

        for step in (-1, 1):
            sends = (z >= r) & (z < Z - 1) if step > 0 else (z <= r) & (z > 0)

            @pl.when(sends)
            def _(step=step):
                outward(k, step).wait_send()


def finish_kernel(
    info, timestep, zfin, sums, hid_g, enc_g, lay,
    lay_o, hid_o, enc_o, time_o, gain_o, shift_o, proj_o, out_o, cq_o, mem_o, co_o, up_o, upb_o, dn_o, dnb_o,
):
    s = info[3]
    R, F = out_o.shape[0], upb_o.shape[1]
    lay_o[...] = lay[...]
    hid_o[...] = hid_g[...]
    enc_o[...] = enc_g[...]
    out_o[...] = zfin[0].astype(F32)
    cq_o[...] = zfin[1].astype(F32)
    co_o[...] = zfin[2].astype(F32)
    for c in range(4):
        up_o[:, 512 * c : 512 * (c + 1)] = zfin[3 + c].astype(F32)
        dn_o[c * R : (c + 1) * R, :] = zfin[7 + c].astype(F32)
    for c in range(3):
        proj_o[:, 512 * c : 512 * (c + 1)] = zfin[11 + c].astype(F32)
    for c in range(2):
        mem_o[:, 512 * c : 512 * (c + 1)] = zfin[14 + c].astype(F32)

    def own(width, first):
        row = lax.broadcasted_iota(jnp.int32, (512, width), 0)
        col = lax.broadcasted_iota(jnp.int32, (512, width), 1)
        pick = jnp.where(row == col + first, 1.0, 0.0)
        return lax.dot_general(
            sums[...], pick, (((1,), (0,)), ((), ())),
            preferred_element_type=F32, precision=lax.Precision.HIGHEST,
        )

    mine = own(R, s * R)
    gain_o[...] = mine[0:3]
    shift_o[...] = mine[3:6]
    dnb_o[...] = mine[8:9]
    step = lax.broadcasted_iota(jnp.int32, time_o.shape, 0)
    grad = jnp.zeros(time_o.shape, F32)
    for d in range(DOCS):
        grad = grad + jnp.where(step == timestep[d], mine[6 + d : 7 + d], 0.0)
    time_o[...] = grad
    wide = own(F, (s * F) % 512)
    row = lax.broadcasted_iota(jnp.int32, wide.shape, 0)
    upb_o[...] = jnp.sum(jnp.where(row == 9 + s * F // 512, wide, 0.0), axis=0, keepdims=True)


def last(v):
    S, Z, G = v["S"], v["Z"], v["G"]
    T, R, F, E = v["T"], v["R"], v["F"], v["encoder"].shape[0]
    FF = v["wup"].shape[1]
    chips = S // 2
    sds = jax.ShapeDtypeStruct
    V = pltpu.VMEM
    GM, ZM = (G, Z) if G > 1 else (1, 1)
    hidden_grad, encoder_grad, zfin, sums = remote_call(
        functools.partial(last_kernel, S, Z, G),
        "gradients_home",
        4,
        (
            v["info"], v["hidden_in"], v["vecs"], v["d_after"], v["x_all"], v["enc_all"], v["dqt"],
            v["dkv"].reshape(G, 8, Z, T, 128), v["dmem"],
            v["gproj"].reshape(512, 1536), v["gmem"].reshape(512, 1024),
            v["wout_grad"], v["cq_grad"], v["co_grad"], v["up_grad"], v["dn_grad"],
            v["small2"], v["small3"], v["upb_grad"],
        ),
        [sds((T, 512), F32), sds((E, 512), F32), sds((NC, R, 512), BF), sds((16, 512), F32)],
        [V((chips, R, 512), BF)] * 3 + [V((chips, R, FF), BF), V((chips, F, 512), BF)]
        + [
            V((2, Z, 8, T, 128), BF), V((8, T, 128), BF), V((GM, 8, ZM, T, 128), BF),
            V((8, T, 128), BF), V((8, HD, T), BF), V((8, E, 128), BF),
            V((512, 8 * T), BF), V((512, 8 * E), BF), V((8 * T, 256), BF),
            V((S, R, 256), BF), V((S, R, 256), BF), V((S, R, 128), BF), V((S, R, 128), BF),
            V((NC, R, 512), BF), V((2, NC, R, 512), BF),
            V((S, 16, 512), F32), V((Z, 16, 512), F32), V((16, 512), F32), V((16, 512), F32),
            DMA((5, chips)), DMA((5, chips)),
            DMA((2, Z, 8)), DMA((2, Z, 8)), DMA((G, 1)), DMA((G, 1)),
            DMA((8,)), DMA((8,)), DMA((8,)), DMA((8,)), DMA((8,)), DMA((8,)),
            DMA((S,)), DMA((S,)), DMA((S,)), DMA((S,)),
            DMA((2, NC)), DMA((2, NC)), DMA((2, NC)), DMA((NC,)),
            DMA((S,)), DMA((S,)), DMA((Z,)), DMA((Z,)),
        ],
        far=(7,) if G > 1 else (),
    )
    vmem = pl.BlockSpec(memory_space=pltpu.VMEM)
    smem = pl.BlockSpec(memory_space=pltpu.SMEM)
    steps = v["time_table"].shape[0]
    outs = [
        sds((T, 512), BF), sds((T, 512), F32), sds((E, 512), F32), sds((steps, R), F32), sds((3, R), F32),
        sds((3, R), F32), sds((R, 1536), F32), sds((R, 512), F32), sds((R, 512), F32), sds((R, 1024), F32),
        sds((R, 512), F32), sds((R, FF), F32), sds((1, F), F32), sds((F, 512), F32), sds((1, R), F32),
    ]
    res = pl.pallas_call(
        finish_kernel,
        out_shape=outs,
        in_specs=[smem, smem] + [vmem] * 5,
        out_specs=[vmem] * len(outs),
        compiler_params=pltpu.CompilerParams(vmem_limit_bytes=room()),
        name="outputs",
    )(v["info"], v["timestep"], zfin, sums, hidden_grad, encoder_grad, v["layer_out"])
    res = list(res)
    res[12] = res[12].reshape(F)
    res[14] = res[14].reshape(R)
    return tuple(res)


def shards(
    hidden_in, encoder, segment_ids, timestep, out_grad, time_table, norm_gain, norm_bias,
    self_proj, self_out, cross_query, cross_memory, cross_out, up_weight, up_bias, down_weight, down_bias,
):
    S, Z = lax.axis_size("shard"), lax.axis_size("seq")
    T, R, F = hidden_in.shape[0], self_proj.shape[0], up_bias.shape[0]
    G = S // 8
    info, x_all, kv, qt, mem, enc_all, vecs, upb, gout, gcq, gco, gup, gdn = gather_call(
        S,
        Z,
        (
            timestep, segment_ids.reshape(-1, 128), hidden_in, time_table, norm_gain, norm_bias,
            up_bias, down_bias, self_proj, cross_memory, encoder,
            self_out, cross_query, cross_out, up_weight, down_weight,
        ),
    )
    wout, wcq, wco = gout.reshape(512, 512), gcq.reshape(512, 512), gco.reshape(512, 512)
    wup, wdn = gup.reshape(512, -1), gdn.reshape(-1, 512)
    kv = kv.reshape(S * Z, T, 128)

    ot, of, lse = attend(Z, True, info, qt, kv)
    at, after, n2, cqt, mkv = middle(G, Z, info, ot, hidden_in, vecs, wout, wcq, mem)
    mkv = mkv.reshape(DOCS * ENC // T, T, 128)
    crt, crf, clse = attend(Z, False, info, cqt, mkv)
    layer_out, d_after2, co_grad, up_grad, dn_grad, small3, upb_grad, dct, gproj, gmem = feed(
        crt, after, vecs, upb, wco, wup, wdn, out_grad, self_proj, cross_memory
    )
    dcqt, dmkv = attend_back(Z, False, info, cqt, mkv, dct, crf, clse)
    d_after, cq_grad, wout_grad, small2, dat, dmem = middle_back(
        dcqt, after, d_after2, n2, at, vecs, wcq, wout, dmkv.reshape(G, 8, Z, -1, 128)
    )
    dqt, dkv = attend_back(Z, True, info, qt, kv, dat, of, lse)
    return last(locals())


def solution(mesh):
    return jax.shard_map(
        shards,
        mesh=mesh,
        in_specs=(
            P(("shard", "seq"), None),
            P(("shard", "seq"), None),
            P(),
            P(),
            P(("shard", "seq"), None),
            P(None, "shard"),
            P(None, "shard"),
            P(None, "shard"),
            P("shard", None),
            P("shard", None),
            P("shard", None),
            P("shard", None),
            P("shard", None),
            P("shard", None),
            P("shard"),
            P("shard", None),
            P("shard"),
        ),
        out_specs=(
            P(("shard", "seq"), None),
            P(("shard", "seq"), None),
            P(("shard", "seq"), None),
            P(None, "shard"),
            P(None, "shard"),
            P(None, "shard"),
            P("shard", None),
            P("shard", None),
            P("shard", None),
            P("shard", None),
            P("shard", None),
            P("shard", None),
            P("shard"),
            P("shard", None),
            P("shard"),
        ),
        check_vma=False,
    )
```

```python
import functools

import jax
import jax.numpy as jnp
from jax import lax
from jax.experimental import pallas as pl
from jax.experimental.pallas import tpu as pltpu
from jax.sharding import PartitionSpec as P

H = 8
HD = 64
DOCS = 2
ENC = 1024
EPS = 1e-05
MASKED = -1e30
SCALE = HD**-0.5
MESH = pl.DeviceIdType.MESH
BF = jnp.bfloat16
F32 = jnp.float32
DMA = pltpu.SemaphoreType.DMA


def room(small=True):
    return (ROOM << 20) if small and lax.axis_size("shard") == 8 else (63 << 20)


ROOM = 30
ORDER = (0, 1, 2, 4, 3, 6, 5, 7)


def mm(a, b, ca=1, cb=0):
    return lax.dot_general(a, b, (((ca,), (cb,)), ((), ())), preferred_element_type=F32)


def flip(j, bits):
    low, mid, high = j % 2, (j // 2) % 2, (j // 4) % 2
    out = j
    if bits & 1:
        out = out + 1 - 2 * low
    if bits & 2:
        out = out + 2 - 4 * mid
    if bits & 4:
        out = out + 4 - 8 * high
    return out


def rcopy(src, dst, send_sem, recv_sem, device_id):
    return pltpu.make_async_remote_copy(
        src_ref=src,
        dst_ref=dst,
        send_sem=send_sem,
        recv_sem=recv_sem,
        device_id=device_id,
        device_id_type=MESH,
    )


def place():
    shard, seq = lax.axis_index("shard"), lax.axis_index("seq")
    return shard, seq, shard % 8, shard // 8


def greet(peers):
    barrier = pltpu.get_barrier_semaphore()
    count = 0
    for condition, device in peers:
        if condition is None:
            pl.semaphore_signal(barrier, inc=1, device_id=device, device_id_type=MESH)
            count = count + 1
        else:

            @pl.when(condition)
            def _(device=device):
                pl.semaphore_signal(barrier, inc=1, device_id=device, device_id_type=MESH)

            count = count + jnp.where(condition, 1, 0)
    pl.semaphore_wait(barrier, count)


def norm_stats(value):
    center = jnp.mean(value, axis=1, keepdims=True)
    offset = value - center
    spread = jnp.mean(offset * offset, axis=1, keepdims=True)
    scale = lax.rsqrt(spread + EPS)
    return offset * scale, scale


def norm_back(d_out, hat, scale, gain):
    d_hat = d_out * gain
    first = jnp.mean(d_hat, axis=1, keepdims=True)
    second = jnp.mean(d_hat * hat, axis=1, keepdims=True)
    d_in = scale * (d_hat - first - hat * second)
    return d_in, jnp.sum(d_out * hat, axis=0, keepdims=True), jnp.sum(d_out, axis=0, keepdims=True)


def embed(hid_ref, bound, vecs_ref, block):
    rows = hid_ref.shape[0]
    pos = block * rows + lax.broadcasted_iota(jnp.int32, (rows, 1), 0)
    picked = jnp.where(pos < bound, vecs_ref[0:1, :], vecs_ref[1:2, :])
    return hid_ref[...].astype(F32) + picked


class Whole:
    def __init__(self, pairs, S, sems):
        self.pairs, self.S = pairs, S
        self.local, self.send, self.recv, self.half, self.pass_on = sems
        self.s = lax.axis_index("shard")
        self.core, self.chip = self.s % 2, self.s // 2
        self.sib = flip(self.s, 1)
        self.near = S == 8
        self.flow = []

    @staticmethod
    def scratch(count, S):
        return [DMA((count,)), DMA((count, max(8, S // 2))), DMA((count, S)), DMA((count, 2)), DMA((count, S // 2))]

    def copy(self, a, source, n, to, half=None):
        shard, whole = self.pairs[a]
        target = whole.at[source]
        if half is not None:
            rows = shard.shape[0] // 2
            target = whole.at[source, pl.ds(half * rows, rows)]
            recv = self.half.at[a, half]
        else:
            recv = self.recv.at[a, source]
        origin = shard if n < 0 else target
        send = self.send.at[a, -n - 1 if n < 0 else n]
        return rcopy(origin, target, send, recv, {"shard": to})

    def go(self, *args):
        c = self.copy(*args)
        c.start()
        self.flow.append(c)

    def arrived(self, a, source, half=None):
        self.copy(a, source, 7, self.sib, half).wait_recv()

    def same_core(self, d):
        return ((self.chip + d) % (self.S // 2)) * 2 + self.core

    def start(self, a):
        shard, whole = self.pairs[a]
        pltpu.make_async_copy(shard, whole.at[self.s], self.local.at[a]).start()
        s = self.s
        if self.near:
            self.go(a, s, -1, flip(s, 2))
            self.go(a, s, -2, flip(s, 4))
            self.go(a, s, -3, self.sib)
            return
        for d in range(1, self.S // 2):
            c = rcopy(shard, whole.at[s], self.send.at[a, d], self.recv.at[a, s], {"shard": self.same_core(d)})
            c.start()
            self.flow.append(c)
        c = rcopy(shard, whole.at[s], self.send.at[a, 0], self.recv.at[a, s], {"shard": self.sib})
        c.start()
        self.flow.append(c)

    def relay(self, a):
        if not self.near:
            return
        x, y = flip(self.s, 2), flip(self.s, 4)
        self.arrived(a, x)
        self.go(a, x, 3, y, 0)
        self.go(a, x, 5, self.sib)
        self.arrived(a, y)
        self.go(a, y, 4, x, 1)
        self.go(a, y, 6, self.sib)

    def finish(self, a):
        if self.near:
            far = flip(self.s, 6)
            self.arrived(a, far, 0)
            self.arrived(a, far, 1)
            self.go(a, far, 7, self.sib)
            return
        _, whole = self.pairs[a]
        for d in range(1, self.S // 2):
            q = self.same_core(self.S // 2 - d)
            self.arrived(a, q)
            c = rcopy(whole.at[q], whole.at[q], self.pass_on.at[a, d], self.recv.at[a, q], {"shard": self.sib})
            c.start()
            self.flow.append(c)

    def wait(self, a):
        shard, whole = self.pairs[a]
        self.arrived(a, self.sib)
        for d in range(1, self.S // 2):
            self.arrived(a, flip(self.same_core(d), 1))
        pltpu.make_async_copy(shard, whole.at[self.s], self.local.at[a]).wait()

    def drain(self):
        for c in self.flow:
            c.wait_send()


def gather_kernel(
    S, Z, G,
    timestep, seg_h, hid_h, table_h, gain_h, shift_h, upb_h, dnb_h, wproj_h, wmem_h, enc_h,
    wout, wcq, wco, wup, wdn,
    info, x_all, kv, qt, mkv, enc_all, vecs, upb_row, gout, gcq, gco, gup, gdn,
    seg, hid, table, gain, shift, upb, dnb, wproj, wmem, enc, in_sem,
    rows_f, small, small_all, wsend, msend, w_all, m_all, sm_s, sm_r, w_s, w_r, mw_s, mw_r,
    x_s, x_r, e_s, e_r, z_s, z_r, mb_s, mb_r, *whole_sems
):
    s, z, j, m = place()
    near = (seg, hid, table, gain, shift, upb, dnb, wproj, wmem, enc)
    far = (seg_h, hid_h, table_h, gain_h, shift_h, upb_h, dnb_h, wproj_h, wmem_h, enc_h)
    loads = [pltpu.make_async_copy(b, a, in_sem.at[n]) for n, (a, b) in enumerate(zip(near, far))]
    for c in loads:
        c.start()
    for c in loads:
        c.wait()
    R, F = wproj.shape[0], upb.shape[0]
    T, E = hid.shape[0], enc.shape[0]
    sib = flip(s, 1)

    step = lax.broadcasted_iota(jnp.int32, table.shape, 0)
    rows_f[...] = jnp.zeros((16, 256), F32)
    for d in range(DOCS):
        picked = jnp.where(step == timestep[d], table[...].astype(F32), 0.0)
        rows_f[d : d + 1, :R] = jnp.sum(picked, axis=0, keepdims=True)
    rows_f[2:5, :R] = gain[...].astype(F32)
    rows_f[5:8, :R] = shift[...].astype(F32)
    rows_f[8:9, :F] = upb[...].astype(F32).reshape(1, F)
    rows_f[9:10, :R] = dnb[...].astype(F32).reshape(1, R)
    small[...] = rows_f[...].astype(BF)
    small_all[s] = small[...]
    bound = jnp.sum(jnp.where(seg[...] == 0, 1.0, 0.0)).astype(jnp.int32)
    info[0] = bound
    info[1] = m
    info[2] = z
    info[3] = s

    greet(
        [(None, {"shard": (s + d) % S}) for d in range(1, S)]
        + [(z > 0, {"seq": z - 1}), (z < Z - 1, {"seq": z + 1})]
    )
    small_copies = []
    for d in range(1, S):
        c = rcopy(small, small_all.at[s], sm_s.at[d], sm_r.at[s], {"shard": (s + d) % S})
        c.start()
        small_copies.append(c)
    for h in range(H):
        k = wproj[:, 512 + HD * h : 512 + HD * (h + 1)]
        v = wproj[:, 1024 + HD * h : 1024 + HD * (h + 1)]
        q = wproj[:, HD * h : HD * (h + 1)]
        wsend[h] = jnp.concatenate([k, v, q, jnp.zeros_like(q)], axis=1)
        msend[h] = jnp.concatenate(
            [wmem[:, HD * h : HD * (h + 1)], wmem[:, 512 + HD * h : 512 + HD * (h + 1)]], axis=1
        )
    w_all[s] = wsend[j]
    m_all[s] = msend[j]
    w_copies = []
    for d in range(1, S):
        p = (s + d) % S
        c = rcopy(wsend.at[p % 8], w_all.at[s], w_s.at[d], w_r.at[s], {"shard": p})
        c.start()
        w_copies.append(c)
        c = rcopy(msend.at[p % 8], m_all.at[s], mw_s.at[d], mw_r.at[s], {"shard": p})
        c.start()
        w_copies.append(c)
    for d in range(1, S):
        p = (s + d) % S
        rcopy(small, small_all.at[p], sm_s.at[d], sm_r.at[p], {"shard": p}).wait_recv()
    rows = jnp.zeros((16, 512), F32)
    lane = lax.broadcasted_iota(jnp.int32, (256, 512), 0)
    col = lax.broadcasted_iota(jnp.int32, (256, 512), 1)
    for p in range(S):
        pick = ((col - p * R) == lane) & (lane < R)
        rows = rows + mm(small_all[p], jnp.where(pick, 1.0, 0.0).astype(BF))
        upb_row[0:1, p * F : (p + 1) * F] = small_all[p].astype(F32)[8:9, :F]
    vecs[...] = rows

    hat, _ = norm_stats(embed(hid, bound, vecs, s * Z + z))
    x_all[j] = (hat * vecs[2:3, :] + vecs[5:6, :]).astype(BF)
    enc_all[j] = enc[...]
    copies = []

    def send_block(ref, bits_source, bits_target, send, recv):
        source = flip(j, bits_source)
        c = rcopy(ref.at[source], ref.at[source], send, recv.at[source], {"shard": flip(s, bits_target)})
        c.start()
        copies.append(c)

    def wait_block(ref, bits, recv):
        source = flip(j, bits)
        rcopy(ref.at[source], ref.at[source], x_s.at[0], recv.at[source], {"shard": sib}).wait_recv()

    for n, bits in enumerate((1, 2, 4, 6)):
        send_block(x_all, 0, bits, x_s.at[n], x_r)
    for n, bits in enumerate((1, 2, 4, 6)):
        send_block(enc_all, 0, bits, e_s.at[n], e_r)
    whole = Whole(
        ((wout, gout), (wcq, gcq), (wco, gco), (wup, gup), (wdn, gdn)), S, whole_sems
    )
    for d in range(1, S):
        p = (s + d) % S
        rcopy(wsend.at[0], w_all.at[p], w_s.at[d], w_r.at[p], {"shard": p}).wait_recv()
        rcopy(msend.at[0], m_all.at[p], mw_s.at[d], mw_r.at[p], {"shard": p}).wait_recv()
    w_head = w_all[...].reshape(S * R, 256)
    m_head = m_all[...].reshape(S * R, 128)

    def z_copy(ref, block, plane, step, hop, slot):
        view = ref.at[:, block, plane] if block is not None else ref.at[:, :, plane]
        way = (step + 1) // 2
        return rcopy(view, view, z_s.at[way, hop, slot], z_r.at[way, hop, slot], {"seq": z + step})

    def z_passes(step, hop):
        origin = z - step * hop
        return (z + step >= 0) & (z + step < Z) & (origin >= 0) & (origin < Z)

    def z_send(ref, block, hop, slot):
        for step in (-1, 1):

            @pl.when(z_passes(step, hop))
            def _(step=step):
                z_copy(ref, block, z - step * hop, step, hop, slot).start()

    def z_recv(ref, block, hop, slot):
        for step in (-1, 1):
            origin = z - step * hop

            @pl.when((origin >= 0) & (origin < Z))
            def _(step=step, origin=origin):
                z_copy(ref, block, origin, step, hop - 1, slot).wait_recv()

    def z_drain(ref, block, hop, slot):
        for step in (-1, 1):

            @pl.when(z_passes(step, hop))
            def _(step=step):
                z_copy(ref, block, z - step * hop, step, hop, slot).wait_send()

    def member_copy(ref, block, d, slot, mine):
        other = (m + d) % G
        at = m if mine else other
        view = ref.at[at, block, z] if block is not None else ref.at[at, :, z]
        return rcopy(view, view, mb_s.at[d, slot], mb_r.at[at, slot], {"shard": other * 8 + j})

    def spread(ref, block, slot):
        for d in range(1, G):
            member_copy(ref, block, d, slot, True).start()
        for d in range(1, G):
            member_copy(ref, block, d, slot, False).wait_recv()
        z_send(ref, block, 0, slot)

    def block_step(n):
        bits = ORDER[n]
        block = flip(j, bits)
        if bits:
            wait_block(x_all, bits, x_r)
            if bits in (2, 4, 6):
                send_block(x_all, bits, 1, x_s.at[3 + bits // 2], x_r)
        kvq = mm(x_all[block], w_head)
        kv[m, block, z] = kvq[:, :128].astype(BF)
        spread(kv, block, n)
        qt[block] = (SCALE * kvq[:, 128:256].T[:HD]).astype(BF)

    def encoder_step():
        for bits in (2, 4, 6):
            wait_block(enc_all, bits, e_r)
            send_block(enc_all, bits, 1, e_s.at[3 + bits // 2], e_r)
        for bits in (1, 3, 5, 7):
            wait_block(enc_all, bits, e_r)
        for b in range(8):
            mkv[b] = mm(enc_all[b], m_head).astype(BF)

    lag = 2
    last_step = max(8, 7 + lag * (Z - 1))
    for n in range(last_step + 1):
        if n < 8:
            block_step(n)
        if n == 8:
            encoder_step()
        if n == 5:
            for a in range(5):
                whole.start(a)
        for hop in range(1, Z):
            slot = n - lag * hop
            if 0 <= slot < 8:
                z_recv(kv, flip(j, ORDER[slot]), hop, slot)
                z_send(kv, flip(j, ORDER[slot]), hop, slot)
        if n == 8:
            for a in range(3):
                whole.relay(a)
        if n == min(10, last_step):
            whole.relay(3)
        if n == min(11, last_step):
            whole.relay(4)
        if n == min(12, last_step):
            for a in range(3):
                whole.finish(a)
    for a in range(3, 5):
        whole.finish(a)
    for a in range(5):
        whole.wait(a)
    whole.drain()
    for c in small_copies + w_copies + copies:
        c.wait_send()
    for n, bits in enumerate(ORDER):
        for d in range(1, G):
            member_copy(kv, flip(j, bits), d, n, True).wait_send()
        for hop in range(Z - 1):
            z_drain(kv, flip(j, bits), hop, n)


def gather_call(S, Z, args):
    G = S // 8
    (timestep, seg, hid, table, gain, shift, upb, dnb, wproj, wmem, enc, *weights) = args
    T, R, E, F = hid.shape[0], wproj.shape[0], enc.shape[0], upb.shape[0]
    vmem = pl.BlockSpec(memory_space=pltpu.VMEM)
    smem = pl.BlockSpec(memory_space=pltpu.SMEM)
    hbm = pl.BlockSpec(memory_space=pl.ANY)
    sds = jax.ShapeDtypeStruct
    outs = [
        sds((4,), jnp.int32),
        sds((8, T, 512), BF),
        sds((G, 8, Z, T, 128), BF),
        sds((8, HD, T), BF),
        sds((8, E, 128), BF),
        sds((8, E, 512), BF),
        sds((16, 512), F32),
        sds((1, S * F), F32),
    ] + [sds((S,) + w.shape, BF) for w in weights]
    return pl.pallas_call(
        functools.partial(gather_kernel, S, Z, G),
        out_shape=outs,
        in_specs=[smem] + [pl.BlockSpec(memory_space=pltpu.HBM)] * (len(args) - 1),
        out_specs=[smem] + [vmem] * 7 + [hbm] * 5,
        scratch_shapes=[pltpu.VMEM(a.shape, a.dtype) for a in args[1:11]]
        + [
            DMA((10,)),
            pltpu.VMEM((16, 256), F32),
            pltpu.VMEM((16, 256), BF),
            pltpu.VMEM((S, 16, 256), BF),
            pltpu.VMEM((8, R, 256), BF),
            pltpu.VMEM((8, R, 128), BF),
            pltpu.VMEM((S, R, 256), BF),
            pltpu.VMEM((S, R, 128), BF),
            DMA((S,)), DMA((S,)), DMA((S,)), DMA((S,)), DMA((S,)), DMA((S,)),
            DMA((8,)), DMA((8,)), DMA((8,)), DMA((8,)),
            DMA((2, Z, 9)), DMA((2, Z, 9)),
            DMA((G, 9)), DMA((G, 9)),
        ] + Whole.scratch(5, S),
        compiler_params=pltpu.CompilerParams(
            collective_id=0, has_side_effects=True, vmem_limit_bytes=room()
        ),
        name="gather_qkv",
    )(args[0], *[pltpu.with_memory_space_constraint(a, pltpu.HBM) for a in args[1:]])


GROUP = 4


class Reach:
    def __init__(self, causal, bound, block, rows):
        self.causal, self.bound, self.rows = causal, bound, rows
        self.query_first = block * rows
        last = self.query_first + rows - 1
        mixed = (self.query_first < bound) & (last >= bound)
        if causal:
            self.least = jnp.where(self.query_first < bound, 0, bound)
            begin, self.end = self.least // rows, block + 1
            self.mixed = mixed | (self.end < GROUP)
        else:
            per = ENC // rows
            self.least = 0
            begin = jnp.where(self.query_first < bound, 0, per)
            self.end = jnp.where(last < bound, per, 2 * per)
            self.mixed = mixed
        self.groups = (self.end - begin + GROUP - 1) // GROUP

    def mask(self, kind, start, limit, n, scores):
        if kind == "plain":
            return scores
        rows = self.rows
        key = (start + n) * rows + lax.broadcasted_iota(jnp.int32, (rows, 1), 0)
        query = self.query_first + lax.broadcasted_iota(jnp.int32, (1, scores.shape[1]), 1)
        if kind == "edge":
            allowed = (key >= self.least) & (key < limit)
            if n == GROUP - 1:
                allowed = allowed & (key <= query)
        elif self.causal:
            least = jnp.where(query < self.bound, 0, self.bound)
            allowed = (key < limit) & (key <= query) & (key >= least)
        else:
            allowed = jnp.where(query < self.bound, 0, 1) == key // ENC
        return jnp.where(allowed, scores, MASKED)

    def walk(self, group, state):
        def turn(kind, g, carry):
            if kind == "edge":
                g = jnp.where(g == 0, 0, self.groups - 1)
            stop = self.end - GROUP * (self.groups - 1 - g)
            return group(kind, jnp.maximum(stop - GROUP, 0), stop * self.rows, carry)

        mixed, groups = self.mixed, self.groups
        state = lax.fori_loop(
            0, jnp.where(mixed, groups, 0), functools.partial(turn, "full"), state
        )
        if not self.causal:
            return lax.fori_loop(
                0, jnp.where(mixed, 0, groups), functools.partial(turn, "plain"), state
            )
        state = lax.fori_loop(
            0,
            jnp.where(mixed, 0, jnp.minimum(groups, 2)),
            functools.partial(turn, "edge"),
            state,
        )
        return lax.fori_loop(
            1, jnp.where(mixed, 1, groups - 1), functools.partial(turn, "plain"), state
        )


def turned_keys(kv, kt, half, begin, end):
    rows = kv.shape[1]

    def turn(kb, carry):
        flat = kv[kb].astype(F32).T[HD * half : HD * (half + 1)].astype(BF)
        kt[:, pl.ds(pl.multiple_of(kb * rows, rows), rows)] = flat
        return carry

    lax.fori_loop(begin, end, turn, 0)


def key_span(causal, bound, low, Z, rows, count):
    if not causal:
        return 0, count
    return jnp.where(low * rows < bound, 0, bound) // rows, low + 7 * Z + 1


def attend_kernel(Z, causal, info, qt, kv, ot, of, lse, vt):
    bound, m, z = info[0], info[1], info[2]
    count, T = kv.shape[0], kv.shape[1]
    low = 8 * m * Z + z

    begin, end = key_span(causal, bound, low, Z, T, count)
    turned_keys(kv, vt, 1, jnp.maximum(begin - GROUP, 0), end)

    def one_block(i, carry):
        reach = Reach(causal, bound, low + i * Z, T)
        queries = jnp.concatenate([qt[i], jnp.zeros((HD, T), BF)], axis=0)

        def group(kind, start, limit, state):
            top, total, acc = state
            half = GROUP // 2
            raws = [
                mm(kv[pl.ds(start + half * h, half)].reshape(half * T, 128), queries) for h in range(2)
            ]
            for h, raw in enumerate(raws):
                scores = [
                    reach.mask(kind, start, limit, half * h + n, raw[n * T : (n + 1) * T])
                    for n in range(half)
                ]
                new_top = top
                for piece in scores:
                    new_top = jnp.maximum(new_top, jnp.max(piece, axis=0, keepdims=True))
                fade = jnp.exp(top - new_top)
                total = total * fade
                parts = []
                for piece in scores:
                    powers = jnp.exp(piece - new_top)
                    total = total + jnp.sum(powers, axis=0, keepdims=True)
                    parts.append(powers.astype(BF))
                values = vt[:, pl.ds(pl.multiple_of((start + half * h) * T, T), half * T)]
                acc = acc * fade + mm(values, jnp.concatenate(parts, axis=0))
                top = new_top
            return top, total, acc

        top, total, acc = reach.walk(
            group,
            (jnp.full((1, T), MASKED, F32), jnp.zeros((1, T), F32), jnp.zeros((HD, T), F32)),
        )
        result = acc / total
        ot[i] = result.astype(BF)
        of[i] = result
        lse[i] = top + jnp.log(total)
        return carry

    lax.fori_loop(0, 8, one_block, 0)


def attend(Z, causal, info, qt, kv):
    T = qt.shape[2]
    sds = jax.ShapeDtypeStruct
    vmem = pl.BlockSpec(memory_space=pltpu.VMEM)
    return pl.pallas_call(
        functools.partial(attend_kernel, Z, causal),
        out_shape=[sds((8, HD, T), BF), sds((8, HD, T), F32), sds((8, 1, T), F32)],
        in_specs=[pl.BlockSpec(memory_space=pltpu.SMEM), vmem, vmem],
        out_specs=[vmem] * 3,
        scratch_shapes=[pltpu.VMEM((HD, kv.shape[0] * T), BF)],
        compiler_params=pltpu.CompilerParams(vmem_limit_bytes=room()),
        name="attend_self" if causal else "attend_cross",
    )(info, qt, kv)


def attend_back_kernel(
    Z, causal, info, qt, kv, dt, of, lse, dq, dkv, kt, dkvf, qd, rows, raw, pair, stage, sem
):
    bound, m, z = info[0], info[1], info[2]
    count, T = kv.shape[0], kv.shape[1]
    low = 8 * m * Z + z
    zero = jnp.zeros((HD, T), BF)

    def clear(kb, carry):
        dkvf[kb] = jnp.zeros((T, 128), F32)
        return carry

    lax.fori_loop(0, count, clear, 0)

    begin, end = key_span(causal, bound, low, Z, T, count)
    turned_keys(kv, kt, 0, jnp.maximum(begin - GROUP, 0), end)

    def one_block(i, carry):
        reach = Reach(causal, bound, low + i * Z, T)
        qd[:HD, :T] = qt[i]
        qd[HD:, :T] = zero
        qd[:HD, T:] = zero
        qd[HD:, T:] = dt[i]
        both = jnp.concatenate([qt[i].astype(F32), dt[i].astype(F32)], axis=0).T
        lane = lax.broadcasted_iota(jnp.int32, both.shape, 1)
        rows[:T] = jnp.where(lane < HD, 0.0, both).astype(BF)
        rows[T:] = jnp.where(lane < HD, both, 0.0).astype(BF)
        delta = jnp.sum(dt[i].astype(F32) * of[i], axis=0, keepdims=True)
        level = lse[i]

        def group(kind, start, limit, acc):
            keys = kv[pl.ds(start, GROUP)].reshape(GROUP * T, 128)
            raw[...] = mm(keys, qd[...])
            for n in range(GROUP):
                at = slice(n * T, (n + 1) * T)
                probs = jnp.exp(reach.mask(kind, start, limit, n, raw[at, :T]) - level)
                pair[at, :T] = probs.astype(BF)
                pair[at, T:] = (probs * (raw[at, T:] - delta)).astype(BF)
            grads = mm(pair[...], rows[...])
            dkvf[pl.ds(start, GROUP)] += grads.reshape(GROUP, T, 128)
            flat = kt[:, pl.ds(pl.multiple_of(start * T, T), GROUP * T)]
            return acc + mm(flat, pair[:, T:])

        acc = reach.walk(group, jnp.zeros((HD, T), F32))
        dq[i] = (SCALE * acc).astype(BF)
        return carry

    lax.fori_loop(0, 8, one_block, 0)

    slots = stage.shape[0]

    def put(kb):
        return pltpu.make_async_copy(stage.at[kb % slots], dkv.at[kb], sem.at[kb % slots])

    def flush(kb, carry):
        @pl.when(kb >= slots)
        def _():
            put(kb).wait()

        stage[kb % slots] = dkvf[kb].astype(BF)
        put(kb).start()
        return carry

    def settle(kb, carry):
        put(kb).wait()
        return carry

    lax.fori_loop(0, count, flush, 0)
    lax.fori_loop(0, slots, settle, 0)


def attend_back(Z, causal, info, qt, kv, dt, of, lse):
    T = qt.shape[2]
    count = kv.shape[0]
    slots = count if count <= 32 else 2
    sds = jax.ShapeDtypeStruct
    vmem = pl.BlockSpec(memory_space=pltpu.VMEM)
    return pl.pallas_call(
        functools.partial(attend_back_kernel, Z, causal),
        out_shape=[sds((8, HD, T), BF), sds(kv.shape, BF)],
        in_specs=[pl.BlockSpec(memory_space=pltpu.SMEM)] + [vmem] * 5,
        out_specs=[vmem, pl.BlockSpec(memory_space=pl.ANY)],
        scratch_shapes=[
            pltpu.VMEM((HD, count * T), BF),
            pltpu.VMEM((count, T, 128), F32),
            pltpu.VMEM((128, 2 * T), BF),
            pltpu.VMEM((2 * T, 128), BF),
            pltpu.VMEM((GROUP * T, 2 * T), F32),
            pltpu.VMEM((GROUP * T, 2 * T), BF),
            pltpu.VMEM((slots, T, 128), BF),
            DMA((slots,)),
        ],
        compiler_params=pltpu.CompilerParams(vmem_limit_bytes=room()),
        name="attend_self_back" if causal else "attend_cross_back",
    )(info, qt, kv, dt, of, lse)


def greet_group(heads=False):
    s, z, j, m = place()
    peers = [(None, {"shard": m * 8 + (j + d) % 8}) for d in range(1, 8)]
    if heads:
        peers = peers + [(None, device) for _, _, _, device in kin()]
    greet(peers)


def kin():
    s, z, j, m = place()
    G, Z = lax.axis_size("shard") // 8, lax.axis_size("seq")
    out = []
    for dm in range(G):
        for dz in range(Z):
            if dm or dz:
                om, oz = (m + dm) % G, (z + dz) % Z
                out.append((dm * Z + dz, om, oz, {"shard": om * 8 + j, "seq": oz}))
    return out


def exchange_copies(src, dst, send, recv):
    s, z, j, m = place()
    out = []
    for d in (1, 2, 3, 4, 5, 6, 7):
        p = flip(j, d)
        out.append(rcopy(src.at[p], dst.at[j], send.at[d], recv.at[j], {"shard": m * 8 + p}))
    return out


def exchange_start(src, dst, send, recv):
    s, z, j, m = place()
    for c in exchange_copies(src, dst, send, recv):
        c.start()
    dst[j] = src[j]


def exchange_recv(src, dst, send, recv):
    s, z, j, m = place()
    for d in (1, 2, 3, 4, 5, 6, 7):
        p = flip(j, d)
        rcopy(src.at[p], dst.at[p], send.at[d], recv.at[p], {"shard": m * 8 + p}).wait_recv()


def exchange_sent(src, dst, send, recv):
    for c in exchange_copies(src, dst, send, recv):
        c.wait_send()


class ChipSums:
    def __init__(self, pairs, send, recv):
        self.pairs, self.send, self.recv = pairs, send, recv
        self.s = lax.axis_index("shard")
        self.core = self.s % 2
        self.chips = lax.axis_size("shard") // 2

    def piece(self, a, p):
        full, kept, _ = self.pairs[a]
        rows = kept.shape[1]
        return full.at[pl.ds(pl.multiple_of(p * rows, rows), rows), :]

    def copies(self):
        for a, (_, kept, buf) in enumerate(self.pairs):
            for q in range(self.chips):
                yield rcopy(
                    self.piece(a, 2 * q + 1 - self.core), buf.at[q], self.send.at[a, q], self.recv.at[a, q],
                    {"shard": flip(self.s, 1)},
                )

    def start(self):
        for c in self.copies():
            c.start()

    def finish(self):
        for c in self.copies():
            c.wait_recv()
        for a, (_, kept, buf) in enumerate(self.pairs):
            for q in range(self.chips):
                mine = self.piece(a, 2 * q + self.core)[...]
                kept[q] = (buf[q].astype(F32) + mine.astype(F32)).astype(BF)
        for c in self.copies():
            c.wait_send()


def remote_call(kernel, name, ident, ins, outs, scratch, smem=1, far=(), far_outs=()):
    vmem = pl.BlockSpec(memory_space=pltpu.VMEM)
    in_specs = [pl.BlockSpec(memory_space=pltpu.SMEM)] * smem + [vmem] * (len(ins) - smem)
    out_specs = [vmem] * len(outs)
    for n in far_outs:
        out_specs[n] = pl.BlockSpec(memory_space=pl.ANY)
    for n in far:
        in_specs[n] = pl.BlockSpec(memory_space=pl.ANY)
    return pl.pallas_call(
        kernel,
        out_shape=outs,
        in_specs=in_specs,
        out_specs=out_specs,
        scratch_shapes=scratch,
        compiler_params=pltpu.CompilerParams(
            collective_id=ident, has_side_effects=True, vmem_limit_bytes=room()
        ),
        name=name,
    )(*ins)


def middle_kernel(
    Z, bnd, ot, hid, vecs, wout, wcq, mem, at, after, n2, cqt, mkv, cq_send, s1, r1, s2, r2, s3, r3
):
    s, z, j, m = place()
    T = hid.shape[0]
    greet_group(True)
    exchange_start(ot, at, s1, r1)

    def memory_copies(mine):
        for n, om, oz, device in kin():
            c = m * Z + z if mine else om * Z + oz
            target = mkv.at[m, :, z] if mine else mkv.at[om, :, oz]
            yield rcopy(mem, target, s3.at[n], r3.at[c], device)

    for c in memory_copies(True):
        c.start()
    mkv[m, :, z] = mem[...]
    base = embed(hid, bnd[0], vecs, s * Z + z)
    exchange_recv(ot, at, s1, r1)
    attn = at[...].reshape(512, T).astype(F32).T.astype(BF)
    value = base + mm(attn, wout[...])
    after[...] = value
    hat, _ = norm_stats(value)
    normed = (hat * vecs[3:4, :] + vecs[6:7, :]).astype(BF)
    n2[...] = normed
    cq = mm(normed, wcq[...])
    cq_send[...] = (SCALE * cq.T).astype(BF).reshape(8, HD, T)
    exchange_start(cq_send, cqt, s2, r2)
    exchange_recv(cq_send, cqt, s2, r2)
    for c in memory_copies(False):
        c.wait_recv()
    exchange_sent(ot, at, s1, r1)
    exchange_sent(cq_send, cqt, s2, r2)
    for c in memory_copies(True):
        c.wait_send()


def middle(G, Z, bnd, ot, hid, vecs, wout, wcq, mem):
    T, E = hid.shape[0], mem.shape[1]
    sds = jax.ShapeDtypeStruct
    return remote_call(
        functools.partial(middle_kernel, Z),
        "middle",
        1,
        (bnd, ot, hid, vecs, wout, wcq, mem),
        [
            sds((8, HD, T), BF), sds((T, 512), F32), sds((T, 512), BF), sds((8, HD, T), BF),
            sds((G, 8, Z, E, 128), BF),
        ],
        [
            pltpu.VMEM((8, HD, T), BF), DMA((8,)), DMA((8,)), DMA((8,)), DMA((8,)),
            DMA((G * Z,)), DMA((G * Z,)),
        ],
    )


def erf(x):
    return lax.erf(x)


def feed_kernel(
    crt, after, vecs, upb, wco, wup, wdn, grad, wproj, wmem,
    layer_out, d_after, co_sum, up_sum, dn_sum, smalls, upb_grad, dct, gproj, gmem,
    ct, send, n3t, out_acc, dn_acc, co_grad, up_grad, dn_grad, co_buf, up_buf, dn_buf,
    s1, r1, s2, r2, s3, r3, *whole_sems
):
    T = after.shape[0]
    FF = wup.shape[1]
    S = lax.axis_size("shard")
    s = lax.axis_index("shard")
    greet([(None, {"shard": (s + d) % S}) for d in range(1, S)])
    exchange_start(crt, ct, s1, r1)
    whole = Whole(((wproj, gproj), (wmem, gmem)), S, whole_sems)
    for a in range(2):
        whole.start(a)
    g = grad[...]
    gf = g.astype(F32)
    gt = gf.T.astype(BF)
    exchange_recv(crt, ct, s1, r1)
    cross_t = ct[...].reshape(512, T)
    value = after[...] + mm(cross_t.astype(F32).T.astype(BF), wco[...])
    hat, scale = norm_stats(value)
    normed = hat * vecs[4:5, :] + vecs[7:8, :]
    n3 = normed.astype(BF)
    n3t[...] = n3.astype(F32).T.astype(BF)
    out_acc[...] = value + vecs[9:10, :]
    dn_acc[...] = jnp.zeros_like(dn_acc)
    width = 512
    for c in range(FF // width):
        lo, hi = c * width, (c + 1) * width
        pre = mm(n3, wup[:, lo:hi]) + upb[0:1, lo:hi]
        half = 0.5 * (1.0 + erf(pre * (0.5**0.5)))
        middle_c = (pre * half).astype(BF)
        out_acc[...] += mm(middle_c, wdn[lo:hi, :])
        slope = half + pre * (jnp.exp(-0.5 * pre * pre) * ((0.5 / jnp.pi) ** 0.5))
        d_pre = mm(g, wdn[lo:hi, :], 1, 1) * slope
        d_pre_b = d_pre.astype(BF)
        upb_grad[0:1, lo:hi] = jnp.sum(d_pre_b.astype(F32), axis=0, keepdims=True)
        dn_grad[lo:hi, :] = mm(middle_c.astype(F32).T.astype(BF), g).astype(BF)
        up_grad[:, lo:hi] = mm(n3t[...], d_pre_b).astype(BF)
        dn_acc[...] += mm(d_pre_b, wup[:, lo:hi], 1, 1)
    for a in range(2):
        whole.relay(a)
    layer_out[...] = out_acc[...].astype(BF)
    d_value, d_gain, d_shift = norm_back(dn_acc[...], hat, scale, vecs[4:5, :])
    total = gf + d_value
    d_after[...] = total
    smalls[0:1, :] = d_gain
    smalls[1:2, :] = d_shift
    smalls[2:3, :] = jnp.sum(gf, axis=0, keepdims=True)
    dc = total.astype(BF)
    d_cross = mm(wco[...], dc, 1, 1)
    send[...] = d_cross.astype(BF).reshape(8, HD, T)
    exchange_start(send, dct, s2, r2)
    co_grad[...] = mm(cross_t, dc).astype(BF)
    sums = ChipSums(
        ((co_grad, co_sum, co_buf), (up_grad, up_sum, up_buf), (dn_grad, dn_sum, dn_buf)), s3, r3
    )
    sums.start()
    for a in range(2):
        whole.finish(a)
    exchange_recv(send, dct, s2, r2)
    sums.finish()
    for a in range(2):
        whole.wait(a)
    whole.drain()
    exchange_sent(crt, ct, s1, r1)
    exchange_sent(send, dct, s2, r2)


def feed(crt, after, vecs, upb, wco, wup, wdn, grad, wproj, wmem):
    T, FF = after.shape[0], wup.shape[1]
    S = lax.axis_size("shard")
    chips, R, F = S // 2, 512 // S, FF // S
    sds = jax.ShapeDtypeStruct
    return remote_call(
        feed_kernel,
        "feed_forward",
        2,
        (crt, after, vecs, upb, wco, wup, wdn, grad, wproj, wmem),
        [
            sds((T, 512), BF),
            sds((T, 512), F32),
            sds((chips, R, 512), BF),
            sds((chips, R, FF), BF),
            sds((chips, F, 512), BF),
            sds((8, 512), F32),
            sds((1, FF), F32),
            sds((8, HD, T), BF),
            sds((S,) + wproj.shape, BF),
            sds((S,) + wmem.shape, BF),
        ],
        [
            pltpu.VMEM((8, HD, T), BF),
            pltpu.VMEM((8, HD, T), BF),
            pltpu.VMEM((512, T), BF),
            pltpu.VMEM((T, 512), F32),
            pltpu.VMEM((T, 512), F32),
            pltpu.VMEM((512, 512), BF),
            pltpu.VMEM((512, FF), BF),
            pltpu.VMEM((FF, 512), BF),
            pltpu.VMEM((chips, R, 512), BF),
            pltpu.VMEM((chips, R, FF), BF),
            pltpu.VMEM((chips, F, 512), BF),
            DMA((8,)), DMA((8,)), DMA((8,)), DMA((8,)), DMA((3, chips)), DMA((3, chips)),
        ] + Whole.scratch(2, S),
        smem=0,
        far_outs=(8, 9),
    )


def middle_back_kernel(
    dcqt, after, d_after2, n2, at, vecs, wcq, wout, dmkv,
    d_after, cq_sum, out_sum, smalls, dat, dmem,
    home, send, parts, cq_grad, out_grad, cq_buf, out_buf, s1, r1, s2, r2, s3, r3, s4, r4
):
    s, z, j, m = place()
    G, Z = dmkv.shape[0], dmkv.shape[2]
    T = after.shape[0]
    greet_group(True)
    exchange_start(dcqt, home, s1, r1)

    def memory_copies(mine):
        for n, om, oz, device in kin():
            c = m * Z + z if mine else om * Z + oz
            yield rcopy(dmkv.at[om, :, oz], parts.at[c], s3.at[n], r3.at[c], device)

    for c in memory_copies(True):
        c.start()
    parts[m * Z + z] = dmkv[m, :, z]
    hat, scale = norm_stats(after[...])
    n2t = n2[...].astype(F32).T.astype(BF)
    exchange_recv(dcqt, home, s1, r1)
    dcq = home[...].reshape(512, T).astype(F32).T.astype(BF)
    d_value, d_gain, d_shift = norm_back(mm(dcq, wcq[...], 1, 1), hat, scale, vecs[3:4, :])
    total = d_after2[...] + d_value
    d_after[...] = total
    smalls[0:1, :] = d_gain
    smalls[1:2, :] = d_shift
    da = total.astype(BF)
    send[...] = mm(wout[...], da, 1, 1).astype(BF).reshape(8, HD, T)
    exchange_start(send, dat, s2, r2)
    cq_grad[...] = mm(n2t, dcq).astype(BF)
    out_grad[...] = mm(at[...].reshape(512, T), da).astype(BF)
    sums = ChipSums(((cq_grad, cq_sum, cq_buf), (out_grad, out_sum, out_buf)), s4, r4)
    sums.start()
    for c in memory_copies(False):
        c.wait_recv()
    total_mem = parts[0].astype(F32)
    for n in range(1, G * Z):
        total_mem = total_mem + parts[n].astype(F32)
    dmem[...] = total_mem.astype(BF)
    sums.finish()
    exchange_recv(send, dat, s2, r2)
    exchange_sent(dcqt, home, s1, r1)
    exchange_sent(send, dat, s2, r2)
    for c in memory_copies(True):
        c.wait_send()


def middle_back(dcqt, after, d_after2, n2, at, vecs, wcq, wout, dmkv):
    T = after.shape[0]
    G, _, Z, E, _ = dmkv.shape
    chips, R = 4 * G, 512 // (8 * G)
    sds = jax.ShapeDtypeStruct
    return remote_call(
        middle_back_kernel,
        "middle_back",
        3,
        (dcqt, after, d_after2, n2, at, vecs, wcq, wout, dmkv),
        [
            sds((T, 512), F32),
            sds((chips, R, 512), BF),
            sds((chips, R, 512), BF),
            sds((8, 512), F32),
            sds((8, HD, T), BF),
            sds((8, E, 128), BF),
        ],
        [
            pltpu.VMEM((8, HD, T), BF),
            pltpu.VMEM((8, HD, T), BF),
            pltpu.VMEM((G * Z, 8, E, 128), BF),
            pltpu.VMEM((512, 512), BF),
            pltpu.VMEM((512, 512), BF),
            pltpu.VMEM((chips, R, 512), BF),
            pltpu.VMEM((chips, R, 512), BF),
            DMA((8,)), DMA((8,)), DMA((8,)), DMA((8,)), DMA((G * Z,)), DMA((G * Z,)),
            DMA((2, chips)), DMA((2, chips)),
        ],
        smem=0,
    )


NC = 16


def last_kernel(
    S, Z, G,
    info, hid, vecs, d_after, x_all, enc_all, dqt, dkv, finm, wproj, wmem,
    out_g, cq_g, co_g, up_g, dn_g, small2, small3, upb_g,
    hidden_grad, encoder_grad, zfin, smalls_o,
    got_out, got_cq, got_co, got_up, got_dn,
    rk, fin, mbuf, hkv, hq, hm, turned, enc_turned, dall, psend, pgot, msend, mgot,
    wz, zin, sm_all, sm_z, sm_plane, sm_mine,
    b_s, b_r, k_s, k_r, mb_s, mb_r, hq_s, hq_r, hk_s, hk_r, hm_s, hm_r,
    p_s, p_r, pm_s, pm_r, c_s, c_r, f_s, f_r, sm_s, sm_r, sz_s, sz_r,
):
    s, z, j, m = place()
    T, E = hid.shape[0], enc_all.shape[1]
    R = 512 // S
    F = dn_g.shape[1]
    bound = info[0]
    chips = S // 2
    core, chip = s % 2, s // 2
    sib = flip(s, 1)
    ends = (Z - 1, 0)
    greet(
        [(None, {"shard": (s + d) % S}) for d in range(1, S)]
        + [(None, {"seq": (z + d) % Z}) for d in range(1, Z)]
    )
    sums = (out_g, cq_g, co_g, up_g, dn_g)
    gots = (got_out, got_cq, got_co, got_up, got_dn)

    if G > 1:
        for d in range(1, G):
            o = (m + d) % G
            rcopy(dkv.at[o], mbuf.at[m], mb_s.at[d, 0], mb_r.at[m, 0], {"shard": o * 8 + j}).start()
        own_part = pltpu.make_async_copy(dkv.at[m], mbuf.at[m], mb_s.at[0, 0])
        own_part.start()
        own_part.wait()
        for d in range(1, G):
            o = (m + d) % G
            rcopy(dkv.at[o], mbuf.at[o], mb_s.at[d, 0], mb_r.at[o, 0], {"shard": o * 8 + j}).wait_recv()
        for b in range(8):
            acc = mbuf[m, b].astype(F32)
            for d in range(1, G):
                acc = acc + mbuf[(m + d) % G, b].astype(F32)
            mbuf[m, b] = acc.astype(BF)
        part = mbuf.at[m]
    else:
        part = dkv.at[0]

    def z_view(slot, t):
        return part.at[slot, t]

    def z_buffer(way, t, slot):
        return rk.at[way, t, slot]

    def z_copy(way, t, slot, source):
        step = 2 * way - 1
        return rcopy(
            source, z_buffer(way, t, slot), k_s.at[way, t, slot], k_r.at[way, t, slot], {"seq": z + step}
        )

    for far in range(Z - 1, 0, -1):
        for slot in range(8):
            for way in (0, 1):
                t = z + (2 * way - 1) * far

                @pl.when((z == ends[way]) & (t >= 0) & (t < Z))
                def _(way=way, t=t, slot=slot):
                    z_copy(way, t, slot, z_view(slot, t)).start()

    def own_copy(a, q):
        return rcopy(
            sums[a].at[q], gots[a].at[chip], b_s.at[a, q], b_r.at[a, chip], {"shard": 2 * q + core}
        )

    for a in range(5):
        for d in range(1, chips):
            own_copy(a, (chip + d) % chips).start()
    exchange_start(dqt, hq, hq_s, hq_r)
    exchange_start(finm, hm, hm_s, hm_r)

    def turn_block(b):
        turned[:, b * T : (b + 1) * T] = x_all[b].astype(F32).T.astype(BF)

    def turn_query(b):
        dq_b = dqt[b].astype(F32)
        dall[b * T : (b + 1) * T, 128:] = (
            jnp.concatenate([dq_b, jnp.zeros_like(dq_b)], axis=0).T.astype(BF)
        )

    def turn_encoder():
        enc_turned[...] = enc_all[...].reshape(8 * E, 512).astype(F32).T.astype(BF)

    def own_sum(a):
        for d in range(1, chips):
            q = (chip + d) % chips
            rcopy(sums[a].at[q], gots[a].at[q], b_s.at[a, q], b_r.at[a, q], {"shard": 2 * q + core}).wait_recv()
        total = sums[a][chip].astype(F32)
        for d in range(1, chips):
            total = total + gots[a][(chip + d) % chips].astype(F32)
        total = total.astype(BF)
        if a < 3:
            wz[a] = total
        elif a == 3:
            for c in range(4):
                wz[3 + c] = total[:, 512 * c : 512 * (c + 1)]
        else:
            for c in range(4):
                wz[7 + c] = total[c * R : (c + 1) * R]

    block = s * Z + z
    work = [functools.partial(turn_block, b) for b in range(8)]
    work += [functools.partial(turn_query, b) for b in range(8)] + [turn_encoder]

    for far in range(Z - 1, 0, -1):
        for slot in range(8):
            if work:
                work.pop(0)()
            for way in (0, 1):
                t = z + (2 * way - 1) * far

                @pl.when((z != ends[way]) & (t >= 0) & (t < Z))
                def _(way=way, t=t, slot=slot):
                    z_copy(way, t, slot, z_view(slot, t)).wait_recv()
                    buf = z_buffer(way, t, slot)
                    buf[...] = (
                        buf[...].astype(F32) + z_view(slot, t)[...].astype(F32)
                    ).astype(BF)
                    z_copy(way, t, slot, buf).start()

    def inward(k, step):
        way = (step + 1) // 2
        return rcopy(wz.at[k], zin.at[way, k], c_s.at[way, k], c_r.at[way, k], {"seq": z + step})

    def outward(k, step):
        return rcopy(zfin.at[k], zfin.at[k], f_s.at[(step + 1) // 2, k], f_r.at[k], {"seq": z + step})

    def root(k):
        return max(Z // 2 - 1 + k % 2, 0) if Z > 1 else 0

    def tips(k):
        r = root(k)
        for step in (-1, 1):
            tip = ends[(step + 1) // 2]
            if tip != r:

                @pl.when(z == tip)
                def _(step=step):
                    inward(k, step).start()

    def partial(k):
        r = root(k)
        for step, beyond in ((-1, z > r), (1, z < r)):
            tip = ends[(step + 1) // 2]
            way = (step + 1) // 2

            @pl.when(beyond & (z != tip))
            def _(step=step, way=way):
                inward(k, step).wait_recv()
                wz[k] = (wz[k].astype(F32) + zin[way, k].astype(F32)).astype(BF)
                inward(k, step).start()

    def total_of(k):
        r = root(k)

        @pl.when(z == r)
        def _():
            total = wz[k].astype(F32)
            if r < Z - 1:
                inward(k, -1).wait_recv()
                total = total + zin[0, k].astype(F32)
            if r > 0:
                inward(k, 1).wait_recv()
                total = total + zin[1, k].astype(F32)
            zfin[k] = total.astype(BF)
            if r < Z - 1:
                outward(k, 1).start()
            if r > 0:
                outward(k, -1).start()

    def send_out(k):
        r = root(k)
        for step, beyond in ((1, z > r), (-1, z < r)):
            tip = Z - 1 if step > 0 else 0

            @pl.when(beyond)
            def _(step=step, tip=tip):
                outward(k, step).wait_recv()

                @pl.when(z != tip)
                def _():
                    outward(k, step).start()

    for task in work:
        task()
    psend_q = mm(turned[...], dall[:, 128:])
    for a in range(5):
        own_sum(a)
        for k in ((0,), (1,), (2,), (3, 4, 5, 6), (7, 8, 9, 10))[a]:
            tips(k)
    hat, scale = norm_stats(embed(hid, bound, vecs, block))

    for slot in range(8):
        for way in (0, 1):

            @pl.when(z != ends[way])
            def _(way=way, slot=slot):
                z_copy(way, z, slot, z_view(slot, z)).wait_recv()

        low = jnp.where(z == ends[0], 0.0, z_buffer(0, z, slot)[...].astype(F32))
        high = jnp.where(z == ends[1], 0.0, z_buffer(1, z, slot)[...].astype(F32))
        total = (low + high + z_view(slot, z)[...].astype(F32)).astype(BF)
        fin[slot] = total
        dall[slot * T : (slot + 1) * T, :128] = total
    exchange_start(fin, hkv, hk_s, hk_r)
    for k in range(3):
        partial(k)

    psend_kv = mm(turned[...], dall[:, :128])
    psend[...] = jnp.concatenate([psend_kv, psend_q], axis=1).astype(BF).reshape(S, R, 256)
    msend[...] = mm(enc_turned[...], finm[...].reshape(8 * E, 128)).astype(BF).reshape(S, R, 128)
    pgot[s] = psend[s]
    mgot[s] = msend[s]
    for d in range(1, S):
        p = (s + d) % S
        rcopy(psend.at[p], pgot.at[s], p_s.at[d], p_r.at[s], {"shard": p}).start()
        rcopy(msend.at[p], mgot.at[s], pm_s.at[d], pm_r.at[s], {"shard": p}).start()

    for k in range(3):
        total_of(k)
    for k in range(3, 6):
        partial(k)

    exchange_recv(dqt, hq, hq_s, hq_r)
    exchange_recv(fin, hkv, hk_s, hk_r)
    exchange_recv(finm, hm, hm_s, hm_r)
    d_query = hq[...].reshape(512, T).astype(F32).T.astype(BF)
    d_keys = jnp.concatenate([hkv[h][:, :HD] for h in range(H)], axis=1)
    d_values = jnp.concatenate([hkv[h][:, HD:] for h in range(H)], axis=1)
    d_norm = (
        mm(d_query, wproj[:, :512], 1, 1)
        + mm(d_keys, wproj[:, 512:1024], 1, 1)
        + mm(d_values, wproj[:, 1024:], 1, 1)
    )
    d_value, d_gain, d_shift = norm_back(d_norm, hat, scale, vecs[2:3, :])
    total = d_after[...] + d_value
    hidden_grad[...] = total
    pos = block * T + lax.broadcasted_iota(jnp.int32, (T, 1), 0)
    sm_mine[...] = jnp.zeros((16, 512), F32)
    sm_mine[0:1, :] = d_gain
    sm_mine[1:2, :] = small2[0:1, :]
    sm_mine[2:3, :] = small3[0:1, :]
    sm_mine[3:4, :] = d_shift
    sm_mine[4:5, :] = small2[1:2, :]
    sm_mine[5:6, :] = small3[1:2, :]
    sm_mine[6:7, :] = jnp.sum(jnp.where(pos < bound, total, 0.0), axis=0, keepdims=True)
    sm_mine[7:8, :] = jnp.sum(jnp.where(pos < bound, 0.0, total), axis=0, keepdims=True)
    sm_mine[8:9, :] = small3[2:3, :]
    for c in range(upb_g.shape[1] // 512):
        sm_mine[9 + c : 10 + c, :] = upb_g[0:1, 512 * c : 512 * (c + 1)]
    for d in range(1, S):
        rcopy(sm_mine, sm_all.at[s], sm_s.at[d], sm_r.at[s], {"shard": (s + d) % S}).start()
    sm_all[s] = sm_mine[...]

    for k in range(6, 11):
        partial(k)
        total_of(k - 3)

    for d in range(1, S):
        p = (s + d) % S
        rcopy(psend.at[p], pgot.at[p], p_s.at[d], p_r.at[p], {"shard": p}).wait_recv()
        rcopy(msend.at[p], mgot.at[p], pm_s.at[d], pm_r.at[p], {"shard": p}).wait_recv()
    heads, mheads = [], []
    for h in range(H):
        acc, accm = pgot[h].astype(F32), mgot[h].astype(F32)
        for g in range(1, G):
            acc = acc + pgot[8 * g + h].astype(F32)
            accm = accm + mgot[8 * g + h].astype(F32)
        heads.append(acc)
        mheads.append(accm)
    wz[11] = jnp.concatenate([v[:, 128 : 128 + HD] for v in heads], axis=1).astype(BF)
    wz[12] = jnp.concatenate([v[:, :HD] for v in heads], axis=1).astype(BF)
    wz[13] = jnp.concatenate([v[:, HD:128] for v in heads], axis=1).astype(BF)
    wz[14] = jnp.concatenate([v[:, :HD] for v in mheads], axis=1).astype(BF)
    wz[15] = jnp.concatenate([v[:, HD:] for v in mheads], axis=1).astype(BF)
    for k in range(11, NC):
        tips(k)
    for k in range(8, 11):
        total_of(k)
    for k in range(6):
        send_out(k)
    e_keys = jnp.concatenate([hm[h][:, :HD] for h in range(H)], axis=1)
    e_values = jnp.concatenate([hm[h][:, HD:] for h in range(H)], axis=1)
    encoder_grad[...] = mm(e_keys, wmem[:, :512], 1, 1) + mm(e_values, wmem[:, 512:], 1, 1)

    for d in range(1, S):
        p = (s + d) % S
        rcopy(sm_mine, sm_all.at[p], sm_s.at[d], sm_r.at[p], {"shard": p}).wait_recv()
    acc = sm_all[0]
    for p in range(1, S):
        acc = acc + sm_all[p]
    sm_plane[...] = acc
    for d in range(1, Z):
        rcopy(sm_plane, sm_z.at[z], sz_s.at[d], sz_r.at[z], {"seq": (z + d) % Z}).start()
    sm_z[z] = acc
    for k in range(11, NC):
        partial(k)
        send_out(k - 5)
    for k in range(11, NC):
        total_of(k)
    for k in range(11, NC):
        send_out(k)
    for d in range(1, Z):
        o = (z + d) % Z
        rcopy(sm_plane, sm_z.at[o], sz_s.at[d], sz_r.at[o], {"seq": o}).wait_recv()
    acc = sm_z[0]
    for o in range(1, Z):
        acc = acc + sm_z[o]
    smalls_o[...] = acc

    for a in range(5):
        for d in range(1, chips):
            own_copy(a, (chip + d) % chips).wait_send()
    for d in range(1, G):
        o = (m + d) % G
        rcopy(dkv.at[o], mbuf.at[m], mb_s.at[d, 0], mb_r.at[m, 0], {"shard": o * 8 + j}).wait_send()
    exchange_sent(dqt, hq, hq_s, hq_r)
    exchange_sent(fin, hkv, hk_s, hk_r)
    exchange_sent(finm, hm, hm_s, hm_r)
    for far in range(Z - 1, 0, -1):
        for slot in range(8):
            for way in (0, 1):
                t = z + (2 * way - 1) * far

                @pl.when((t >= 0) & (t < Z))
                def _(way=way, t=t, slot=slot):
                    z_copy(way, t, slot, z_view(slot, t)).wait_send()

    for d in range(1, S):
        p = (s + d) % S
        rcopy(psend.at[p], pgot.at[s], p_s.at[d], p_r.at[s], {"shard": p}).wait_send()
        rcopy(msend.at[p], mgot.at[s], pm_s.at[d], pm_r.at[s], {"shard": p}).wait_send()
        rcopy(sm_mine, sm_all.at[s], sm_s.at[d], sm_r.at[s], {"shard": p}).wait_send()
    for d in range(1, Z):
        rcopy(sm_plane, sm_z.at[z], sz_s.at[d], sz_r.at[z], {"seq": (z + d) % Z}).wait_send()
    for k in range(NC):
        r = root(k)
        for step, beyond in ((-1, z > r), (1, z < r)):

            @pl.when(beyond)
            def _(step=step):
                inward(k, step).wait_send()

        for step in (-1, 1):
            sends = (z >= r) & (z < Z - 1) if step > 0 else (z <= r) & (z > 0)

            @pl.when(sends)
            def _(step=step):
                outward(k, step).wait_send()


def finish_kernel(
    info, timestep, zfin, sums, hid_g, enc_g, lay,
    lay_o, hid_o, enc_o, time_o, gain_o, shift_o, proj_o, out_o, cq_o, mem_o, co_o, up_o, upb_o, dn_o, dnb_o,
):
    s = info[3]
    R, F = out_o.shape[0], upb_o.shape[1]
    lay_o[...] = lay[...]
    hid_o[...] = hid_g[...]
    enc_o[...] = enc_g[...]
    out_o[...] = zfin[0].astype(F32)
    cq_o[...] = zfin[1].astype(F32)
    co_o[...] = zfin[2].astype(F32)
    for c in range(4):
        up_o[:, 512 * c : 512 * (c + 1)] = zfin[3 + c].astype(F32)
        dn_o[c * R : (c + 1) * R, :] = zfin[7 + c].astype(F32)
    for c in range(3):
        proj_o[:, 512 * c : 512 * (c + 1)] = zfin[11 + c].astype(F32)
    for c in range(2):
        mem_o[:, 512 * c : 512 * (c + 1)] = zfin[14 + c].astype(F32)

    def own(width, first):
        row = lax.broadcasted_iota(jnp.int32, (512, width), 0)
        col = lax.broadcasted_iota(jnp.int32, (512, width), 1)
        pick = jnp.where(row == col + first, 1.0, 0.0)
        return lax.dot_general(
            sums[...], pick, (((1,), (0,)), ((), ())),
            preferred_element_type=F32, precision=lax.Precision.HIGHEST,
        )

    mine = own(R, s * R)
    gain_o[...] = mine[0:3]
    shift_o[...] = mine[3:6]
    dnb_o[...] = mine[8:9]
    step = lax.broadcasted_iota(jnp.int32, time_o.shape, 0)
    grad = jnp.zeros(time_o.shape, F32)
    for d in range(DOCS):
        grad = grad + jnp.where(step == timestep[d], mine[6 + d : 7 + d], 0.0)
    time_o[...] = grad
    wide = own(F, (s * F) % 512)
    row = lax.broadcasted_iota(jnp.int32, wide.shape, 0)
    upb_o[...] = jnp.sum(jnp.where(row == 9 + s * F // 512, wide, 0.0), axis=0, keepdims=True)


def last(v):
    S, Z, G = v["S"], v["Z"], v["G"]
    T, R, F, E = v["T"], v["R"], v["F"], v["encoder"].shape[0]
    FF = v["wup"].shape[1]
    chips = S // 2
    sds = jax.ShapeDtypeStruct
    V = pltpu.VMEM
    GM, ZM = (G, Z) if G > 1 else (1, 1)
    hidden_grad, encoder_grad, zfin, sums = remote_call(
        functools.partial(last_kernel, S, Z, G),
        "gradients_home",
        4,
        (
            v["info"], v["hidden_in"], v["vecs"], v["d_after"], v["x_all"], v["enc_all"], v["dqt"],
            v["dkv"].reshape(G, 8, Z, T, 128), v["dmem"],
            v["gproj"].reshape(512, 1536), v["gmem"].reshape(512, 1024),
            v["wout_grad"], v["cq_grad"], v["co_grad"], v["up_grad"], v["dn_grad"],
            v["small2"], v["small3"], v["upb_grad"],
        ),
        [sds((T, 512), F32), sds((E, 512), F32), sds((NC, R, 512), BF), sds((16, 512), F32)],
        [V((chips, R, 512), BF)] * 3 + [V((chips, R, FF), BF), V((chips, F, 512), BF)]
        + [
            V((2, Z, 8, T, 128), BF), V((8, T, 128), BF), V((GM, 8, ZM, T, 128), BF),
            V((8, T, 128), BF), V((8, HD, T), BF), V((8, E, 128), BF),
            V((512, 8 * T), BF), V((512, 8 * E), BF), V((8 * T, 256), BF),
            V((S, R, 256), BF), V((S, R, 256), BF), V((S, R, 128), BF), V((S, R, 128), BF),
            V((NC, R, 512), BF), V((2, NC, R, 512), BF),
            V((S, 16, 512), F32), V((Z, 16, 512), F32), V((16, 512), F32), V((16, 512), F32),
            DMA((5, chips)), DMA((5, chips)),
            DMA((2, Z, 8)), DMA((2, Z, 8)), DMA((G, 1)), DMA((G, 1)),
            DMA((8,)), DMA((8,)), DMA((8,)), DMA((8,)), DMA((8,)), DMA((8,)),
            DMA((S,)), DMA((S,)), DMA((S,)), DMA((S,)),
            DMA((2, NC)), DMA((2, NC)), DMA((2, NC)), DMA((NC,)),
            DMA((S,)), DMA((S,)), DMA((Z,)), DMA((Z,)),
        ],
        far=(7,) if G > 1 else (),
    )
    vmem = pl.BlockSpec(memory_space=pltpu.VMEM)
    smem = pl.BlockSpec(memory_space=pltpu.SMEM)
    steps = v["time_table"].shape[0]
    outs = [
        sds((T, 512), BF), sds((T, 512), F32), sds((E, 512), F32), sds((steps, R), F32), sds((3, R), F32),
        sds((3, R), F32), sds((R, 1536), F32), sds((R, 512), F32), sds((R, 512), F32), sds((R, 1024), F32),
        sds((R, 512), F32), sds((R, FF), F32), sds((1, F), F32), sds((F, 512), F32), sds((1, R), F32),
    ]
    res = pl.pallas_call(
        finish_kernel,
        out_shape=outs,
        in_specs=[smem, smem] + [vmem] * 5,
        out_specs=[vmem] * len(outs),
        compiler_params=pltpu.CompilerParams(vmem_limit_bytes=room()),
        name="outputs",
    )(v["info"], v["timestep"], zfin, sums, hidden_grad, encoder_grad, v["layer_out"])
    res = list(res)
    res[12] = res[12].reshape(F)
    res[14] = res[14].reshape(R)
    return tuple(res)


def shards(
    hidden_in, encoder, segment_ids, timestep, out_grad, time_table, norm_gain, norm_bias,
    self_proj, self_out, cross_query, cross_memory, cross_out, up_weight, up_bias, down_weight, down_bias,
):
    S, Z = lax.axis_size("shard"), lax.axis_size("seq")
    T, R, F = hidden_in.shape[0], self_proj.shape[0], up_bias.shape[0]
    G = S // 8
    info, x_all, kv, qt, mem, enc_all, vecs, upb, gout, gcq, gco, gup, gdn = gather_call(
        S,
        Z,
        (
            timestep, segment_ids.reshape(-1, 128), hidden_in, time_table, norm_gain, norm_bias,
            up_bias, down_bias, self_proj, cross_memory, encoder,
            self_out, cross_query, cross_out, up_weight, down_weight,
        ),
    )
    wout, wcq, wco = gout.reshape(512, 512), gcq.reshape(512, 512), gco.reshape(512, 512)
    wup, wdn = gup.reshape(512, -1), gdn.reshape(-1, 512)
    kv = kv.reshape(S * Z, T, 128)

    ot, of, lse = attend(Z, True, info, qt, kv)
    at, after, n2, cqt, mkv = middle(G, Z, info, ot, hidden_in, vecs, wout, wcq, mem)
    mkv = mkv.reshape(DOCS * ENC // T, T, 128)
    crt, crf, clse = attend(Z, False, info, cqt, mkv)
    layer_out, d_after2, co_grad, up_grad, dn_grad, small3, upb_grad, dct, gproj, gmem = feed(
        crt, after, vecs, upb, wco, wup, wdn, out_grad, self_proj, cross_memory
    )
    dcqt, dmkv = attend_back(Z, False, info, cqt, mkv, dct, crf, clse)
    d_after, cq_grad, wout_grad, small2, dat, dmem = middle_back(
        dcqt, after, d_after2, n2, at, vecs, wcq, wout, dmkv.reshape(G, 8, Z, -1, 128)
    )
    dqt, dkv = attend_back(Z, True, info, qt, kv, dat, of, lse)
    return last(locals())


def solution(mesh):
    return jax.shard_map(
        shards,
        mesh=mesh,
        in_specs=(
            P(("shard", "seq"), None),
            P(("shard", "seq"), None),
            P(),
            P(),
            P(("shard", "seq"), None),
            P(None, "shard"),
            P(None, "shard"),
            P(None, "shard"),
            P("shard", None),
            P("shard", None),
            P("shard", None),
            P("shard", None),
            P("shard", None),
            P("shard", None),
            P("shard"),
            P("shard", None),
            P("shard"),
        ),
        out_specs=(
            P(("shard", "seq"), None),
            P(("shard", "seq"), None),
            P(("shard", "seq"), None),
            P(None, "shard"),
            P(None, "shard"),
            P(None, "shard"),
            P("shard", None),
            P("shard", None),
            P("shard", None),
            P("shard", None),
            P("shard", None),
            P("shard", None),
            P("shard"),
            P("shard", None),
            P("shard"),
        ),
        check_vma=False,
    )
```

```python
import functools

import jax
import jax.numpy as jnp
from jax import lax
from jax.experimental import pallas as pl
from jax.experimental.pallas import tpu as pltpu
from jax.sharding import PartitionSpec as P

H = 8
HD = 64
DOCS = 2
ENC = 1024
EPS = 1e-05
MASKED = -1e30
SCALE = HD**-0.5
MESH = pl.DeviceIdType.MESH
BF = jnp.bfloat16
F32 = jnp.float32
DMA = pltpu.SemaphoreType.DMA


def room(small=True):
    return (ROOM << 20) if small and lax.axis_size("shard") == 8 else (63 << 20)


ROOM = 30
ORDER = (0, 1, 2, 4, 3, 6, 5, 7)


def mm(a, b, ca=1, cb=0):
    return lax.dot_general(a, b, (((ca,), (cb,)), ((), ())), preferred_element_type=F32)


def flip(j, bits):
    low, mid, high = j % 2, (j // 2) % 2, (j // 4) % 2
    out = j
    if bits & 1:
        out = out + 1 - 2 * low
    if bits & 2:
        out = out + 2 - 4 * mid
    if bits & 4:
        out = out + 4 - 8 * high
    return out


def rcopy(src, dst, send_sem, recv_sem, device_id):
    return pltpu.make_async_remote_copy(
        src_ref=src,
        dst_ref=dst,
        send_sem=send_sem,
        recv_sem=recv_sem,
        device_id=device_id,
        device_id_type=MESH,
    )


def place():
    shard, seq = lax.axis_index("shard"), lax.axis_index("seq")
    return shard, seq, shard % 8, shard // 8


def greet(peers):
    barrier = pltpu.get_barrier_semaphore()
    count = 0
    for condition, device in peers:
        if condition is None:
            pl.semaphore_signal(barrier, inc=1, device_id=device, device_id_type=MESH)
            count = count + 1
        else:

            @pl.when(condition)
            def _(device=device):
                pl.semaphore_signal(barrier, inc=1, device_id=device, device_id_type=MESH)

            count = count + jnp.where(condition, 1, 0)
    pl.semaphore_wait(barrier, count)


def norm_stats(value):
    center = jnp.mean(value, axis=1, keepdims=True)
    offset = value - center
    spread = jnp.mean(offset * offset, axis=1, keepdims=True)
    scale = lax.rsqrt(spread + EPS)
    return offset * scale, scale


def norm_back(d_out, hat, scale, gain):
    d_hat = d_out * gain
    first = jnp.mean(d_hat, axis=1, keepdims=True)
    second = jnp.mean(d_hat * hat, axis=1, keepdims=True)
    d_in = scale * (d_hat - first - hat * second)
    return d_in, jnp.sum(d_out * hat, axis=0, keepdims=True), jnp.sum(d_out, axis=0, keepdims=True)


def embed(hid_ref, bound, vecs_ref, block):
    rows = hid_ref.shape[0]
    pos = block * rows + lax.broadcasted_iota(jnp.int32, (rows, 1), 0)
    picked = jnp.where(pos < bound, vecs_ref[0:1, :], vecs_ref[1:2, :])
    return hid_ref[...].astype(F32) + picked


class Whole:
    def __init__(self, pairs, S, sems):
        self.pairs, self.S = pairs, S
        self.local, self.send, self.recv, self.half, self.pass_on = sems
        self.s = lax.axis_index("shard")
        self.core, self.chip = self.s % 2, self.s // 2
        self.sib = flip(self.s, 1)
        self.near = S == 8
        self.flow = []

    @staticmethod
    def scratch(count, S):
        return [DMA((count,)), DMA((count, max(8, S // 2))), DMA((count, S)), DMA((count, 2)), DMA((count, S // 2))]

    def copy(self, a, source, n, to, half=None):
        shard, whole = self.pairs[a]
        target = whole.at[source]
        if half is not None:
            rows = shard.shape[0] // 2
            target = whole.at[source, pl.ds(half * rows, rows)]
            recv = self.half.at[a, half]
        else:
            recv = self.recv.at[a, source]
        origin = shard if n < 0 else target
        send = self.send.at[a, -n - 1 if n < 0 else n]
        return rcopy(origin, target, send, recv, {"shard": to})

    def go(self, *args):
        c = self.copy(*args)
        c.start()
        self.flow.append(c)

    def arrived(self, a, source, half=None):
        self.copy(a, source, 7, self.sib, half).wait_recv()

    def same_core(self, d):
        return ((self.chip + d) % (self.S // 2)) * 2 + self.core

    def start(self, a):
        shard, whole = self.pairs[a]
        pltpu.make_async_copy(shard, whole.at[self.s], self.local.at[a]).start()
        s = self.s
        if self.near:
            self.go(a, s, -1, flip(s, 2))
            self.go(a, s, -2, flip(s, 4))
            self.go(a, s, -3, self.sib)
            return
        for d in range(1, self.S // 2):
            c = rcopy(shard, whole.at[s], self.send.at[a, d], self.recv.at[a, s], {"shard": self.same_core(d)})
            c.start()
            self.flow.append(c)
        c = rcopy(shard, whole.at[s], self.send.at[a, 0], self.recv.at[a, s], {"shard": self.sib})
        c.start()
        self.flow.append(c)

    def relay(self, a):
        if not self.near:
            return
        x, y = flip(self.s, 2), flip(self.s, 4)
        self.arrived(a, x)
        self.go(a, x, 3, y, 0)
        self.go(a, x, 5, self.sib)
        self.arrived(a, y)
        self.go(a, y, 4, x, 1)
        self.go(a, y, 6, self.sib)

    def finish(self, a):
        if self.near:
            far = flip(self.s, 6)
            self.arrived(a, far, 0)
            self.arrived(a, far, 1)
            self.go(a, far, 7, self.sib)
            return
        _, whole = self.pairs[a]
        for d in range(1, self.S // 2):
            q = self.same_core(self.S // 2 - d)
            self.arrived(a, q)
            c = rcopy(whole.at[q], whole.at[q], self.pass_on.at[a, d], self.recv.at[a, q], {"shard": self.sib})
            c.start()
            self.flow.append(c)

    def wait(self, a):
        shard, whole = self.pairs[a]
        self.arrived(a, self.sib)
        for d in range(1, self.S // 2):
            self.arrived(a, flip(self.same_core(d), 1))
        pltpu.make_async_copy(shard, whole.at[self.s], self.local.at[a]).wait()

    def drain(self):
        for c in self.flow:
            c.wait_send()


def gather_kernel(
    S, Z, G,
    timestep, seg_h, hid_h, table_h, gain_h, shift_h, upb_h, dnb_h, wproj_h, wmem_h, enc_h,
    wout, wcq, wco, wup, wdn,
    info, x_all, kv, qt, mkv, enc_all, vecs, upb_row, gout, gcq, gco, gup, gdn,
    seg, hid, table, gain, shift, upb, dnb, wproj, wmem, enc, in_sem,
    rows_f, small, small_all, wsend, msend, w_all, m_all, sm_s, sm_r, w_s, w_r, mw_s, mw_r,
    x_s, x_r, e_s, e_r, z_s, z_r, mb_s, mb_r, *whole_sems
):
    s, z, j, m = place()
    near = (seg, hid, table, gain, shift, upb, dnb, wproj, wmem, enc)
    far = (seg_h, hid_h, table_h, gain_h, shift_h, upb_h, dnb_h, wproj_h, wmem_h, enc_h)
    loads = [pltpu.make_async_copy(b, a, in_sem.at[n]) for n, (a, b) in enumerate(zip(near, far))]
    for c in loads:
        c.start()
    for c in loads:
        c.wait()
    R, F = wproj.shape[0], upb.shape[0]
    T, E = hid.shape[0], enc.shape[0]
    sib = flip(s, 1)

    step = lax.broadcasted_iota(jnp.int32, table.shape, 0)
    rows_f[...] = jnp.zeros((16, 256), F32)
    for d in range(DOCS):
        picked = jnp.where(step == timestep[d], table[...].astype(F32), 0.0)
        rows_f[d : d + 1, :R] = jnp.sum(picked, axis=0, keepdims=True)
    rows_f[2:5, :R] = gain[...].astype(F32)
    rows_f[5:8, :R] = shift[...].astype(F32)
    rows_f[8:9, :F] = upb[...].astype(F32).reshape(1, F)
    rows_f[9:10, :R] = dnb[...].astype(F32).reshape(1, R)
    small[...] = rows_f[...].astype(BF)
    small_all[s] = small[...]
    bound = jnp.sum(jnp.where(seg[...] == 0, 1.0, 0.0)).astype(jnp.int32)
    info[0] = bound
    info[1] = m
    info[2] = z
    info[3] = s

    greet(
        [(None, {"shard": (s + d) % S}) for d in range(1, S)]
        + [(z > 0, {"seq": z - 1}), (z < Z - 1, {"seq": z + 1})]
    )
    small_copies = []
    for d in range(1, S):
        c = rcopy(small, small_all.at[s], sm_s.at[d], sm_r.at[s], {"shard": (s + d) % S})
        c.start()
        small_copies.append(c)
    for h in range(H):
        k = wproj[:, 512 + HD * h : 512 + HD * (h + 1)]
        v = wproj[:, 1024 + HD * h : 1024 + HD * (h + 1)]
        q = wproj[:, HD * h : HD * (h + 1)]
        wsend[h] = jnp.concatenate([k, v, q, jnp.zeros_like(q)], axis=1)
        msend[h] = jnp.concatenate(
            [wmem[:, HD * h : HD * (h + 1)], wmem[:, 512 + HD * h : 512 + HD * (h + 1)]], axis=1
        )
    w_all[s] = wsend[j]
    m_all[s] = msend[j]
    w_copies = []
    for d in range(1, S):
        p = (s + d) % S
        c = rcopy(wsend.at[p % 8], w_all.at[s], w_s.at[d], w_r.at[s], {"shard": p})
        c.start()
        w_copies.append(c)
        c = rcopy(msend.at[p % 8], m_all.at[s], mw_s.at[d], mw_r.at[s], {"shard": p})
        c.start()
        w_copies.append(c)
    for d in range(1, S):
        p = (s + d) % S
        rcopy(small, small_all.at[p], sm_s.at[d], sm_r.at[p], {"shard": p}).wait_recv()
    rows = jnp.zeros((16, 512), F32)
    lane = lax.broadcasted_iota(jnp.int32, (256, 512), 0)
    col = lax.broadcasted_iota(jnp.int32, (256, 512), 1)
    for p in range(S):
        pick = ((col - p * R) == lane) & (lane < R)
        rows = rows + mm(small_all[p], jnp.where(pick, 1.0, 0.0).astype(BF))
        upb_row[0:1, p * F : (p + 1) * F] = small_all[p].astype(F32)[8:9, :F]
    vecs[...] = rows

    hat, _ = norm_stats(embed(hid, bound, vecs, s * Z + z))
    x_all[j] = (hat * vecs[2:3, :] + vecs[5:6, :]).astype(BF)
    enc_all[j] = enc[...]
    copies = []

    def send_block(ref, bits_source, bits_target, send, recv):
        source = flip(j, bits_source)
        c = rcopy(ref.at[source], ref.at[source], send, recv.at[source], {"shard": flip(s, bits_target)})
        c.start()
        copies.append(c)

    def wait_block(ref, bits, recv):
        source = flip(j, bits)
        rcopy(ref.at[source], ref.at[source], x_s.at[0], recv.at[source], {"shard": sib}).wait_recv()

    for n, bits in enumerate((1, 2, 4, 6)):
        send_block(x_all, 0, bits, x_s.at[n], x_r)
    for n, bits in enumerate((1, 2, 4, 6)):
        send_block(enc_all, 0, bits, e_s.at[n], e_r)
    whole = Whole(
        ((wout, gout), (wcq, gcq), (wco, gco), (wup, gup), (wdn, gdn)), S, whole_sems
    )
    for d in range(1, S):
        p = (s + d) % S
        rcopy(wsend.at[0], w_all.at[p], w_s.at[d], w_r.at[p], {"shard": p}).wait_recv()
        rcopy(msend.at[0], m_all.at[p], mw_s.at[d], mw_r.at[p], {"shard": p}).wait_recv()
    w_head = w_all[...].reshape(S * R, 256)
    m_head = m_all[...].reshape(S * R, 128)

    def z_copy(ref, block, plane, step, hop, slot):
        view = ref.at[:, block, plane] if block is not None else ref.at[:, :, plane]
        way = (step + 1) // 2
        return rcopy(view, view, z_s.at[way, hop, slot], z_r.at[way, hop, slot], {"seq": z + step})

    def z_passes(step, hop):
        origin = z - step * hop
        return (z + step >= 0) & (z + step < Z) & (origin >= 0) & (origin < Z)

    def z_send(ref, block, hop, slot):
        for step in (-1, 1):

            @pl.when(z_passes(step, hop))
            def _(step=step):
                z_copy(ref, block, z - step * hop, step, hop, slot).start()

    def z_recv(ref, block, hop, slot):
        for step in (-1, 1):
            origin = z - step * hop

            @pl.when((origin >= 0) & (origin < Z))
            def _(step=step, origin=origin):
                z_copy(ref, block, origin, step, hop - 1, slot).wait_recv()

    def z_drain(ref, block, hop, slot):
        for step in (-1, 1):

            @pl.when(z_passes(step, hop))
            def _(step=step):
                z_copy(ref, block, z - step * hop, step, hop, slot).wait_send()

    def member_copy(ref, block, d, slot, mine):
        other = (m + d) % G
        at = m if mine else other
        view = ref.at[at, block, z] if block is not None else ref.at[at, :, z]
        return rcopy(view, view, mb_s.at[d, slot], mb_r.at[at, slot], {"shard": other * 8 + j})

    def spread(ref, block, slot):
        for d in range(1, G):
            member_copy(ref, block, d, slot, True).start()
        for d in range(1, G):
            member_copy(ref, block, d, slot, False).wait_recv()
        z_send(ref, block, 0, slot)

    def block_step(n):
        bits = ORDER[n]
        block = flip(j, bits)
        if bits:
            wait_block(x_all, bits, x_r)
            if bits in (2, 4, 6):
                send_block(x_all, bits, 1, x_s.at[3 + bits // 2], x_r)
        kvq = mm(x_all[block], w_head)
        kv[m, block, z] = kvq[:, :128].astype(BF)
        spread(kv, block, n)
        qt[block] = (SCALE * kvq[:, 128:256].T[:HD]).astype(BF)

    def encoder_step():
        for bits in (2, 4, 6):
            wait_block(enc_all, bits, e_r)
            send_block(enc_all, bits, 1, e_s.at[3 + bits // 2], e_r)
        for bits in (1, 3, 5, 7):
            wait_block(enc_all, bits, e_r)
        for b in range(8):
            mkv[b] = mm(enc_all[b], m_head).astype(BF)

    lag = 3
    last_step = max(8, 7 + lag * (Z - 1))
    for n in range(last_step + 1):
        if n < 8:
            block_step(n)
        if n == 8:
            encoder_step()
        if n == 5:
            for a in range(5):
                whole.start(a)
        for hop in range(1, Z):
            slot = n - lag * hop
            if 0 <= slot < 8:
                z_recv(kv, flip(j, ORDER[slot]), hop, slot)
                z_send(kv, flip(j, ORDER[slot]), hop, slot)
        if n == 8:
            for a in range(3):
                whole.relay(a)
        if n == min(10, last_step):
            whole.relay(3)
        if n == min(11, last_step):
            whole.relay(4)
        if n == min(12, last_step):
            for a in range(3):
                whole.finish(a)
    for a in range(3, 5):
        whole.finish(a)
    for a in range(5):
        whole.wait(a)
    whole.drain()
    for c in small_copies + w_copies + copies:
        c.wait_send()
    for n, bits in enumerate(ORDER):
        for d in range(1, G):
            member_copy(kv, flip(j, bits), d, n, True).wait_send()
        for hop in range(Z - 1):
            z_drain(kv, flip(j, bits), hop, n)


def gather_call(S, Z, args):
    G = S // 8
    (timestep, seg, hid, table, gain, shift, upb, dnb, wproj, wmem, enc, *weights) = args
    T, R, E, F = hid.shape[0], wproj.shape[0], enc.shape[0], upb.shape[0]
    vmem = pl.BlockSpec(memory_space=pltpu.VMEM)
    smem = pl.BlockSpec(memory_space=pltpu.SMEM)
    hbm = pl.BlockSpec(memory_space=pl.ANY)
    sds = jax.ShapeDtypeStruct
    outs = [
        sds((4,), jnp.int32),
        sds((8, T, 512), BF),
        sds((G, 8, Z, T, 128), BF),
        sds((8, HD, T), BF),
        sds((8, E, 128), BF),
        sds((8, E, 512), BF),
        sds((16, 512), F32),
        sds((1, S * F), F32),
    ] + [sds((S,) + w.shape, BF) for w in weights]
    return pl.pallas_call(
        functools.partial(gather_kernel, S, Z, G),
        out_shape=outs,
        in_specs=[smem] + [pl.BlockSpec(memory_space=pltpu.HBM)] * (len(args) - 1),
        out_specs=[smem] + [vmem] * 7 + [hbm] * 5,
        scratch_shapes=[pltpu.VMEM(a.shape, a.dtype) for a in args[1:11]]
        + [
            DMA((10,)),
            pltpu.VMEM((16, 256), F32),
            pltpu.VMEM((16, 256), BF),
            pltpu.VMEM((S, 16, 256), BF),
            pltpu.VMEM((8, R, 256), BF),
            pltpu.VMEM((8, R, 128), BF),
            pltpu.VMEM((S, R, 256), BF),
            pltpu.VMEM((S, R, 128), BF),
            DMA((S,)), DMA((S,)), DMA((S,)), DMA((S,)), DMA((S,)), DMA((S,)),
            DMA((8,)), DMA((8,)), DMA((8,)), DMA((8,)),
            DMA((2, Z, 9)), DMA((2, Z, 9)),
            DMA((G, 9)), DMA((G, 9)),
        ] + Whole.scratch(5, S),
        compiler_params=pltpu.CompilerParams(
            collective_id=0, has_side_effects=True, vmem_limit_bytes=room()
        ),
        name="gather_qkv",
    )(args[0], *[pltpu.with_memory_space_constraint(a, pltpu.HBM) for a in args[1:]])


GROUP = 4


class Reach:
    def __init__(self, causal, bound, block, rows):
        self.causal, self.bound, self.rows = causal, bound, rows
        self.query_first = block * rows
        last = self.query_first + rows - 1
        mixed = (self.query_first < bound) & (last >= bound)
        if causal:
            self.least = jnp.where(self.query_first < bound, 0, bound)
            begin, self.end = self.least // rows, block + 1
            self.mixed = mixed | (self.end < GROUP)
        else:
            per = ENC // rows
            self.least = 0
            begin = jnp.where(self.query_first < bound, 0, per)
            self.end = jnp.where(last < bound, per, 2 * per)
            self.mixed = mixed
        self.groups = (self.end - begin + GROUP - 1) // GROUP

    def mask(self, kind, start, limit, n, scores):
        if kind == "plain":
            return scores
        rows = self.rows
        key = (start + n) * rows + lax.broadcasted_iota(jnp.int32, (rows, 1), 0)
        query = self.query_first + lax.broadcasted_iota(jnp.int32, (1, scores.shape[1]), 1)
        if kind == "edge":
            allowed = (key >= self.least) & (key < limit)
            if n == GROUP - 1:
                allowed = allowed & (key <= query)
        elif self.causal:
            least = jnp.where(query < self.bound, 0, self.bound)
            allowed = (key < limit) & (key <= query) & (key >= least)
        else:
            allowed = jnp.where(query < self.bound, 0, 1) == key // ENC
        return jnp.where(allowed, scores, MASKED)

    def walk(self, group, state):
        def turn(kind, g, carry):
            if kind == "edge":
                g = jnp.where(g == 0, 0, self.groups - 1)
            stop = self.end - GROUP * (self.groups - 1 - g)
            return group(kind, jnp.maximum(stop - GROUP, 0), stop * self.rows, carry)

        mixed, groups = self.mixed, self.groups
        state = lax.fori_loop(
            0, jnp.where(mixed, groups, 0), functools.partial(turn, "full"), state
        )
        if not self.causal:
            return lax.fori_loop(
                0, jnp.where(mixed, 0, groups), functools.partial(turn, "plain"), state
            )
        state = lax.fori_loop(
            0,
            jnp.where(mixed, 0, jnp.minimum(groups, 2)),
            functools.partial(turn, "edge"),
            state,
        )
        return lax.fori_loop(
            1, jnp.where(mixed, 1, groups - 1), functools.partial(turn, "plain"), state
        )


def turned_keys(kv, kt, half, begin, end):
    rows = kv.shape[1]

    def turn(kb, carry):
        flat = kv[kb].astype(F32).T[HD * half : HD * (half + 1)].astype(BF)
        kt[:, pl.ds(pl.multiple_of(kb * rows, rows), rows)] = flat
        return carry

    lax.fori_loop(begin, end, turn, 0)


def key_span(causal, bound, low, Z, rows, count):
    if not causal:
        return 0, count
    return jnp.where(low * rows < bound, 0, bound) // rows, low + 7 * Z + 1


def attend_kernel(Z, causal, info, qt, kv, ot, of, lse, vt):
    bound, m, z = info[0], info[1], info[2]
    count, T = kv.shape[0], kv.shape[1]
    low = 8 * m * Z + z

    begin, end = key_span(causal, bound, low, Z, T, count)
    turned_keys(kv, vt, 1, jnp.maximum(begin - GROUP, 0), end)

    def one_block(i, carry):
        reach = Reach(causal, bound, low + i * Z, T)
        queries = jnp.concatenate([qt[i], jnp.zeros((HD, T), BF)], axis=0)

        def group(kind, start, limit, state):
            top, total, acc = state
            half = GROUP // 2
            raws = [
                mm(kv[pl.ds(start + half * h, half)].reshape(half * T, 128), queries) for h in range(2)
            ]
            for h, raw in enumerate(raws):
                scores = [
                    reach.mask(kind, start, limit, half * h + n, raw[n * T : (n + 1) * T])
                    for n in range(half)
                ]
                new_top = top
                for piece in scores:
                    new_top = jnp.maximum(new_top, jnp.max(piece, axis=0, keepdims=True))
                fade = jnp.exp(top - new_top)
                total = total * fade
                parts = []
                for piece in scores:
                    powers = jnp.exp(piece - new_top)
                    total = total + jnp.sum(powers, axis=0, keepdims=True)
                    parts.append(powers.astype(BF))
                values = vt[:, pl.ds(pl.multiple_of((start + half * h) * T, T), half * T)]
                acc = acc * fade + mm(values, jnp.concatenate(parts, axis=0))
                top = new_top
            return top, total, acc

        top, total, acc = reach.walk(
            group,
            (jnp.full((1, T), MASKED, F32), jnp.zeros((1, T), F32), jnp.zeros((HD, T), F32)),
        )
        result = acc / total
        ot[i] = result.astype(BF)
        of[i] = result
        lse[i] = top + jnp.log(total)
        return carry

    lax.fori_loop(0, 8, one_block, 0)


def attend(Z, causal, info, qt, kv):
    T = qt.shape[2]
    sds = jax.ShapeDtypeStruct
    vmem = pl.BlockSpec(memory_space=pltpu.VMEM)
    return pl.pallas_call(
        functools.partial(attend_kernel, Z, causal),
        out_shape=[sds((8, HD, T), BF), sds((8, HD, T), F32), sds((8, 1, T), F32)],
        in_specs=[pl.BlockSpec(memory_space=pltpu.SMEM), vmem, vmem],
        out_specs=[vmem] * 3,
        scratch_shapes=[pltpu.VMEM((HD, kv.shape[0] * T), BF)],
        compiler_params=pltpu.CompilerParams(vmem_limit_bytes=room()),
        name="attend_self" if causal else "attend_cross",
    )(info, qt, kv)


def attend_back_kernel(
    Z, causal, info, qt, kv, dt, of, lse, dq, dkv, kt, dkvf, qd, rows, raw, pair, stage, sem
):
    bound, m, z = info[0], info[1], info[2]
    count, T = kv.shape[0], kv.shape[1]
    low = 8 * m * Z + z
    zero = jnp.zeros((HD, T), BF)

    def clear(kb, carry):
        dkvf[kb] = jnp.zeros((T, 128), F32)
        return carry

    lax.fori_loop(0, count, clear, 0)

    begin, end = key_span(causal, bound, low, Z, T, count)
    turned_keys(kv, kt, 0, jnp.maximum(begin - GROUP, 0), end)

    def one_block(i, carry):
        reach = Reach(causal, bound, low + i * Z, T)
        qd[:HD, :T] = qt[i]
        qd[HD:, :T] = zero
        qd[:HD, T:] = zero
        qd[HD:, T:] = dt[i]
        both = jnp.concatenate([qt[i].astype(F32), dt[i].astype(F32)], axis=0).T
        lane = lax.broadcasted_iota(jnp.int32, both.shape, 1)
        rows[:T] = jnp.where(lane < HD, 0.0, both).astype(BF)
        rows[T:] = jnp.where(lane < HD, both, 0.0).astype(BF)
        delta = jnp.sum(dt[i].astype(F32) * of[i], axis=0, keepdims=True)
        level = lse[i]

        def group(kind, start, limit, acc):
            for n in range(GROUP):
                raw[n * T : (n + 1) * T] = mm(kv[start + n], qd[...])
            for n in range(GROUP):
                at = slice(n * T, (n + 1) * T)
                probs = jnp.exp(reach.mask(kind, start, limit, n, raw[at, :T]) - level)
                pair[at, :T] = probs.astype(BF)
                pair[at, T:] = (probs * (raw[at, T:] - delta)).astype(BF)
                dkvf[start + n] += mm(pair[at], rows[...])
                flat = kt[:, pl.ds(pl.multiple_of((start + n) * T, T), T)]
                acc = acc + mm(flat, pair[at, T:])
            return acc

        acc = reach.walk(group, jnp.zeros((HD, T), F32))
        dq[i] = (SCALE * acc).astype(BF)
        return carry

    lax.fori_loop(0, 8, one_block, 0)

    slots = stage.shape[0]

    def put(kb):
        return pltpu.make_async_copy(stage.at[kb % slots], dkv.at[kb], sem.at[kb % slots])

    def flush(kb, carry):
        @pl.when(kb >= slots)
        def _():
            put(kb).wait()

        stage[kb % slots] = dkvf[kb].astype(BF)
        put(kb).start()
        return carry

    def settle(kb, carry):
        put(kb).wait()
        return carry

    lax.fori_loop(0, count, flush, 0)
    lax.fori_loop(0, slots, settle, 0)


def attend_back(Z, causal, info, qt, kv, dt, of, lse):
    T = qt.shape[2]
    count = kv.shape[0]
    slots = count if count <= 32 else 2
    sds = jax.ShapeDtypeStruct
    vmem = pl.BlockSpec(memory_space=pltpu.VMEM)
    return pl.pallas_call(
        functools.partial(attend_back_kernel, Z, causal),
        out_shape=[sds((8, HD, T), BF), sds(kv.shape, BF)],
        in_specs=[pl.BlockSpec(memory_space=pltpu.SMEM)] + [vmem] * 5,
        out_specs=[vmem, pl.BlockSpec(memory_space=pl.ANY)],
        scratch_shapes=[
            pltpu.VMEM((HD, count * T), BF),
            pltpu.VMEM((count, T, 128), F32),
            pltpu.VMEM((128, 2 * T), BF),
            pltpu.VMEM((2 * T, 128), BF),
            pltpu.VMEM((GROUP * T, 2 * T), F32),
            pltpu.VMEM((GROUP * T, 2 * T), BF),
            pltpu.VMEM((slots, T, 128), BF),
            DMA((slots,)),
        ],
        compiler_params=pltpu.CompilerParams(vmem_limit_bytes=room()),
        name="attend_self_back" if causal else "attend_cross_back",
    )(info, qt, kv, dt, of, lse)


def greet_group(heads=False):
    s, z, j, m = place()
    peers = [(None, {"shard": m * 8 + (j + d) % 8}) for d in range(1, 8)]
    if heads:
        peers = peers + [(None, device) for _, _, _, device in kin()]
    greet(peers)


def kin():
    s, z, j, m = place()
    G, Z = lax.axis_size("shard") // 8, lax.axis_size("seq")
    out = []
    for dm in range(G):
        for dz in range(Z):
            if dm or dz:
                om, oz = (m + dm) % G, (z + dz) % Z
                out.append((dm * Z + dz, om, oz, {"shard": om * 8 + j, "seq": oz}))
    return out


def exchange_copies(src, dst, send, recv):
    s, z, j, m = place()
    out = []
    for d in (1, 2, 3, 4, 5, 6, 7):
        p = flip(j, d)
        out.append(rcopy(src.at[p], dst.at[j], send.at[d], recv.at[j], {"shard": m * 8 + p}))
    return out


def exchange_start(src, dst, send, recv):
    s, z, j, m = place()
    for c in exchange_copies(src, dst, send, recv):
        c.start()
    dst[j] = src[j]


def exchange_recv(src, dst, send, recv):
    s, z, j, m = place()
    for d in (1, 2, 3, 4, 5, 6, 7):
        p = flip(j, d)
        rcopy(src.at[p], dst.at[p], send.at[d], recv.at[p], {"shard": m * 8 + p}).wait_recv()


def exchange_sent(src, dst, send, recv):
    for c in exchange_copies(src, dst, send, recv):
        c.wait_send()


class ChipSums:
    def __init__(self, pairs, send, recv):
        self.pairs, self.send, self.recv = pairs, send, recv
        self.s = lax.axis_index("shard")
        self.core = self.s % 2
        self.chips = lax.axis_size("shard") // 2

    def piece(self, a, p):
        full, kept, _ = self.pairs[a]
        rows = kept.shape[1]
        return full.at[pl.ds(pl.multiple_of(p * rows, rows), rows), :]

    def copies(self):
        for a, (_, kept, buf) in enumerate(self.pairs):
            for q in range(self.chips):
                yield rcopy(
                    self.piece(a, 2 * q + 1 - self.core), buf.at[q], self.send.at[a, q], self.recv.at[a, q],
                    {"shard": flip(self.s, 1)},
                )

    def start(self):
        for c in self.copies():
            c.start()

    def finish(self):
        for c in self.copies():
            c.wait_recv()
        for a, (_, kept, buf) in enumerate(self.pairs):
            for q in range(self.chips):
                mine = self.piece(a, 2 * q + self.core)[...]
                kept[q] = (buf[q].astype(F32) + mine.astype(F32)).astype(BF)
        for c in self.copies():
            c.wait_send()


def remote_call(kernel, name, ident, ins, outs, scratch, smem=1, far=(), far_outs=()):
    vmem = pl.BlockSpec(memory_space=pltpu.VMEM)
    in_specs = [pl.BlockSpec(memory_space=pltpu.SMEM)] * smem + [vmem] * (len(ins) - smem)
    out_specs = [vmem] * len(outs)
    for n in far_outs:
        out_specs[n] = pl.BlockSpec(memory_space=pl.ANY)
    for n in far:
        in_specs[n] = pl.BlockSpec(memory_space=pl.ANY)
    return pl.pallas_call(
        kernel,
        out_shape=outs,
        in_specs=in_specs,
        out_specs=out_specs,
        scratch_shapes=scratch,
        compiler_params=pltpu.CompilerParams(
            collective_id=ident, has_side_effects=True, vmem_limit_bytes=room()
        ),
        name=name,
    )(*ins)


def middle_kernel(
    Z, bnd, ot, hid, vecs, wout, wcq, mem, at, after, n2, cqt, mkv, cq_send, s1, r1, s2, r2, s3, r3
):
    s, z, j, m = place()
    T = hid.shape[0]
    greet_group(True)
    exchange_start(ot, at, s1, r1)

    def memory_copies(mine):
        for n, om, oz, device in kin():
            c = m * Z + z if mine else om * Z + oz
            target = mkv.at[m, :, z] if mine else mkv.at[om, :, oz]
            yield rcopy(mem, target, s3.at[n], r3.at[c], device)

    for c in memory_copies(True):
        c.start()
    mkv[m, :, z] = mem[...]
    base = embed(hid, bnd[0], vecs, s * Z + z)
    exchange_recv(ot, at, s1, r1)
    attn = at[...].reshape(512, T).astype(F32).T.astype(BF)
    value = base + mm(attn, wout[...])
    after[...] = value
    hat, _ = norm_stats(value)
    normed = (hat * vecs[3:4, :] + vecs[6:7, :]).astype(BF)
    n2[...] = normed
    cq = mm(normed, wcq[...])
    cq_send[...] = (SCALE * cq.T).astype(BF).reshape(8, HD, T)
    exchange_start(cq_send, cqt, s2, r2)
    exchange_recv(cq_send, cqt, s2, r2)
    for c in memory_copies(False):
        c.wait_recv()
    exchange_sent(ot, at, s1, r1)
    exchange_sent(cq_send, cqt, s2, r2)
    for c in memory_copies(True):
        c.wait_send()


def middle(G, Z, bnd, ot, hid, vecs, wout, wcq, mem):
    T, E = hid.shape[0], mem.shape[1]
    sds = jax.ShapeDtypeStruct
    return remote_call(
        functools.partial(middle_kernel, Z),
        "middle",
        1,
        (bnd, ot, hid, vecs, wout, wcq, mem),
        [
            sds((8, HD, T), BF), sds((T, 512), F32), sds((T, 512), BF), sds((8, HD, T), BF),
            sds((G, 8, Z, E, 128), BF),
        ],
        [
            pltpu.VMEM((8, HD, T), BF), DMA((8,)), DMA((8,)), DMA((8,)), DMA((8,)),
            DMA((G * Z,)), DMA((G * Z,)),
        ],
    )


def erf(x):
    return lax.erf(x)


def feed_kernel(
    crt, after, vecs, upb, wco, wup, wdn, grad, wproj, wmem,
    layer_out, d_after, co_sum, up_sum, dn_sum, smalls, upb_grad, dct, gproj, gmem,
    ct, send, n3t, out_acc, dn_acc, co_grad, up_grad, dn_grad, co_buf, up_buf, dn_buf,
    s1, r1, s2, r2, s3, r3, *whole_sems
):
    T = after.shape[0]
    FF = wup.shape[1]
    S = lax.axis_size("shard")
    s = lax.axis_index("shard")
    greet([(None, {"shard": (s + d) % S}) for d in range(1, S)])
    exchange_start(crt, ct, s1, r1)
    whole = Whole(((wproj, gproj), (wmem, gmem)), S, whole_sems)
    for a in range(2):
        whole.start(a)
    g = grad[...]
    gf = g.astype(F32)
    gt = gf.T.astype(BF)
    exchange_recv(crt, ct, s1, r1)
    cross_t = ct[...].reshape(512, T)
    value = after[...] + mm(cross_t.astype(F32).T.astype(BF), wco[...])
    hat, scale = norm_stats(value)
    normed = hat * vecs[4:5, :] + vecs[7:8, :]
    n3 = normed.astype(BF)
    n3t[...] = n3.astype(F32).T.astype(BF)
    out_acc[...] = value + vecs[9:10, :]
    dn_acc[...] = jnp.zeros_like(dn_acc)
    width = 512
    for c in range(FF // width):
        lo, hi = c * width, (c + 1) * width
        pre = mm(n3, wup[:, lo:hi]) + upb[0:1, lo:hi]
        half = 0.5 * (1.0 + erf(pre * (0.5**0.5)))
        middle_c = (pre * half).astype(BF)
        out_acc[...] += mm(middle_c, wdn[lo:hi, :])
        slope = half + pre * (jnp.exp(-0.5 * pre * pre) * ((0.5 / jnp.pi) ** 0.5))
        d_pre = mm(g, wdn[lo:hi, :], 1, 1) * slope
        d_pre_b = d_pre.astype(BF)
        upb_grad[0:1, lo:hi] = jnp.sum(d_pre_b.astype(F32), axis=0, keepdims=True)
        dn_grad[lo:hi, :] = mm(middle_c.astype(F32).T.astype(BF), g).astype(BF)
        up_grad[:, lo:hi] = mm(n3t[...], d_pre_b).astype(BF)
        dn_acc[...] += mm(d_pre_b, wup[:, lo:hi], 1, 1)
    for a in range(2):
        whole.relay(a)
    layer_out[...] = out_acc[...].astype(BF)
    d_value, d_gain, d_shift = norm_back(dn_acc[...], hat, scale, vecs[4:5, :])
    total = gf + d_value
    d_after[...] = total
    smalls[0:1, :] = d_gain
    smalls[1:2, :] = d_shift
    smalls[2:3, :] = jnp.sum(gf, axis=0, keepdims=True)
    dc = total.astype(BF)
    d_cross = mm(wco[...], dc, 1, 1)
    send[...] = d_cross.astype(BF).reshape(8, HD, T)
    exchange_start(send, dct, s2, r2)
    co_grad[...] = mm(cross_t, dc).astype(BF)
    sums = ChipSums(
        ((co_grad, co_sum, co_buf), (up_grad, up_sum, up_buf), (dn_grad, dn_sum, dn_buf)), s3, r3
    )
    sums.start()
    for a in range(2):
        whole.finish(a)
    exchange_recv(send, dct, s2, r2)
    sums.finish()
    for a in range(2):
        whole.wait(a)
    whole.drain()
    exchange_sent(crt, ct, s1, r1)
    exchange_sent(send, dct, s2, r2)


def feed(crt, after, vecs, upb, wco, wup, wdn, grad, wproj, wmem):
    T, FF = after.shape[0], wup.shape[1]
    S = lax.axis_size("shard")
    chips, R, F = S // 2, 512 // S, FF // S
    sds = jax.ShapeDtypeStruct
    return remote_call(
        feed_kernel,
        "feed_forward",
        2,
        (crt, after, vecs, upb, wco, wup, wdn, grad, wproj, wmem),
        [
            sds((T, 512), BF),
            sds((T, 512), F32),
            sds((chips, R, 512), BF),
            sds((chips, R, FF), BF),
            sds((chips, F, 512), BF),
            sds((8, 512), F32),
            sds((1, FF), F32),
            sds((8, HD, T), BF),
            sds((S,) + wproj.shape, BF),
            sds((S,) + wmem.shape, BF),
        ],
        [
            pltpu.VMEM((8, HD, T), BF),
            pltpu.VMEM((8, HD, T), BF),
            pltpu.VMEM((512, T), BF),
            pltpu.VMEM((T, 512), F32),
            pltpu.VMEM((T, 512), F32),
            pltpu.VMEM((512, 512), BF),
            pltpu.VMEM((512, FF), BF),
            pltpu.VMEM((FF, 512), BF),
            pltpu.VMEM((chips, R, 512), BF),
            pltpu.VMEM((chips, R, FF), BF),
            pltpu.VMEM((chips, F, 512), BF),
            DMA((8,)), DMA((8,)), DMA((8,)), DMA((8,)), DMA((3, chips)), DMA((3, chips)),
        ] + Whole.scratch(2, S),
        smem=0,
        far_outs=(8, 9),
    )


def middle_back_kernel(
    dcqt, after, d_after2, n2, at, vecs, wcq, wout, dmkv,
    d_after, cq_sum, out_sum, smalls, dat, dmem,
    home, send, parts, cq_grad, out_grad, cq_buf, out_buf, s1, r1, s2, r2, s3, r3, s4, r4
):
    s, z, j, m = place()
    G, Z = dmkv.shape[0], dmkv.shape[2]
    T = after.shape[0]
    greet_group(True)
    exchange_start(dcqt, home, s1, r1)

    def memory_copies(mine):
        for n, om, oz, device in kin():
            c = m * Z + z if mine else om * Z + oz
            yield rcopy(dmkv.at[om, :, oz], parts.at[c], s3.at[n], r3.at[c], device)

    for c in memory_copies(True):
        c.start()
    parts[m * Z + z] = dmkv[m, :, z]
    hat, scale = norm_stats(after[...])
    n2t = n2[...].astype(F32).T.astype(BF)
    exchange_recv(dcqt, home, s1, r1)
    dcq = home[...].reshape(512, T).astype(F32).T.astype(BF)
    d_value, d_gain, d_shift = norm_back(mm(dcq, wcq[...], 1, 1), hat, scale, vecs[3:4, :])
    total = d_after2[...] + d_value
    d_after[...] = total
    smalls[0:1, :] = d_gain
    smalls[1:2, :] = d_shift
    da = total.astype(BF)
    send[...] = mm(wout[...], da, 1, 1).astype(BF).reshape(8, HD, T)
    exchange_start(send, dat, s2, r2)
    cq_grad[...] = mm(n2t, dcq).astype(BF)
    out_grad[...] = mm(at[...].reshape(512, T), da).astype(BF)
    sums = ChipSums(((cq_grad, cq_sum, cq_buf), (out_grad, out_sum, out_buf)), s4, r4)
    sums.start()
    for c in memory_copies(False):
        c.wait_recv()
    total_mem = parts[0].astype(F32)
    for n in range(1, G * Z):
        total_mem = total_mem + parts[n].astype(F32)
    dmem[...] = total_mem.astype(BF)
    sums.finish()
    exchange_recv(send, dat, s2, r2)
    exchange_sent(dcqt, home, s1, r1)
    exchange_sent(send, dat, s2, r2)
    for c in memory_copies(True):
        c.wait_send()


def middle_back(dcqt, after, d_after2, n2, at, vecs, wcq, wout, dmkv):
    T = after.shape[0]
    G, _, Z, E, _ = dmkv.shape
    chips, R = 4 * G, 512 // (8 * G)
    sds = jax.ShapeDtypeStruct
    return remote_call(
        middle_back_kernel,
        "middle_back",
        3,
        (dcqt, after, d_after2, n2, at, vecs, wcq, wout, dmkv),
        [
            sds((T, 512), F32),
            sds((chips, R, 512), BF),
            sds((chips, R, 512), BF),
            sds((8, 512), F32),
            sds((8, HD, T), BF),
            sds((8, E, 128), BF),
        ],
        [
            pltpu.VMEM((8, HD, T), BF),
            pltpu.VMEM((8, HD, T), BF),
            pltpu.VMEM((G * Z, 8, E, 128), BF),
            pltpu.VMEM((512, 512), BF),
            pltpu.VMEM((512, 512), BF),
            pltpu.VMEM((chips, R, 512), BF),
            pltpu.VMEM((chips, R, 512), BF),
            DMA((8,)), DMA((8,)), DMA((8,)), DMA((8,)), DMA((G * Z,)), DMA((G * Z,)),
            DMA((2, chips)), DMA((2, chips)),
        ],
        smem=0,
    )


NC = 16


def last_kernel(
    S, Z, G,
    info, hid, vecs, d_after, x_all, enc_all, dqt, dkv, finm, wproj, wmem,
    out_g, cq_g, co_g, up_g, dn_g, small2, small3, upb_g,
    hidden_grad, encoder_grad, zfin, smalls_o,
    got_out, got_cq, got_co, got_up, got_dn,
    rk, fin, mbuf, hkv, hq, hm, turned, enc_turned, dall, psend, pgot, msend, mgot,
    wz, zin, sm_all, sm_z, sm_plane, sm_mine,
    b_s, b_r, k_s, k_r, mb_s, mb_r, hq_s, hq_r, hk_s, hk_r, hm_s, hm_r,
    p_s, p_r, pm_s, pm_r, c_s, c_r, f_s, f_r, sm_s, sm_r, sz_s, sz_r,
):
    s, z, j, m = place()
    T, E = hid.shape[0], enc_all.shape[1]
    R = 512 // S
    F = dn_g.shape[1]
    bound = info[0]
    chips = S // 2
    core, chip = s % 2, s // 2
    sib = flip(s, 1)
    ends = (Z - 1, 0)
    greet(
        [(None, {"shard": (s + d) % S}) for d in range(1, S)]
        + [(None, {"seq": (z + d) % Z}) for d in range(1, Z)]
    )
    sums = (out_g, cq_g, co_g, up_g, dn_g)
    gots = (got_out, got_cq, got_co, got_up, got_dn)

    if G > 1:
        for d in range(1, G):
            o = (m + d) % G
            rcopy(dkv.at[o], mbuf.at[m], mb_s.at[d, 0], mb_r.at[m, 0], {"shard": o * 8 + j}).start()
        own_part = pltpu.make_async_copy(dkv.at[m], mbuf.at[m], mb_s.at[0, 0])
        own_part.start()
        own_part.wait()
        for d in range(1, G):
            o = (m + d) % G
            rcopy(dkv.at[o], mbuf.at[o], mb_s.at[d, 0], mb_r.at[o, 0], {"shard": o * 8 + j}).wait_recv()
        for b in range(8):
            acc = mbuf[m, b].astype(F32)
            for d in range(1, G):
                acc = acc + mbuf[(m + d) % G, b].astype(F32)
            mbuf[m, b] = acc.astype(BF)
        part = mbuf.at[m]
    else:
        part = dkv.at[0]

    def z_view(slot, t):
        return part.at[slot, t]

    def z_buffer(way, t, slot):
        return rk.at[way, t, slot]

    def z_copy(way, t, slot, source):
        step = 2 * way - 1
        return rcopy(
            source, z_buffer(way, t, slot), k_s.at[way, t, slot], k_r.at[way, t, slot], {"seq": z + step}
        )

    for far in range(Z - 1, 0, -1):
        for slot in range(8):
            for way in (0, 1):
                t = z + (2 * way - 1) * far

                @pl.when((z == ends[way]) & (t >= 0) & (t < Z))
                def _(way=way, t=t, slot=slot):
                    z_copy(way, t, slot, z_view(slot, t)).start()

    def own_copy(a, q):
        return rcopy(
            sums[a].at[q], gots[a].at[chip], b_s.at[a, q], b_r.at[a, chip], {"shard": 2 * q + core}
        )

    for a in range(5):
        for d in range(1, chips):
            own_copy(a, (chip + d) % chips).start()
    exchange_start(dqt, hq, hq_s, hq_r)
    exchange_start(finm, hm, hm_s, hm_r)

    def turn_block(b):
        turned[:, b * T : (b + 1) * T] = x_all[b].astype(F32).T.astype(BF)

    def turn_query(b):
        dq_b = dqt[b].astype(F32)
        dall[b * T : (b + 1) * T, 128:] = (
            jnp.concatenate([dq_b, jnp.zeros_like(dq_b)], axis=0).T.astype(BF)
        )

    def turn_encoder():
        enc_turned[...] = enc_all[...].reshape(8 * E, 512).astype(F32).T.astype(BF)

    def own_sum(a):
        for d in range(1, chips):
            q = (chip + d) % chips
            rcopy(sums[a].at[q], gots[a].at[q], b_s.at[a, q], b_r.at[a, q], {"shard": 2 * q + core}).wait_recv()
        total = sums[a][chip].astype(F32)
        for d in range(1, chips):
            total = total + gots[a][(chip + d) % chips].astype(F32)
        total = total.astype(BF)
        if a < 3:
            wz[a] = total
        elif a == 3:
            for c in range(4):
                wz[3 + c] = total[:, 512 * c : 512 * (c + 1)]
        else:
            for c in range(4):
                wz[7 + c] = total[c * R : (c + 1) * R]

    block = s * Z + z
    work = [functools.partial(turn_block, b) for b in range(8)]
    work += [functools.partial(turn_query, b) for b in range(8)] + [turn_encoder]

    for far in range(Z - 1, 0, -1):
        for slot in range(8):
            if work:
                work.pop(0)()
            for way in (0, 1):
                t = z + (2 * way - 1) * far

                @pl.when((z != ends[way]) & (t >= 0) & (t < Z))
                def _(way=way, t=t, slot=slot):
                    z_copy(way, t, slot, z_view(slot, t)).wait_recv()
                    buf = z_buffer(way, t, slot)
                    buf[...] = (
                        buf[...].astype(F32) + z_view(slot, t)[...].astype(F32)
                    ).astype(BF)
                    z_copy(way, t, slot, buf).start()

    def inward(k, step):
        way = (step + 1) // 2
        return rcopy(wz.at[k], zin.at[way, k], c_s.at[way, k], c_r.at[way, k], {"seq": z + step})

    def outward(k, step):
        return rcopy(zfin.at[k], zfin.at[k], f_s.at[(step + 1) // 2, k], f_r.at[k], {"seq": z + step})

    def root(k):
        return max(Z // 2 - 1 + k % 2, 0) if Z > 1 else 0

    def tips(k):
        r = root(k)
        for step in (-1, 1):
            tip = ends[(step + 1) // 2]
            if tip != r:

                @pl.when(z == tip)
                def _(step=step):
                    inward(k, step).start()

    def partial(k):
        r = root(k)
        for step, beyond in ((-1, z > r), (1, z < r)):
            tip = ends[(step + 1) // 2]
            way = (step + 1) // 2

            @pl.when(beyond & (z != tip))
            def _(step=step, way=way):
                inward(k, step).wait_recv()
                wz[k] = (wz[k].astype(F32) + zin[way, k].astype(F32)).astype(BF)
                inward(k, step).start()

    def total_of(k):
        r = root(k)

        @pl.when(z == r)
        def _():
            total = wz[k].astype(F32)
            if r < Z - 1:
                inward(k, -1).wait_recv()
                total = total + zin[0, k].astype(F32)
            if r > 0:
                inward(k, 1).wait_recv()
                total = total + zin[1, k].astype(F32)
            zfin[k] = total.astype(BF)
            if r < Z - 1:
                outward(k, 1).start()
            if r > 0:
                outward(k, -1).start()

    def send_out(k):
        r = root(k)
        for step, beyond in ((1, z > r), (-1, z < r)):
            tip = Z - 1 if step > 0 else 0

            @pl.when(beyond)
            def _(step=step, tip=tip):
                outward(k, step).wait_recv()

                @pl.when(z != tip)
                def _():
                    outward(k, step).start()

    for task in work:
        task()
    psend_q = mm(turned[...], dall[:, 128:])
    for a in range(5):
        own_sum(a)
        for k in ((0,), (1,), (2,), (3, 4, 5, 6), (7, 8, 9, 10))[a]:
            tips(k)
    hat, scale = norm_stats(embed(hid, bound, vecs, block))

    for slot in range(8):
        for way in (0, 1):

            @pl.when(z != ends[way])
            def _(way=way, slot=slot):
                z_copy(way, z, slot, z_view(slot, z)).wait_recv()

        low = jnp.where(z == ends[0], 0.0, z_buffer(0, z, slot)[...].astype(F32))
        high = jnp.where(z == ends[1], 0.0, z_buffer(1, z, slot)[...].astype(F32))
        total = (low + high + z_view(slot, z)[...].astype(F32)).astype(BF)
        fin[slot] = total
        dall[slot * T : (slot + 1) * T, :128] = total
    exchange_start(fin, hkv, hk_s, hk_r)
    for k in range(3):
        partial(k)

    psend_kv = mm(turned[...], dall[:, :128])
    psend[...] = jnp.concatenate([psend_kv, psend_q], axis=1).astype(BF).reshape(S, R, 256)
    msend[...] = mm(enc_turned[...], finm[...].reshape(8 * E, 128)).astype(BF).reshape(S, R, 128)
    pgot[s] = psend[s]
    mgot[s] = msend[s]
    for d in range(1, S):
        p = (s + d) % S
        rcopy(psend.at[p], pgot.at[s], p_s.at[d], p_r.at[s], {"shard": p}).start()
        rcopy(msend.at[p], mgot.at[s], pm_s.at[d], pm_r.at[s], {"shard": p}).start()

    for k in range(3):
        total_of(k)
    for k in range(3, 6):
        partial(k)

    exchange_recv(dqt, hq, hq_s, hq_r)
    exchange_recv(fin, hkv, hk_s, hk_r)
    exchange_recv(finm, hm, hm_s, hm_r)
    d_query = hq[...].reshape(512, T).astype(F32).T.astype(BF)
    d_keys = jnp.concatenate([hkv[h][:, :HD] for h in range(H)], axis=1)
    d_values = jnp.concatenate([hkv[h][:, HD:] for h in range(H)], axis=1)
    d_norm = (
        mm(d_query, wproj[:, :512], 1, 1)
        + mm(d_keys, wproj[:, 512:1024], 1, 1)
        + mm(d_values, wproj[:, 1024:], 1, 1)
    )
    d_value, d_gain, d_shift = norm_back(d_norm, hat, scale, vecs[2:3, :])
    total = d_after[...] + d_value
    hidden_grad[...] = total
    pos = block * T + lax.broadcasted_iota(jnp.int32, (T, 1), 0)
    sm_mine[...] = jnp.zeros((16, 512), F32)
    sm_mine[0:1, :] = d_gain
    sm_mine[1:2, :] = small2[0:1, :]
    sm_mine[2:3, :] = small3[0:1, :]
    sm_mine[3:4, :] = d_shift
    sm_mine[4:5, :] = small2[1:2, :]
    sm_mine[5:6, :] = small3[1:2, :]
    sm_mine[6:7, :] = jnp.sum(jnp.where(pos < bound, total, 0.0), axis=0, keepdims=True)
    sm_mine[7:8, :] = jnp.sum(jnp.where(pos < bound, 0.0, total), axis=0, keepdims=True)
    sm_mine[8:9, :] = small3[2:3, :]
    for c in range(upb_g.shape[1] // 512):
        sm_mine[9 + c : 10 + c, :] = upb_g[0:1, 512 * c : 512 * (c + 1)]
    for d in range(1, S):
        rcopy(sm_mine, sm_all.at[s], sm_s.at[d], sm_r.at[s], {"shard": (s + d) % S}).start()
    sm_all[s] = sm_mine[...]

    for k in range(6, 11):
        partial(k)
        total_of(k - 3)

    for d in range(1, S):
        p = (s + d) % S
        rcopy(psend.at[p], pgot.at[p], p_s.at[d], p_r.at[p], {"shard": p}).wait_recv()
        rcopy(msend.at[p], mgot.at[p], pm_s.at[d], pm_r.at[p], {"shard": p}).wait_recv()
    heads, mheads = [], []
    for h in range(H):
        acc, accm = pgot[h].astype(F32), mgot[h].astype(F32)
        for g in range(1, G):
            acc = acc + pgot[8 * g + h].astype(F32)
            accm = accm + mgot[8 * g + h].astype(F32)
        heads.append(acc)
        mheads.append(accm)
    wz[11] = jnp.concatenate([v[:, 128 : 128 + HD] for v in heads], axis=1).astype(BF)
    wz[12] = jnp.concatenate([v[:, :HD] for v in heads], axis=1).astype(BF)
    wz[13] = jnp.concatenate([v[:, HD:128] for v in heads], axis=1).astype(BF)
    wz[14] = jnp.concatenate([v[:, :HD] for v in mheads], axis=1).astype(BF)
    wz[15] = jnp.concatenate([v[:, HD:] for v in mheads], axis=1).astype(BF)
    for k in range(11, NC):
        tips(k)
    for k in range(8, 11):
        total_of(k)
    for k in range(6):
        send_out(k)
    for k in range(11, NC):
        partial(k)
    e_keys = jnp.concatenate([hm[h][:, :HD] for h in range(H)], axis=1)
    e_values = jnp.concatenate([hm[h][:, HD:] for h in range(H)], axis=1)
    encoder_grad[...] = mm(e_keys, wmem[:, :512], 1, 1) + mm(e_values, wmem[:, 512:], 1, 1)

    for d in range(1, S):
        p = (s + d) % S
        rcopy(sm_mine, sm_all.at[p], sm_s.at[d], sm_r.at[p], {"shard": p}).wait_recv()
    acc = sm_all[0]
    for p in range(1, S):
        acc = acc + sm_all[p]
    sm_plane[...] = acc
    for d in range(1, Z):
        rcopy(sm_plane, sm_z.at[z], sz_s.at[d], sz_r.at[z], {"seq": (z + d) % Z}).start()
    sm_z[z] = acc
    for k in range(11, NC):
        total_of(k)
        send_out(k - 5)
    for k in range(11, NC):
        send_out(k)
    for d in range(1, Z):
        o = (z + d) % Z
        rcopy(sm_plane, sm_z.at[o], sz_s.at[d], sz_r.at[o], {"seq": o}).wait_recv()
    acc = sm_z[0]
    for o in range(1, Z):
        acc = acc + sm_z[o]
    smalls_o[...] = acc

    for a in range(5):
        for d in range(1, chips):
            own_copy(a, (chip + d) % chips).wait_send()
    for d in range(1, G):
        o = (m + d) % G
        rcopy(dkv.at[o], mbuf.at[m], mb_s.at[d, 0], mb_r.at[m, 0], {"shard": o * 8 + j}).wait_send()
    exchange_sent(dqt, hq, hq_s, hq_r)
    exchange_sent(fin, hkv, hk_s, hk_r)
    exchange_sent(finm, hm, hm_s, hm_r)
    for far in range(Z - 1, 0, -1):
        for slot in range(8):
            for way in (0, 1):
                t = z + (2 * way - 1) * far

                @pl.when((t >= 0) & (t < Z))
                def _(way=way, t=t, slot=slot):
                    z_copy(way, t, slot, z_view(slot, t)).wait_send()

    for d in range(1, S):
        p = (s + d) % S
        rcopy(psend.at[p], pgot.at[s], p_s.at[d], p_r.at[s], {"shard": p}).wait_send()
        rcopy(msend.at[p], mgot.at[s], pm_s.at[d], pm_r.at[s], {"shard": p}).wait_send()
        rcopy(sm_mine, sm_all.at[s], sm_s.at[d], sm_r.at[s], {"shard": p}).wait_send()
    for d in range(1, Z):
        rcopy(sm_plane, sm_z.at[z], sz_s.at[d], sz_r.at[z], {"seq": (z + d) % Z}).wait_send()
    for k in range(NC):
        r = root(k)
        for step, beyond in ((-1, z > r), (1, z < r)):

            @pl.when(beyond)
            def _(step=step):
                inward(k, step).wait_send()

        for step in (-1, 1):
            sends = (z >= r) & (z < Z - 1) if step > 0 else (z <= r) & (z > 0)

            @pl.when(sends)
            def _(step=step):
                outward(k, step).wait_send()


def finish_kernel(
    info, timestep, zfin, sums, hid_g, enc_g, lay,
    lay_o, hid_o, enc_o, time_o, gain_o, shift_o, proj_o, out_o, cq_o, mem_o, co_o, up_o, upb_o, dn_o, dnb_o,
):
    s = info[3]
    R, F = out_o.shape[0], upb_o.shape[1]
    lay_o[...] = lay[...]
    hid_o[...] = hid_g[...]
    enc_o[...] = enc_g[...]
    out_o[...] = zfin[0].astype(F32)
    cq_o[...] = zfin[1].astype(F32)
    co_o[...] = zfin[2].astype(F32)
    for c in range(4):
        up_o[:, 512 * c : 512 * (c + 1)] = zfin[3 + c].astype(F32)
        dn_o[c * R : (c + 1) * R, :] = zfin[7 + c].astype(F32)
    for c in range(3):
        proj_o[:, 512 * c : 512 * (c + 1)] = zfin[11 + c].astype(F32)
    for c in range(2):
        mem_o[:, 512 * c : 512 * (c + 1)] = zfin[14 + c].astype(F32)

    def own(width, first):
        row = lax.broadcasted_iota(jnp.int32, (512, width), 0)
        col = lax.broadcasted_iota(jnp.int32, (512, width), 1)
        pick = jnp.where(row == col + first, 1.0, 0.0)
        return lax.dot_general(
            sums[...], pick, (((1,), (0,)), ((), ())),
            preferred_element_type=F32, precision=lax.Precision.HIGHEST,
        )

    mine = own(R, s * R)
    gain_o[...] = mine[0:3]
    shift_o[...] = mine[3:6]
    dnb_o[...] = mine[8:9]
    step = lax.broadcasted_iota(jnp.int32, time_o.shape, 0)
    grad = jnp.zeros(time_o.shape, F32)
    for d in range(DOCS):
        grad = grad + jnp.where(step == timestep[d], mine[6 + d : 7 + d], 0.0)
    time_o[...] = grad
    wide = own(F, (s * F) % 512)
    row = lax.broadcasted_iota(jnp.int32, wide.shape, 0)
    upb_o[...] = jnp.sum(jnp.where(row == 9 + s * F // 512, wide, 0.0), axis=0, keepdims=True)


def last(v):
    S, Z, G = v["S"], v["Z"], v["G"]
    T, R, F, E = v["T"], v["R"], v["F"], v["encoder"].shape[0]
    FF = v["wup"].shape[1]
    chips = S // 2
    sds = jax.ShapeDtypeStruct
    V = pltpu.VMEM
    GM, ZM = (G, Z) if G > 1 else (1, 1)
    hidden_grad, encoder_grad, zfin, sums = remote_call(
        functools.partial(last_kernel, S, Z, G),
        "gradients_home",
        4,
        (
            v["info"], v["hidden_in"], v["vecs"], v["d_after"], v["x_all"], v["enc_all"], v["dqt"],
            v["dkv"].reshape(G, 8, Z, T, 128), v["dmem"],
            v["gproj"].reshape(512, 1536), v["gmem"].reshape(512, 1024),
            v["wout_grad"], v["cq_grad"], v["co_grad"], v["up_grad"], v["dn_grad"],
            v["small2"], v["small3"], v["upb_grad"],
        ),
        [sds((T, 512), F32), sds((E, 512), F32), sds((NC, R, 512), BF), sds((16, 512), F32)],
        [V((chips, R, 512), BF)] * 3 + [V((chips, R, FF), BF), V((chips, F, 512), BF)]
        + [
            V((2, Z, 8, T, 128), BF), V((8, T, 128), BF), V((GM, 8, ZM, T, 128), BF),
            V((8, T, 128), BF), V((8, HD, T), BF), V((8, E, 128), BF),
            V((512, 8 * T), BF), V((512, 8 * E), BF), V((8 * T, 256), BF),
            V((S, R, 256), BF), V((S, R, 256), BF), V((S, R, 128), BF), V((S, R, 128), BF),
            V((NC, R, 512), BF), V((2, NC, R, 512), BF),
            V((S, 16, 512), F32), V((Z, 16, 512), F32), V((16, 512), F32), V((16, 512), F32),
            DMA((5, chips)), DMA((5, chips)),
            DMA((2, Z, 8)), DMA((2, Z, 8)), DMA((G, 1)), DMA((G, 1)),
            DMA((8,)), DMA((8,)), DMA((8,)), DMA((8,)), DMA((8,)), DMA((8,)),
            DMA((S,)), DMA((S,)), DMA((S,)), DMA((S,)),
            DMA((2, NC)), DMA((2, NC)), DMA((2, NC)), DMA((NC,)),
            DMA((S,)), DMA((S,)), DMA((Z,)), DMA((Z,)),
        ],
        far=(7,) if G > 1 else (),
    )
    vmem = pl.BlockSpec(memory_space=pltpu.VMEM)
    smem = pl.BlockSpec(memory_space=pltpu.SMEM)
    steps = v["time_table"].shape[0]
    outs = [
        sds((T, 512), BF), sds((T, 512), F32), sds((E, 512), F32), sds((steps, R), F32), sds((3, R), F32),
        sds((3, R), F32), sds((R, 1536), F32), sds((R, 512), F32), sds((R, 512), F32), sds((R, 1024), F32),
        sds((R, 512), F32), sds((R, FF), F32), sds((1, F), F32), sds((F, 512), F32), sds((1, R), F32),
    ]
    res = pl.pallas_call(
        finish_kernel,
        out_shape=outs,
        in_specs=[smem, smem] + [vmem] * 5,
        out_specs=[vmem] * len(outs),
        compiler_params=pltpu.CompilerParams(vmem_limit_bytes=room()),
        name="outputs",
    )(v["info"], v["timestep"], zfin, sums, hidden_grad, encoder_grad, v["layer_out"])
    res = list(res)
    res[12] = res[12].reshape(F)
    res[14] = res[14].reshape(R)
    return tuple(res)


def shards(
    hidden_in, encoder, segment_ids, timestep, out_grad, time_table, norm_gain, norm_bias,
    self_proj, self_out, cross_query, cross_memory, cross_out, up_weight, up_bias, down_weight, down_bias,
):
    S, Z = lax.axis_size("shard"), lax.axis_size("seq")
    T, R, F = hidden_in.shape[0], self_proj.shape[0], up_bias.shape[0]
    G = S // 8
    info, x_all, kv, qt, mem, enc_all, vecs, upb, gout, gcq, gco, gup, gdn = gather_call(
        S,
        Z,
        (
            timestep, segment_ids.reshape(-1, 128), hidden_in, time_table, norm_gain, norm_bias,
            up_bias, down_bias, self_proj, cross_memory, encoder,
            self_out, cross_query, cross_out, up_weight, down_weight,
        ),
    )
    wout, wcq, wco = gout.reshape(512, 512), gcq.reshape(512, 512), gco.reshape(512, 512)
    wup, wdn = gup.reshape(512, -1), gdn.reshape(-1, 512)
    kv = kv.reshape(S * Z, T, 128)

    ot, of, lse = attend(Z, True, info, qt, kv)
    at, after, n2, cqt, mkv = middle(G, Z, info, ot, hidden_in, vecs, wout, wcq, mem)
    mkv = mkv.reshape(DOCS * ENC // T, T, 128)
    crt, crf, clse = attend(Z, False, info, cqt, mkv)
    layer_out, d_after2, co_grad, up_grad, dn_grad, small3, upb_grad, dct, gproj, gmem = feed(
        crt, after, vecs, upb, wco, wup, wdn, out_grad, self_proj, cross_memory
    )
    dcqt, dmkv = attend_back(Z, False, info, cqt, mkv, dct, crf, clse)
    d_after, cq_grad, wout_grad, small2, dat, dmem = middle_back(
        dcqt, after, d_after2, n2, at, vecs, wcq, wout, dmkv.reshape(G, 8, Z, -1, 128)
    )
    dqt, dkv = attend_back(Z, True, info, qt, kv, dat, of, lse)
    return last(locals())


def solution(mesh):
    return jax.shard_map(
        shards,
        mesh=mesh,
        in_specs=(
            P(("shard", "seq"), None),
            P(("shard", "seq"), None),
            P(),
            P(),
            P(("shard", "seq"), None),
            P(None, "shard"),
            P(None, "shard"),
            P(None, "shard"),
            P("shard", None),
            P("shard", None),
            P("shard", None),
            P("shard", None),
            P("shard", None),
            P("shard", None),
            P("shard"),
            P("shard", None),
            P("shard"),
        ),
        out_specs=(
            P(("shard", "seq"), None),
            P(("shard", "seq"), None),
            P(("shard", "seq"), None),
            P(None, "shard"),
            P(None, "shard"),
            P(None, "shard"),
            P("shard", None),
            P("shard", None),
            P("shard", None),
            P("shard", None),
            P("shard", None),
            P("shard", None),
            P("shard"),
            P("shard", None),
            P("shard"),
        ),
        check_vma=False,
    )
```

```python
import functools

import jax
import jax.numpy as jnp
from jax import lax
from jax.experimental import pallas as pl
from jax.experimental.pallas import tpu as pltpu
from jax.sharding import PartitionSpec as P

H = 8
HD = 64
DOCS = 2
ENC = 1024
EPS = 1e-05
MASKED = -1e30
SCALE = HD**-0.5
MESH = pl.DeviceIdType.MESH
BF = jnp.bfloat16
F32 = jnp.float32
DMA = pltpu.SemaphoreType.DMA


def room(small=True):
    return (ROOM << 20) if small and lax.axis_size("shard") == 8 else (63 << 20)


ROOM = 30
ORDER = (0, 1, 2, 4, 3, 6, 5, 7)


def mm(a, b, ca=1, cb=0):
    return lax.dot_general(a, b, (((ca,), (cb,)), ((), ())), preferred_element_type=F32)


def flip(j, bits):
    low, mid, high = j % 2, (j // 2) % 2, (j // 4) % 2
    out = j
    if bits & 1:
        out = out + 1 - 2 * low
    if bits & 2:
        out = out + 2 - 4 * mid
    if bits & 4:
        out = out + 4 - 8 * high
    return out


def rcopy(src, dst, send_sem, recv_sem, device_id):
    return pltpu.make_async_remote_copy(
        src_ref=src,
        dst_ref=dst,
        send_sem=send_sem,
        recv_sem=recv_sem,
        device_id=device_id,
        device_id_type=MESH,
    )


def place():
    shard, seq = lax.axis_index("shard"), lax.axis_index("seq")
    return shard, seq, shard % 8, shard // 8


def greet(peers):
    barrier = pltpu.get_barrier_semaphore()
    count = 0
    for condition, device in peers:
        if condition is None:
            pl.semaphore_signal(barrier, inc=1, device_id=device, device_id_type=MESH)
            count = count + 1
        else:

            @pl.when(condition)
            def _(device=device):
                pl.semaphore_signal(barrier, inc=1, device_id=device, device_id_type=MESH)

            count = count + jnp.where(condition, 1, 0)
    pl.semaphore_wait(barrier, count)


def norm_stats(value):
    center = jnp.mean(value, axis=1, keepdims=True)
    offset = value - center
    spread = jnp.mean(offset * offset, axis=1, keepdims=True)
    scale = lax.rsqrt(spread + EPS)
    return offset * scale, scale


def norm_back(d_out, hat, scale, gain):
    d_hat = d_out * gain
    first = jnp.mean(d_hat, axis=1, keepdims=True)
    second = jnp.mean(d_hat * hat, axis=1, keepdims=True)
    d_in = scale * (d_hat - first - hat * second)
    return d_in, jnp.sum(d_out * hat, axis=0, keepdims=True), jnp.sum(d_out, axis=0, keepdims=True)


def embed(hid_ref, bound, vecs_ref, block):
    rows = hid_ref.shape[0]
    pos = block * rows + lax.broadcasted_iota(jnp.int32, (rows, 1), 0)
    picked = jnp.where(pos < bound, vecs_ref[0:1, :], vecs_ref[1:2, :])
    return hid_ref[...].astype(F32) + picked


class Whole:
    def __init__(self, pairs, S, sems):
        self.pairs, self.S = pairs, S
        self.local, self.send, self.recv, self.half, self.pass_on = sems
        self.s = lax.axis_index("shard")
        self.core, self.chip = self.s % 2, self.s // 2
        self.sib = flip(self.s, 1)
        self.near = S == 8
        self.flow = []

    @staticmethod
    def scratch(count, S):
        return [DMA((count,)), DMA((count, max(8, S // 2))), DMA((count, S)), DMA((count, 2)), DMA((count, S // 2))]

    def copy(self, a, source, n, to, half=None):
        shard, whole = self.pairs[a]
        target = whole.at[source]
        if half is not None:
            rows = shard.shape[0] // 2
            target = whole.at[source, pl.ds(half * rows, rows)]
            recv = self.half.at[a, half]
        else:
            recv = self.recv.at[a, source]
        origin = shard if n < 0 else target
        send = self.send.at[a, -n - 1 if n < 0 else n]
        return rcopy(origin, target, send, recv, {"shard": to})

    def go(self, *args):
        c = self.copy(*args)
        c.start()
        self.flow.append(c)

    def arrived(self, a, source, half=None):
        self.copy(a, source, 7, self.sib, half).wait_recv()

    def same_core(self, d):
        return ((self.chip + d) % (self.S // 2)) * 2 + self.core

    def start(self, a):
        shard, whole = self.pairs[a]
        pltpu.make_async_copy(shard, whole.at[self.s], self.local.at[a]).start()
        s = self.s
        if self.near:
            self.go(a, s, -1, flip(s, 2))
            self.go(a, s, -2, flip(s, 4))
            self.go(a, s, -3, self.sib)
            return
        for d in range(1, self.S // 2):
            c = rcopy(shard, whole.at[s], self.send.at[a, d], self.recv.at[a, s], {"shard": self.same_core(d)})
            c.start()
            self.flow.append(c)
        c = rcopy(shard, whole.at[s], self.send.at[a, 0], self.recv.at[a, s], {"shard": self.sib})
        c.start()
        self.flow.append(c)

    def relay(self, a):
        if not self.near:
            return
        x, y = flip(self.s, 2), flip(self.s, 4)
        self.arrived(a, x)
        self.go(a, x, 3, y, 0)
        self.go(a, x, 5, self.sib)
        self.arrived(a, y)
        self.go(a, y, 4, x, 1)
        self.go(a, y, 6, self.sib)

    def finish(self, a):
        if self.near:
            far = flip(self.s, 6)
            self.arrived(a, far, 0)
            self.arrived(a, far, 1)
            self.go(a, far, 7, self.sib)
            return
        _, whole = self.pairs[a]
        for d in range(1, self.S // 2):
            q = self.same_core(self.S // 2 - d)
            self.arrived(a, q)
            c = rcopy(whole.at[q], whole.at[q], self.pass_on.at[a, d], self.recv.at[a, q], {"shard": self.sib})
            c.start()
            self.flow.append(c)

    def wait(self, a):
        shard, whole = self.pairs[a]
        self.arrived(a, self.sib)
        for d in range(1, self.S // 2):
            self.arrived(a, flip(self.same_core(d), 1))
        pltpu.make_async_copy(shard, whole.at[self.s], self.local.at[a]).wait()

    def drain(self):
        for c in self.flow:
            c.wait_send()


def gather_kernel(
    S, Z, G,
    timestep, seg_h, hid_h, table_h, gain_h, shift_h, upb_h, dnb_h, wproj_h, wmem_h, enc_h,
    wout, wcq, wco, wup, wdn,
    info, x_all, kv, qt, mkv, enc_all, vecs, upb_row, gout, gcq, gco, gup, gdn,
    seg, hid, table, gain, shift, upb, dnb, wproj, wmem, enc, in_sem,
    rows_f, small, small_all, wsend, msend, w_all, m_all, sm_s, sm_r, w_s, w_r, mw_s, mw_r,
    x_s, x_r, e_s, e_r, z_s, z_r, mb_s, mb_r, *whole_sems
):
    s, z, j, m = place()
    near = (seg, hid, table, gain, shift, upb, dnb, wproj, wmem, enc)
    far = (seg_h, hid_h, table_h, gain_h, shift_h, upb_h, dnb_h, wproj_h, wmem_h, enc_h)
    loads = [pltpu.make_async_copy(b, a, in_sem.at[n]) for n, (a, b) in enumerate(zip(near, far))]
    for c in loads:
        c.start()
    for c in loads:
        c.wait()
    R, F = wproj.shape[0], upb.shape[0]
    T, E = hid.shape[0], enc.shape[0]
    sib = flip(s, 1)

    step = lax.broadcasted_iota(jnp.int32, table.shape, 0)
    rows_f[...] = jnp.zeros((16, 256), F32)
    for d in range(DOCS):
        picked = jnp.where(step == timestep[d], table[...].astype(F32), 0.0)
        rows_f[d : d + 1, :R] = jnp.sum(picked, axis=0, keepdims=True)
    rows_f[2:5, :R] = gain[...].astype(F32)
    rows_f[5:8, :R] = shift[...].astype(F32)
    rows_f[8:9, :F] = upb[...].astype(F32).reshape(1, F)
    rows_f[9:10, :R] = dnb[...].astype(F32).reshape(1, R)
    small[...] = rows_f[...].astype(BF)
    small_all[s] = small[...]
    bound = jnp.sum(jnp.where(seg[...] == 0, 1.0, 0.0)).astype(jnp.int32)
    info[0] = bound
    info[1] = m
    info[2] = z
    info[3] = s

    greet(
        [(None, {"shard": (s + d) % S}) for d in range(1, S)]
        + [(z > 0, {"seq": z - 1}), (z < Z - 1, {"seq": z + 1})]
    )
    small_copies = []
    for d in range(1, S):
        c = rcopy(small, small_all.at[s], sm_s.at[d], sm_r.at[s], {"shard": (s + d) % S})
        c.start()
        small_copies.append(c)
    for h in range(H):
        k = wproj[:, 512 + HD * h : 512 + HD * (h + 1)]
        v = wproj[:, 1024 + HD * h : 1024 + HD * (h + 1)]
        q = wproj[:, HD * h : HD * (h + 1)]
        wsend[h] = jnp.concatenate([k, v, q, jnp.zeros_like(q)], axis=1)
        msend[h] = jnp.concatenate(
            [wmem[:, HD * h : HD * (h + 1)], wmem[:, 512 + HD * h : 512 + HD * (h + 1)]], axis=1
        )
    w_all[s] = wsend[j]
    m_all[s] = msend[j]
    w_copies = []
    for d in range(1, S):
        p = (s + d) % S
        c = rcopy(wsend.at[p % 8], w_all.at[s], w_s.at[d], w_r.at[s], {"shard": p})
        c.start()
        w_copies.append(c)
        c = rcopy(msend.at[p % 8], m_all.at[s], mw_s.at[d], mw_r.at[s], {"shard": p})
        c.start()
        w_copies.append(c)
    for d in range(1, S):
        p = (s + d) % S
        rcopy(small, small_all.at[p], sm_s.at[d], sm_r.at[p], {"shard": p}).wait_recv()
    rows = jnp.zeros((16, 512), F32)
    lane = lax.broadcasted_iota(jnp.int32, (256, 512), 0)
    col = lax.broadcasted_iota(jnp.int32, (256, 512), 1)
    for p in range(S):
        pick = ((col - p * R) == lane) & (lane < R)
        rows = rows + mm(small_all[p], jnp.where(pick, 1.0, 0.0).astype(BF))
        upb_row[0:1, p * F : (p + 1) * F] = small_all[p].astype(F32)[8:9, :F]
    vecs[...] = rows

    hat, _ = norm_stats(embed(hid, bound, vecs, s * Z + z))
    x_all[j] = (hat * vecs[2:3, :] + vecs[5:6, :]).astype(BF)
    enc_all[j] = enc[...]
    copies = []

    def send_block(ref, bits_source, bits_target, send, recv):
        source = flip(j, bits_source)
        c = rcopy(ref.at[source], ref.at[source], send, recv.at[source], {"shard": flip(s, bits_target)})
        c.start()
        copies.append(c)

    def wait_block(ref, bits, recv):
        source = flip(j, bits)
        rcopy(ref.at[source], ref.at[source], x_s.at[0], recv.at[source], {"shard": sib}).wait_recv()

    for n, bits in enumerate((1, 2, 4, 6)):
        send_block(x_all, 0, bits, x_s.at[n], x_r)
    for n, bits in enumerate((1, 2, 4, 6)):
        send_block(enc_all, 0, bits, e_s.at[n], e_r)
    whole = Whole(
        ((wout, gout), (wcq, gcq), (wco, gco), (wup, gup), (wdn, gdn)), S, whole_sems
    )
    for d in range(1, S):
        p = (s + d) % S
        rcopy(wsend.at[0], w_all.at[p], w_s.at[d], w_r.at[p], {"shard": p}).wait_recv()
        rcopy(msend.at[0], m_all.at[p], mw_s.at[d], mw_r.at[p], {"shard": p}).wait_recv()
    w_head = w_all[...].reshape(S * R, 256)
    m_head = m_all[...].reshape(S * R, 128)

    def z_copy(ref, block, plane, step, hop, slot):
        view = ref.at[:, block, plane] if block is not None else ref.at[:, :, plane]
        way = (step + 1) // 2
        return rcopy(view, view, z_s.at[way, hop, slot], z_r.at[way, hop, slot], {"seq": z + step})

    def z_passes(step, hop):
        origin = z - step * hop
        return (z + step >= 0) & (z + step < Z) & (origin >= 0) & (origin < Z)

    def z_send(ref, block, hop, slot):
        for step in (-1, 1):

            @pl.when(z_passes(step, hop))
            def _(step=step):
                z_copy(ref, block, z - step * hop, step, hop, slot).start()

    def z_recv(ref, block, hop, slot):
        for step in (-1, 1):
            origin = z - step * hop

            @pl.when((origin >= 0) & (origin < Z))
            def _(step=step, origin=origin):
                z_copy(ref, block, origin, step, hop - 1, slot).wait_recv()

    def z_drain(ref, block, hop, slot):
        for step in (-1, 1):

            @pl.when(z_passes(step, hop))
            def _(step=step):
                z_copy(ref, block, z - step * hop, step, hop, slot).wait_send()

    def member_copy(ref, block, d, slot, mine):
        other = (m + d) % G
        at = m if mine else other
        view = ref.at[at, block, z] if block is not None else ref.at[at, :, z]
        return rcopy(view, view, mb_s.at[d, slot], mb_r.at[at, slot], {"shard": other * 8 + j})

    def spread(ref, block, slot):
        for d in range(1, G):
            member_copy(ref, block, d, slot, True).start()
        for d in range(1, G):
            member_copy(ref, block, d, slot, False).wait_recv()
        z_send(ref, block, 0, slot)

    def block_step(n):
        bits = ORDER[n]
        block = flip(j, bits)
        if bits:
            wait_block(x_all, bits, x_r)
            if bits in (2, 4, 6):
                send_block(x_all, bits, 1, x_s.at[3 + bits // 2], x_r)
        kvq = mm(x_all[block], w_head)
        kv[m, block, z] = kvq[:, :128].astype(BF)
        spread(kv, block, n)
        qt[block] = (SCALE * kvq[:, 128:256].T[:HD]).astype(BF)

    def encoder_step():
        for bits in (2, 4, 6):
            wait_block(enc_all, bits, e_r)
            send_block(enc_all, bits, 1, e_s.at[3 + bits // 2], e_r)
        for bits in (1, 3, 5, 7):
            wait_block(enc_all, bits, e_r)
        for b in range(8):
            mkv[b] = mm(enc_all[b], m_head).astype(BF)

    lag = 3
    last_step = max(8, 7 + lag * (Z - 1))
    for n in range(last_step + 1):
        if n < 8:
            block_step(n)
        if n == 8:
            encoder_step()
        if n == 3:
            for a in range(5):
                whole.start(a)
        for hop in range(1, Z):
            slot = n - lag * hop
            if 0 <= slot < 8:
                z_recv(kv, flip(j, ORDER[slot]), hop, slot)
                z_send(kv, flip(j, ORDER[slot]), hop, slot)
        if n == 8:
            for a in range(3):
                whole.relay(a)
        if n == min(10, last_step):
            whole.relay(3)
        if n == min(11, last_step):
            whole.relay(4)
        if n == min(12, last_step):
            for a in range(3):
                whole.finish(a)
    for a in range(3, 5):
        whole.finish(a)
    for a in range(5):
        whole.wait(a)
    whole.drain()
    for c in small_copies + w_copies + copies:
        c.wait_send()
    for n, bits in enumerate(ORDER):
        for d in range(1, G):
            member_copy(kv, flip(j, bits), d, n, True).wait_send()
        for hop in range(Z - 1):
            z_drain(kv, flip(j, bits), hop, n)


def gather_call(S, Z, args):
    G = S // 8
    (timestep, seg, hid, table, gain, shift, upb, dnb, wproj, wmem, enc, *weights) = args
    T, R, E, F = hid.shape[0], wproj.shape[0], enc.shape[0], upb.shape[0]
    vmem = pl.BlockSpec(memory_space=pltpu.VMEM)
    smem = pl.BlockSpec(memory_space=pltpu.SMEM)
    hbm = pl.BlockSpec(memory_space=pl.ANY)
    sds = jax.ShapeDtypeStruct
    outs = [
        sds((4,), jnp.int32),
        sds((8, T, 512), BF),
        sds((G, 8, Z, T, 128), BF),
        sds((8, HD, T), BF),
        sds((8, E, 128), BF),
        sds((8, E, 512), BF),
        sds((16, 512), F32),
        sds((1, S * F), F32),
    ] + [sds((S,) + w.shape, BF) for w in weights]
    return pl.pallas_call(
        functools.partial(gather_kernel, S, Z, G),
        out_shape=outs,
        in_specs=[smem] + [pl.BlockSpec(memory_space=pltpu.HBM)] * (len(args) - 1),
        out_specs=[smem] + [vmem] * 7 + [hbm] * 5,
        scratch_shapes=[pltpu.VMEM(a.shape, a.dtype) for a in args[1:11]]
        + [
            DMA((10,)),
            pltpu.VMEM((16, 256), F32),
            pltpu.VMEM((16, 256), BF),
            pltpu.VMEM((S, 16, 256), BF),
            pltpu.VMEM((8, R, 256), BF),
            pltpu.VMEM((8, R, 128), BF),
            pltpu.VMEM((S, R, 256), BF),
            pltpu.VMEM((S, R, 128), BF),
            DMA((S,)), DMA((S,)), DMA((S,)), DMA((S,)), DMA((S,)), DMA((S,)),
            DMA((8,)), DMA((8,)), DMA((8,)), DMA((8,)),
            DMA((2, Z, 9)), DMA((2, Z, 9)),
            DMA((G, 9)), DMA((G, 9)),
        ] + Whole.scratch(5, S),
        compiler_params=pltpu.CompilerParams(
            collective_id=0, has_side_effects=True, vmem_limit_bytes=room()
        ),
        name="gather_qkv",
    )(args[0], *[pltpu.with_memory_space_constraint(a, pltpu.HBM) for a in args[1:]])


GROUP = 4


class Reach:
    def __init__(self, causal, bound, block, rows):
        self.causal, self.bound, self.rows = causal, bound, rows
        self.query_first = block * rows
        last = self.query_first + rows - 1
        mixed = (self.query_first < bound) & (last >= bound)
        if causal:
            self.least = jnp.where(self.query_first < bound, 0, bound)
            begin, self.end = self.least // rows, block + 1
            self.mixed = mixed | (self.end < GROUP)
        else:
            per = ENC // rows
            self.least = 0
            begin = jnp.where(self.query_first < bound, 0, per)
            self.end = jnp.where(last < bound, per, 2 * per)
            self.mixed = mixed
        self.groups = (self.end - begin + GROUP - 1) // GROUP

    def mask(self, kind, start, limit, n, scores):
        if kind == "plain":
            return scores
        rows = self.rows
        key = (start + n) * rows + lax.broadcasted_iota(jnp.int32, (rows, 1), 0)
        query = self.query_first + lax.broadcasted_iota(jnp.int32, (1, scores.shape[1]), 1)
        if kind == "edge":
            allowed = (key >= self.least) & (key < limit)
            if n == GROUP - 1:
                allowed = allowed & (key <= query)
        elif self.causal:
            least = jnp.where(query < self.bound, 0, self.bound)
            allowed = (key < limit) & (key <= query) & (key >= least)
        else:
            allowed = jnp.where(query < self.bound, 0, 1) == key // ENC
        return jnp.where(allowed, scores, MASKED)

    def walk(self, group, state):
        def turn(kind, g, carry):
            if kind == "edge":
                g = jnp.where(g == 0, 0, self.groups - 1)
            stop = self.end - GROUP * (self.groups - 1 - g)
            return group(kind, jnp.maximum(stop - GROUP, 0), stop * self.rows, carry)

        mixed, groups = self.mixed, self.groups
        state = lax.fori_loop(
            0, jnp.where(mixed, groups, 0), functools.partial(turn, "full"), state
        )
        if not self.causal:
            return lax.fori_loop(
                0, jnp.where(mixed, 0, groups), functools.partial(turn, "plain"), state
            )
        state = lax.fori_loop(
            0,
            jnp.where(mixed, 0, jnp.minimum(groups, 2)),
            functools.partial(turn, "edge"),
            state,
        )
        return lax.fori_loop(
            1, jnp.where(mixed, 1, groups - 1), functools.partial(turn, "plain"), state
        )


def turned_keys(kv, kt, half, begin, end):
    rows = kv.shape[1]

    def turn(kb, carry):
        flat = kv[kb].astype(F32).T[HD * half : HD * (half + 1)].astype(BF)
        kt[:, pl.ds(pl.multiple_of(kb * rows, rows), rows)] = flat
        return carry

    lax.fori_loop(begin, end, turn, 0)


def key_span(causal, bound, low, Z, rows, count):
    if not causal:
        return 0, count
    return jnp.where(low * rows < bound, 0, bound) // rows, low + 7 * Z + 1


def attend_kernel(Z, causal, info, qt, kv, ot, of, lse, vt):
    bound, m, z = info[0], info[1], info[2]
    count, T = kv.shape[0], kv.shape[1]
    low = 8 * m * Z + z

    begin, end = key_span(causal, bound, low, Z, T, count)
    turned_keys(kv, vt, 1, jnp.maximum(begin - GROUP, 0), end)

    def one_block(i, carry):
        reach = Reach(causal, bound, low + i * Z, T)
        queries = jnp.concatenate([qt[i], jnp.zeros((HD, T), BF)], axis=0)

        def group(kind, start, limit, state):
            top, total, acc = state
            half = GROUP // 2
            raws = [
                mm(kv[pl.ds(start + half * h, half)].reshape(half * T, 128), queries) for h in range(2)
            ]
            for h, raw in enumerate(raws):
                scores = [
                    reach.mask(kind, start, limit, half * h + n, raw[n * T : (n + 1) * T])
                    for n in range(half)
                ]
                new_top = top
                for piece in scores:
                    new_top = jnp.maximum(new_top, jnp.max(piece, axis=0, keepdims=True))
                fade = jnp.exp(top - new_top)
                total = total * fade
                parts = []
                for piece in scores:
                    powers = jnp.exp(piece - new_top)
                    total = total + jnp.sum(powers, axis=0, keepdims=True)
                    parts.append(powers.astype(BF))
                values = vt[:, pl.ds(pl.multiple_of((start + half * h) * T, T), half * T)]
                acc = acc * fade + mm(values, jnp.concatenate(parts, axis=0))
                top = new_top
            return top, total, acc

        top, total, acc = reach.walk(
            group,
            (jnp.full((1, T), MASKED, F32), jnp.zeros((1, T), F32), jnp.zeros((HD, T), F32)),
        )
        result = acc / total
        ot[i] = result.astype(BF)
        of[i] = result
        lse[i] = top + jnp.log(total)
        return carry

    lax.fori_loop(0, 8, one_block, 0)


def attend(Z, causal, info, qt, kv):
    T = qt.shape[2]
    sds = jax.ShapeDtypeStruct
    vmem = pl.BlockSpec(memory_space=pltpu.VMEM)
    return pl.pallas_call(
        functools.partial(attend_kernel, Z, causal),
        out_shape=[sds((8, HD, T), BF), sds((8, HD, T), F32), sds((8, 1, T), F32)],
        in_specs=[pl.BlockSpec(memory_space=pltpu.SMEM), vmem, vmem],
        out_specs=[vmem] * 3,
        scratch_shapes=[pltpu.VMEM((HD, kv.shape[0] * T), BF)],
        compiler_params=pltpu.CompilerParams(vmem_limit_bytes=room()),
        name="attend_self" if causal else "attend_cross",
    )(info, qt, kv)


def attend_back_kernel(
    Z, causal, info, qt, kv, dt, of, lse, dq, dkv, kt, dkvf, qd, rows, raw, pair, stage, sem
):
    bound, m, z = info[0], info[1], info[2]
    count, T = kv.shape[0], kv.shape[1]
    low = 8 * m * Z + z
    zero = jnp.zeros((HD, T), BF)

    def clear(kb, carry):
        dkvf[kb] = jnp.zeros((T, 128), F32)
        return carry

    lax.fori_loop(0, count, clear, 0)

    begin, end = key_span(causal, bound, low, Z, T, count)
    turned_keys(kv, kt, 0, jnp.maximum(begin - GROUP, 0), end)

    def one_block(i, carry):
        reach = Reach(causal, bound, low + i * Z, T)
        qd[:HD, :T] = qt[i]
        qd[HD:, :T] = zero
        qd[:HD, T:] = zero
        qd[HD:, T:] = dt[i]
        both = jnp.concatenate([qt[i].astype(F32), dt[i].astype(F32)], axis=0).T
        lane = lax.broadcasted_iota(jnp.int32, both.shape, 1)
        rows[:T] = jnp.where(lane < HD, 0.0, both).astype(BF)
        rows[T:] = jnp.where(lane < HD, both, 0.0).astype(BF)
        delta = jnp.sum(dt[i].astype(F32) * of[i], axis=0, keepdims=True)
        level = lse[i]

        def group(kind, start, limit, acc):
            for n in range(GROUP):
                raw[n * T : (n + 1) * T] = mm(kv[start + n], qd[...])
            for n in range(GROUP):
                at = slice(n * T, (n + 1) * T)
                probs = jnp.exp(reach.mask(kind, start, limit, n, raw[at, :T]) - level)
                pair[at, :T] = probs.astype(BF)
                pair[at, T:] = (probs * (raw[at, T:] - delta)).astype(BF)
                dkvf[start + n] += mm(pair[at], rows[...])
                flat = kt[:, pl.ds(pl.multiple_of((start + n) * T, T), T)]
                acc = acc + mm(flat, pair[at, T:])
            return acc

        acc = reach.walk(group, jnp.zeros((HD, T), F32))
        dq[i] = (SCALE * acc).astype(BF)
        return carry

    lax.fori_loop(0, 8, one_block, 0)

    slots = stage.shape[0]

    def put(kb):
        return pltpu.make_async_copy(stage.at[kb % slots], dkv.at[kb], sem.at[kb % slots])

    def flush(kb, carry):
        @pl.when(kb >= slots)
        def _():
            put(kb).wait()

        stage[kb % slots] = dkvf[kb].astype(BF)
        put(kb).start()
        return carry

    def settle(kb, carry):
        put(kb).wait()
        return carry

    lax.fori_loop(0, count, flush, 0)
    lax.fori_loop(0, slots, settle, 0)


def attend_back(Z, causal, info, qt, kv, dt, of, lse):
    T = qt.shape[2]
    count = kv.shape[0]
    slots = count if count <= 32 else 2
    sds = jax.ShapeDtypeStruct
    vmem = pl.BlockSpec(memory_space=pltpu.VMEM)
    return pl.pallas_call(
        functools.partial(attend_back_kernel, Z, causal),
        out_shape=[sds((8, HD, T), BF), sds(kv.shape, BF)],
        in_specs=[pl.BlockSpec(memory_space=pltpu.SMEM)] + [vmem] * 5,
        out_specs=[vmem, pl.BlockSpec(memory_space=pl.ANY)],
        scratch_shapes=[
            pltpu.VMEM((HD, count * T), BF),
            pltpu.VMEM((count, T, 128), F32),
            pltpu.VMEM((128, 2 * T), BF),
            pltpu.VMEM((2 * T, 128), BF),
            pltpu.VMEM((GROUP * T, 2 * T), F32),
            pltpu.VMEM((GROUP * T, 2 * T), BF),
            pltpu.VMEM((slots, T, 128), BF),
            DMA((slots,)),
        ],
        compiler_params=pltpu.CompilerParams(vmem_limit_bytes=room()),
        name="attend_self_back" if causal else "attend_cross_back",
    )(info, qt, kv, dt, of, lse)


def greet_group(heads=False):
    s, z, j, m = place()
    peers = [(None, {"shard": m * 8 + (j + d) % 8}) for d in range(1, 8)]
    if heads:
        peers = peers + [(None, device) for _, _, _, device in kin()]
    greet(peers)


def kin():
    s, z, j, m = place()
    G, Z = lax.axis_size("shard") // 8, lax.axis_size("seq")
    out = []
    for dm in range(G):
        for dz in range(Z):
            if dm or dz:
                om, oz = (m + dm) % G, (z + dz) % Z
                out.append((dm * Z + dz, om, oz, {"shard": om * 8 + j, "seq": oz}))
    return out


def exchange_copies(src, dst, send, recv):
    s, z, j, m = place()
    out = []
    for d in (1, 2, 3, 4, 5, 6, 7):
        p = flip(j, d)
        out.append(rcopy(src.at[p], dst.at[j], send.at[d], recv.at[j], {"shard": m * 8 + p}))
    return out


def exchange_start(src, dst, send, recv):
    s, z, j, m = place()
    for c in exchange_copies(src, dst, send, recv):
        c.start()
    dst[j] = src[j]


def exchange_recv(src, dst, send, recv):
    s, z, j, m = place()
    for d in (1, 2, 3, 4, 5, 6, 7):
        p = flip(j, d)
        rcopy(src.at[p], dst.at[p], send.at[d], recv.at[p], {"shard": m * 8 + p}).wait_recv()


def exchange_sent(src, dst, send, recv):
    for c in exchange_copies(src, dst, send, recv):
        c.wait_send()


class ChipSums:
    def __init__(self, pairs, send, recv):
        self.pairs, self.send, self.recv = pairs, send, recv
        self.s = lax.axis_index("shard")
        self.core = self.s % 2
        self.chips = lax.axis_size("shard") // 2

    def piece(self, a, p):
        full, kept, _ = self.pairs[a]
        rows = kept.shape[1]
        return full.at[pl.ds(pl.multiple_of(p * rows, rows), rows), :]

    def copies(self):
        for a, (_, kept, buf) in enumerate(self.pairs):
            for q in range(self.chips):
                yield rcopy(
                    self.piece(a, 2 * q + 1 - self.core), buf.at[q], self.send.at[a, q], self.recv.at[a, q],
                    {"shard": flip(self.s, 1)},
                )

    def start(self):
        for c in self.copies():
            c.start()

    def finish(self):
        for c in self.copies():
            c.wait_recv()
        for a, (_, kept, buf) in enumerate(self.pairs):
            for q in range(self.chips):
                mine = self.piece(a, 2 * q + self.core)[...]
                kept[q] = (buf[q].astype(F32) + mine.astype(F32)).astype(BF)
        for c in self.copies():
            c.wait_send()


def remote_call(kernel, name, ident, ins, outs, scratch, smem=1, far=(), far_outs=()):
    vmem = pl.BlockSpec(memory_space=pltpu.VMEM)
    in_specs = [pl.BlockSpec(memory_space=pltpu.SMEM)] * smem + [vmem] * (len(ins) - smem)
    out_specs = [vmem] * len(outs)
    for n in far_outs:
        out_specs[n] = pl.BlockSpec(memory_space=pl.ANY)
    for n in far:
        in_specs[n] = pl.BlockSpec(memory_space=pl.ANY)
    return pl.pallas_call(
        kernel,
        out_shape=outs,
        in_specs=in_specs,
        out_specs=out_specs,
        scratch_shapes=scratch,
        compiler_params=pltpu.CompilerParams(
            collective_id=ident, has_side_effects=True, vmem_limit_bytes=room()
        ),
        name=name,
    )(*ins)


def middle_kernel(
    Z, bnd, ot, hid, vecs, wout, wcq, mem, at, after, n2, cqt, mkv, cq_send, s1, r1, s2, r2, s3, r3
):
    s, z, j, m = place()
    T = hid.shape[0]
    greet_group(True)
    exchange_start(ot, at, s1, r1)

    def memory_copies(mine):
        for n, om, oz, device in kin():
            c = m * Z + z if mine else om * Z + oz
            target = mkv.at[m, :, z] if mine else mkv.at[om, :, oz]
            yield rcopy(mem, target, s3.at[n], r3.at[c], device)

    for c in memory_copies(True):
        c.start()
    mkv[m, :, z] = mem[...]
    base = embed(hid, bnd[0], vecs, s * Z + z)
    exchange_recv(ot, at, s1, r1)
    attn = at[...].reshape(512, T).astype(F32).T.astype(BF)
    value = base + mm(attn, wout[...])
    after[...] = value
    hat, _ = norm_stats(value)
    normed = (hat * vecs[3:4, :] + vecs[6:7, :]).astype(BF)
    n2[...] = normed
    cq = mm(normed, wcq[...])
    cq_send[...] = (SCALE * cq.T).astype(BF).reshape(8, HD, T)
    exchange_start(cq_send, cqt, s2, r2)
    exchange_recv(cq_send, cqt, s2, r2)
    for c in memory_copies(False):
        c.wait_recv()
    exchange_sent(ot, at, s1, r1)
    exchange_sent(cq_send, cqt, s2, r2)
    for c in memory_copies(True):
        c.wait_send()


def middle(G, Z, bnd, ot, hid, vecs, wout, wcq, mem):
    T, E = hid.shape[0], mem.shape[1]
    sds = jax.ShapeDtypeStruct
    return remote_call(
        functools.partial(middle_kernel, Z),
        "middle",
        1,
        (bnd, ot, hid, vecs, wout, wcq, mem),
        [
            sds((8, HD, T), BF), sds((T, 512), F32), sds((T, 512), BF), sds((8, HD, T), BF),
            sds((G, 8, Z, E, 128), BF),
        ],
        [
            pltpu.VMEM((8, HD, T), BF), DMA((8,)), DMA((8,)), DMA((8,)), DMA((8,)),
            DMA((G * Z,)), DMA((G * Z,)),
        ],
    )


def erf(x):
    return lax.erf(x)


def feed_kernel(
    crt, after, vecs, upb, wco, wup, wdn, grad, wproj, wmem,
    layer_out, d_after, co_sum, up_sum, dn_sum, smalls, upb_grad, dct, gproj, gmem,
    ct, send, n3t, out_acc, dn_acc, co_grad, up_grad, dn_grad, co_buf, up_buf, dn_buf,
    s1, r1, s2, r2, s3, r3, *whole_sems
):
    T = after.shape[0]
    FF = wup.shape[1]
    S = lax.axis_size("shard")
    s = lax.axis_index("shard")
    greet([(None, {"shard": (s + d) % S}) for d in range(1, S)])
    exchange_start(crt, ct, s1, r1)
    whole = Whole(((wproj, gproj), (wmem, gmem)), S, whole_sems)
    for a in range(2):
        whole.start(a)
    g = grad[...]
    gf = g.astype(F32)
    gt = gf.T.astype(BF)
    exchange_recv(crt, ct, s1, r1)
    cross_t = ct[...].reshape(512, T)
    value = after[...] + mm(cross_t.astype(F32).T.astype(BF), wco[...])
    hat, scale = norm_stats(value)
    normed = hat * vecs[4:5, :] + vecs[7:8, :]
    n3 = normed.astype(BF)
    n3t[...] = n3.astype(F32).T.astype(BF)
    out_acc[...] = value + vecs[9:10, :]
    dn_acc[...] = jnp.zeros_like(dn_acc)
    width = 512
    for c in range(FF // width):
        lo, hi = c * width, (c + 1) * width
        pre = mm(n3, wup[:, lo:hi]) + upb[0:1, lo:hi]
        half = 0.5 * (1.0 + erf(pre * (0.5**0.5)))
        middle_c = (pre * half).astype(BF)
        out_acc[...] += mm(middle_c, wdn[lo:hi, :])
        slope = half + pre * (jnp.exp(-0.5 * pre * pre) * ((0.5 / jnp.pi) ** 0.5))
        d_pre = mm(g, wdn[lo:hi, :], 1, 1) * slope
        d_pre_b = d_pre.astype(BF)
        upb_grad[0:1, lo:hi] = jnp.sum(d_pre_b.astype(F32), axis=0, keepdims=True)
        dn_grad[lo:hi, :] = mm(middle_c.astype(F32).T.astype(BF), g).astype(BF)
        up_grad[:, lo:hi] = mm(n3t[...], d_pre_b).astype(BF)
        dn_acc[...] += mm(d_pre_b, wup[:, lo:hi], 1, 1)
    for a in range(2):
        whole.relay(a)
    layer_out[...] = out_acc[...].astype(BF)
    d_value, d_gain, d_shift = norm_back(dn_acc[...], hat, scale, vecs[4:5, :])
    total = gf + d_value
    d_after[...] = total
    smalls[0:1, :] = d_gain
    smalls[1:2, :] = d_shift
    smalls[2:3, :] = jnp.sum(gf, axis=0, keepdims=True)
    dc = total.astype(BF)
    d_cross = mm(wco[...], dc, 1, 1)
    send[...] = d_cross.astype(BF).reshape(8, HD, T)
    exchange_start(send, dct, s2, r2)
    co_grad[...] = mm(cross_t, dc).astype(BF)
    sums = ChipSums(
        ((co_grad, co_sum, co_buf), (up_grad, up_sum, up_buf), (dn_grad, dn_sum, dn_buf)), s3, r3
    )
    sums.start()
    for a in range(2):
        whole.finish(a)
    exchange_recv(send, dct, s2, r2)
    sums.finish()
    for a in range(2):
        whole.wait(a)
    whole.drain()
    exchange_sent(crt, ct, s1, r1)
    exchange_sent(send, dct, s2, r2)


def feed(crt, after, vecs, upb, wco, wup, wdn, grad, wproj, wmem):
    T, FF = after.shape[0], wup.shape[1]
    S = lax.axis_size("shard")
    chips, R, F = S // 2, 512 // S, FF // S
    sds = jax.ShapeDtypeStruct
    return remote_call(
        feed_kernel,
        "feed_forward",
        2,
        (crt, after, vecs, upb, wco, wup, wdn, grad, wproj, wmem),
        [
            sds((T, 512), BF),
            sds((T, 512), F32),
            sds((chips, R, 512), BF),
            sds((chips, R, FF), BF),
            sds((chips, F, 512), BF),
            sds((8, 512), F32),
            sds((1, FF), F32),
            sds((8, HD, T), BF),
            sds((S,) + wproj.shape, BF),
            sds((S,) + wmem.shape, BF),
        ],
        [
            pltpu.VMEM((8, HD, T), BF),
            pltpu.VMEM((8, HD, T), BF),
            pltpu.VMEM((512, T), BF),
            pltpu.VMEM((T, 512), F32),
            pltpu.VMEM((T, 512), F32),
            pltpu.VMEM((512, 512), BF),
            pltpu.VMEM((512, FF), BF),
            pltpu.VMEM((FF, 512), BF),
            pltpu.VMEM((chips, R, 512), BF),
            pltpu.VMEM((chips, R, FF), BF),
            pltpu.VMEM((chips, F, 512), BF),
            DMA((8,)), DMA((8,)), DMA((8,)), DMA((8,)), DMA((3, chips)), DMA((3, chips)),
        ] + Whole.scratch(2, S),
        smem=0,
        far_outs=(8, 9),
    )


def middle_back_kernel(
    dcqt, after, d_after2, n2, at, vecs, wcq, wout, dmkv,
    d_after, cq_sum, out_sum, smalls, dat, dmem,
    home, send, parts, cq_grad, out_grad, cq_buf, out_buf, s1, r1, s2, r2, s3, r3, s4, r4
):
    s, z, j, m = place()
    G, Z = dmkv.shape[0], dmkv.shape[2]
    T = after.shape[0]
    greet_group(True)
    exchange_start(dcqt, home, s1, r1)

    def memory_copies(mine):
        for n, om, oz, device in kin():
            c = m * Z + z if mine else om * Z + oz
            yield rcopy(dmkv.at[om, :, oz], parts.at[c], s3.at[n], r3.at[c], device)

    for c in memory_copies(True):
        c.start()
    parts[m * Z + z] = dmkv[m, :, z]
    hat, scale = norm_stats(after[...])
    n2t = n2[...].astype(F32).T.astype(BF)
    exchange_recv(dcqt, home, s1, r1)
    dcq = home[...].reshape(512, T).astype(F32).T.astype(BF)
    d_value, d_gain, d_shift = norm_back(mm(dcq, wcq[...], 1, 1), hat, scale, vecs[3:4, :])
    total = d_after2[...] + d_value
    d_after[...] = total
    smalls[0:1, :] = d_gain
    smalls[1:2, :] = d_shift
    da = total.astype(BF)
    send[...] = mm(wout[...], da, 1, 1).astype(BF).reshape(8, HD, T)
    exchange_start(send, dat, s2, r2)
    cq_grad[...] = mm(n2t, dcq).astype(BF)
    out_grad[...] = mm(at[...].reshape(512, T), da).astype(BF)
    sums = ChipSums(((cq_grad, cq_sum, cq_buf), (out_grad, out_sum, out_buf)), s4, r4)
    sums.start()
    for c in memory_copies(False):
        c.wait_recv()
    total_mem = parts[0].astype(F32)
    for n in range(1, G * Z):
        total_mem = total_mem + parts[n].astype(F32)
    dmem[...] = total_mem.astype(BF)
    sums.finish()
    exchange_recv(send, dat, s2, r2)
    exchange_sent(dcqt, home, s1, r1)
    exchange_sent(send, dat, s2, r2)
    for c in memory_copies(True):
        c.wait_send()


def middle_back(dcqt, after, d_after2, n2, at, vecs, wcq, wout, dmkv):
    T = after.shape[0]
    G, _, Z, E, _ = dmkv.shape
    chips, R = 4 * G, 512 // (8 * G)
    sds = jax.ShapeDtypeStruct
    return remote_call(
        middle_back_kernel,
        "middle_back",
        3,
        (dcqt, after, d_after2, n2, at, vecs, wcq, wout, dmkv),
        [
            sds((T, 512), F32),
            sds((chips, R, 512), BF),
            sds((chips, R, 512), BF),
            sds((8, 512), F32),
            sds((8, HD, T), BF),
            sds((8, E, 128), BF),
        ],
        [
            pltpu.VMEM((8, HD, T), BF),
            pltpu.VMEM((8, HD, T), BF),
            pltpu.VMEM((G * Z, 8, E, 128), BF),
            pltpu.VMEM((512, 512), BF),
            pltpu.VMEM((512, 512), BF),
            pltpu.VMEM((chips, R, 512), BF),
            pltpu.VMEM((chips, R, 512), BF),
            DMA((8,)), DMA((8,)), DMA((8,)), DMA((8,)), DMA((G * Z,)), DMA((G * Z,)),
            DMA((2, chips)), DMA((2, chips)),
        ],
        smem=0,
    )


NC = 16


def last_kernel(
    S, Z, G,
    info, hid, vecs, d_after, x_all, enc_all, dqt, dkv, finm, wproj, wmem,
    out_g, cq_g, co_g, up_g, dn_g, small2, small3, upb_g,
    hidden_grad, encoder_grad, zfin, smalls_o,
    got_out, got_cq, got_co, got_up, got_dn,
    rk, fin, mbuf, hkv, hq, hm, turned, enc_turned, dall, psend, pgot, msend, mgot,
    wz, zin, sm_all, sm_z, sm_plane, sm_mine,
    b_s, b_r, k_s, k_r, mb_s, mb_r, hq_s, hq_r, hk_s, hk_r, hm_s, hm_r,
    p_s, p_r, pm_s, pm_r, c_s, c_r, f_s, f_r, sm_s, sm_r, sz_s, sz_r,
):
    s, z, j, m = place()
    T, E = hid.shape[0], enc_all.shape[1]
    R = 512 // S
    F = dn_g.shape[1]
    bound = info[0]
    chips = S // 2
    core, chip = s % 2, s // 2
    sib = flip(s, 1)
    ends = (Z - 1, 0)
    greet(
        [(None, {"shard": (s + d) % S}) for d in range(1, S)]
        + [(None, {"seq": (z + d) % Z}) for d in range(1, Z)]
    )
    sums = (out_g, cq_g, co_g, up_g, dn_g)
    gots = (got_out, got_cq, got_co, got_up, got_dn)

    if G > 1:
        for d in range(1, G):
            o = (m + d) % G
            rcopy(dkv.at[o], mbuf.at[m], mb_s.at[d, 0], mb_r.at[m, 0], {"shard": o * 8 + j}).start()
        own_part = pltpu.make_async_copy(dkv.at[m], mbuf.at[m], mb_s.at[0, 0])
        own_part.start()
        own_part.wait()
        for d in range(1, G):
            o = (m + d) % G
            rcopy(dkv.at[o], mbuf.at[o], mb_s.at[d, 0], mb_r.at[o, 0], {"shard": o * 8 + j}).wait_recv()
        for b in range(8):
            acc = mbuf[m, b].astype(F32)
            for d in range(1, G):
                acc = acc + mbuf[(m + d) % G, b].astype(F32)
            mbuf[m, b] = acc.astype(BF)
        part = mbuf.at[m]
    else:
        part = dkv.at[0]

    def z_view(slot, t):
        return part.at[slot, t]

    def z_buffer(way, t, slot):
        return rk.at[way, t, slot]

    def z_copy(way, t, slot, source):
        step = 2 * way - 1
        return rcopy(
            source, z_buffer(way, t, slot), k_s.at[way, t, slot], k_r.at[way, t, slot], {"seq": z + step}
        )

    for far in range(Z - 1, 0, -1):
        for slot in range(8):
            for way in (0, 1):
                t = z + (2 * way - 1) * far

                @pl.when((z == ends[way]) & (t >= 0) & (t < Z))
                def _(way=way, t=t, slot=slot):
                    z_copy(way, t, slot, z_view(slot, t)).start()

    def own_copy(a, q):
        return rcopy(
            sums[a].at[q], gots[a].at[chip], b_s.at[a, q], b_r.at[a, chip], {"shard": 2 * q + core}
        )

    for a in range(5):
        for d in range(1, chips):
            own_copy(a, (chip + d) % chips).start()
    exchange_start(dqt, hq, hq_s, hq_r)
    exchange_start(finm, hm, hm_s, hm_r)

    def turn_block(b):
        turned[:, b * T : (b + 1) * T] = x_all[b].astype(F32).T.astype(BF)

    def turn_query(b):
        dq_b = dqt[b].astype(F32)
        dall[b * T : (b + 1) * T, 128:] = (
            jnp.concatenate([dq_b, jnp.zeros_like(dq_b)], axis=0).T.astype(BF)
        )

    def turn_encoder():
        enc_turned[...] = enc_all[...].reshape(8 * E, 512).astype(F32).T.astype(BF)

    def own_sum(a):
        for d in range(1, chips):
            q = (chip + d) % chips
            rcopy(sums[a].at[q], gots[a].at[q], b_s.at[a, q], b_r.at[a, q], {"shard": 2 * q + core}).wait_recv()
        total = sums[a][chip].astype(F32)
        for d in range(1, chips):
            total = total + gots[a][(chip + d) % chips].astype(F32)
        total = total.astype(BF)
        if a < 3:
            wz[a] = total
        elif a == 3:
            for c in range(4):
                wz[3 + c] = total[:, 512 * c : 512 * (c + 1)]
        else:
            for c in range(4):
                wz[7 + c] = total[c * R : (c + 1) * R]

    block = s * Z + z
    work = [functools.partial(turn_block, b) for b in range(8)]
    work += [functools.partial(turn_query, b) for b in range(8)] + [turn_encoder]

    for far in range(Z - 1, 0, -1):
        for slot in range(8):
            if work:
                work.pop(0)()
            for way in (0, 1):
                t = z + (2 * way - 1) * far

                @pl.when((z != ends[way]) & (t >= 0) & (t < Z))
                def _(way=way, t=t, slot=slot):
                    z_copy(way, t, slot, z_view(slot, t)).wait_recv()
                    buf = z_buffer(way, t, slot)
                    buf[...] = (
                        buf[...].astype(F32) + z_view(slot, t)[...].astype(F32)
                    ).astype(BF)
                    z_copy(way, t, slot, buf).start()

    def inward(k, step):
        way = (step + 1) // 2
        return rcopy(wz.at[k], zin.at[way, k], c_s.at[way, k], c_r.at[way, k], {"seq": z + step})

    def outward(k, step):
        return rcopy(zfin.at[k], zfin.at[k], f_s.at[(step + 1) // 2, k], f_r.at[k], {"seq": z + step})

    def root(k):
        return max(Z // 2 - 1 + k % 2, 0) if Z > 1 else 0

    def tips(k):
        r = root(k)
        for step in (-1, 1):
            tip = ends[(step + 1) // 2]
            if tip != r:

                @pl.when(z == tip)
                def _(step=step):
                    inward(k, step).start()

    def partial(k):
        r = root(k)
        for step, beyond in ((-1, z > r), (1, z < r)):
            tip = ends[(step + 1) // 2]
            way = (step + 1) // 2

            @pl.when(beyond & (z != tip))
            def _(step=step, way=way):
                inward(k, step).wait_recv()
                wz[k] = (wz[k].astype(F32) + zin[way, k].astype(F32)).astype(BF)
                inward(k, step).start()

    def total_of(k):
        r = root(k)

        @pl.when(z == r)
        def _():
            total = wz[k].astype(F32)
            if r < Z - 1:
                inward(k, -1).wait_recv()
                total = total + zin[0, k].astype(F32)
            if r > 0:
                inward(k, 1).wait_recv()
                total = total + zin[1, k].astype(F32)
            zfin[k] = total.astype(BF)
            if r < Z - 1:
                outward(k, 1).start()
            if r > 0:
                outward(k, -1).start()

    def send_out(k):
        r = root(k)
        for step, beyond in ((1, z > r), (-1, z < r)):
            tip = Z - 1 if step > 0 else 0

            @pl.when(beyond)
            def _(step=step, tip=tip):
                outward(k, step).wait_recv()

                @pl.when(z != tip)
                def _():
                    outward(k, step).start()

    for task in work:
        task()
    psend_q = mm(turned[...], dall[:, 128:])
    for a in range(5):
        own_sum(a)
        for k in ((0,), (1,), (2,), (3, 4, 5, 6), (7, 8, 9, 10))[a]:
            tips(k)
    hat, scale = norm_stats(embed(hid, bound, vecs, block))

    for slot in range(8):
        for way in (0, 1):

            @pl.when(z != ends[way])
            def _(way=way, slot=slot):
                z_copy(way, z, slot, z_view(slot, z)).wait_recv()

        low = jnp.where(z == ends[0], 0.0, z_buffer(0, z, slot)[...].astype(F32))
        high = jnp.where(z == ends[1], 0.0, z_buffer(1, z, slot)[...].astype(F32))
        total = (low + high + z_view(slot, z)[...].astype(F32)).astype(BF)
        fin[slot] = total
        dall[slot * T : (slot + 1) * T, :128] = total
    exchange_start(fin, hkv, hk_s, hk_r)
    for k in range(3):
        partial(k)

    psend_kv = mm(turned[...], dall[:, :128])
    psend[...] = jnp.concatenate([psend_kv, psend_q], axis=1).astype(BF).reshape(S, R, 256)
    msend[...] = mm(enc_turned[...], finm[...].reshape(8 * E, 128)).astype(BF).reshape(S, R, 128)
    pgot[s] = psend[s]
    mgot[s] = msend[s]
    for d in range(1, S):
        p = (s + d) % S
        rcopy(psend.at[p], pgot.at[s], p_s.at[d], p_r.at[s], {"shard": p}).start()
        rcopy(msend.at[p], mgot.at[s], pm_s.at[d], pm_r.at[s], {"shard": p}).start()

    for k in range(3):
        total_of(k)
    for k in range(3, 6):
        partial(k)

    exchange_recv(dqt, hq, hq_s, hq_r)
    exchange_recv(fin, hkv, hk_s, hk_r)
    exchange_recv(finm, hm, hm_s, hm_r)
    d_query = hq[...].reshape(512, T).astype(F32).T.astype(BF)
    d_keys = jnp.concatenate([hkv[h][:, :HD] for h in range(H)], axis=1)
    d_values = jnp.concatenate([hkv[h][:, HD:] for h in range(H)], axis=1)
    d_norm = (
        mm(d_query, wproj[:, :512], 1, 1)
        + mm(d_keys, wproj[:, 512:1024], 1, 1)
        + mm(d_values, wproj[:, 1024:], 1, 1)
    )
    d_value, d_gain, d_shift = norm_back(d_norm, hat, scale, vecs[2:3, :])
    total = d_after[...] + d_value
    hidden_grad[...] = total
    pos = block * T + lax.broadcasted_iota(jnp.int32, (T, 1), 0)
    sm_mine[...] = jnp.zeros((16, 512), F32)
    sm_mine[0:1, :] = d_gain
    sm_mine[1:2, :] = small2[0:1, :]
    sm_mine[2:3, :] = small3[0:1, :]
    sm_mine[3:4, :] = d_shift
    sm_mine[4:5, :] = small2[1:2, :]
    sm_mine[5:6, :] = small3[1:2, :]
    sm_mine[6:7, :] = jnp.sum(jnp.where(pos < bound, total, 0.0), axis=0, keepdims=True)
    sm_mine[7:8, :] = jnp.sum(jnp.where(pos < bound, 0.0, total), axis=0, keepdims=True)
    sm_mine[8:9, :] = small3[2:3, :]
    for c in range(upb_g.shape[1] // 512):
        sm_mine[9 + c : 10 + c, :] = upb_g[0:1, 512 * c : 512 * (c + 1)]
    for d in range(1, S):
        rcopy(sm_mine, sm_all.at[s], sm_s.at[d], sm_r.at[s], {"shard": (s + d) % S}).start()
    sm_all[s] = sm_mine[...]

    for k in range(6, 11):
        partial(k)
        total_of(k - 3)

    for d in range(1, S):
        p = (s + d) % S
        rcopy(psend.at[p], pgot.at[p], p_s.at[d], p_r.at[p], {"shard": p}).wait_recv()
        rcopy(msend.at[p], mgot.at[p], pm_s.at[d], pm_r.at[p], {"shard": p}).wait_recv()
    heads, mheads = [], []
    for h in range(H):
        acc, accm = pgot[h].astype(F32), mgot[h].astype(F32)
        for g in range(1, G):
            acc = acc + pgot[8 * g + h].astype(F32)
            accm = accm + mgot[8 * g + h].astype(F32)
        heads.append(acc)
        mheads.append(accm)
    wz[11] = jnp.concatenate([v[:, 128 : 128 + HD] for v in heads], axis=1).astype(BF)
    wz[12] = jnp.concatenate([v[:, :HD] for v in heads], axis=1).astype(BF)
    wz[13] = jnp.concatenate([v[:, HD:128] for v in heads], axis=1).astype(BF)
    wz[14] = jnp.concatenate([v[:, :HD] for v in mheads], axis=1).astype(BF)
    wz[15] = jnp.concatenate([v[:, HD:] for v in mheads], axis=1).astype(BF)
    for k in range(11, NC):
        tips(k)
    for k in range(8, 11):
        total_of(k)
    for k in range(6):
        send_out(k)
    for k in range(11, NC):
        partial(k)
    e_keys = jnp.concatenate([hm[h][:, :HD] for h in range(H)], axis=1)
    e_values = jnp.concatenate([hm[h][:, HD:] for h in range(H)], axis=1)
    encoder_grad[...] = mm(e_keys, wmem[:, :512], 1, 1) + mm(e_values, wmem[:, 512:], 1, 1)

    for d in range(1, S):
        p = (s + d) % S
        rcopy(sm_mine, sm_all.at[p], sm_s.at[d], sm_r.at[p], {"shard": p}).wait_recv()
    acc = sm_all[0]
    for p in range(1, S):
        acc = acc + sm_all[p]
    sm_plane[...] = acc
    for d in range(1, Z):
        rcopy(sm_plane, sm_z.at[z], sz_s.at[d], sz_r.at[z], {"seq": (z + d) % Z}).start()
    sm_z[z] = acc
    for k in range(11, NC):
        total_of(k)
        send_out(k - 5)
    for k in range(11, NC):
        send_out(k)
    for d in range(1, Z):
        o = (z + d) % Z
        rcopy(sm_plane, sm_z.at[o], sz_s.at[d], sz_r.at[o], {"seq": o}).wait_recv()
    acc = sm_z[0]
    for o in range(1, Z):
        acc = acc + sm_z[o]
    smalls_o[...] = acc

    for a in range(5):
        for d in range(1, chips):
            own_copy(a, (chip + d) % chips).wait_send()
    for d in range(1, G):
        o = (m + d) % G
        rcopy(dkv.at[o], mbuf.at[m], mb_s.at[d, 0], mb_r.at[m, 0], {"shard": o * 8 + j}).wait_send()
    exchange_sent(dqt, hq, hq_s, hq_r)
    exchange_sent(fin, hkv, hk_s, hk_r)
    exchange_sent(finm, hm, hm_s, hm_r)
    for far in range(Z - 1, 0, -1):
        for slot in range(8):
            for way in (0, 1):
                t = z + (2 * way - 1) * far

                @pl.when((t >= 0) & (t < Z))
                def _(way=way, t=t, slot=slot):
                    z_copy(way, t, slot, z_view(slot, t)).wait_send()

    for d in range(1, S):
        p = (s + d) % S
        rcopy(psend.at[p], pgot.at[s], p_s.at[d], p_r.at[s], {"shard": p}).wait_send()
        rcopy(msend.at[p], mgot.at[s], pm_s.at[d], pm_r.at[s], {"shard": p}).wait_send()
        rcopy(sm_mine, sm_all.at[s], sm_s.at[d], sm_r.at[s], {"shard": p}).wait_send()
    for d in range(1, Z):
        rcopy(sm_plane, sm_z.at[z], sz_s.at[d], sz_r.at[z], {"seq": (z + d) % Z}).wait_send()
    for k in range(NC):
        r = root(k)
        for step, beyond in ((-1, z > r), (1, z < r)):

            @pl.when(beyond)
            def _(step=step):
                inward(k, step).wait_send()

        for step in (-1, 1):
            sends = (z >= r) & (z < Z - 1) if step > 0 else (z <= r) & (z > 0)

            @pl.when(sends)
            def _(step=step):
                outward(k, step).wait_send()


def finish_kernel(
    info, timestep, zfin, sums, hid_g, enc_g, lay,
    lay_o, hid_o, enc_o, time_o, gain_o, shift_o, proj_o, out_o, cq_o, mem_o, co_o, up_o, upb_o, dn_o, dnb_o,
):
    s = info[3]
    R, F = out_o.shape[0], upb_o.shape[1]
    lay_o[...] = lay[...]
    hid_o[...] = hid_g[...]
    enc_o[...] = enc_g[...]
    out_o[...] = zfin[0].astype(F32)
    cq_o[...] = zfin[1].astype(F32)
    co_o[...] = zfin[2].astype(F32)
    for c in range(4):
        up_o[:, 512 * c : 512 * (c + 1)] = zfin[3 + c].astype(F32)
        dn_o[c * R : (c + 1) * R, :] = zfin[7 + c].astype(F32)
    for c in range(3):
        proj_o[:, 512 * c : 512 * (c + 1)] = zfin[11 + c].astype(F32)
    for c in range(2):
        mem_o[:, 512 * c : 512 * (c + 1)] = zfin[14 + c].astype(F32)

    def own(width, first):
        row = lax.broadcasted_iota(jnp.int32, (512, width), 0)
        col = lax.broadcasted_iota(jnp.int32, (512, width), 1)
        pick = jnp.where(row == col + first, 1.0, 0.0)
        return lax.dot_general(
            sums[...], pick, (((1,), (0,)), ((), ())),
            preferred_element_type=F32, precision=lax.Precision.HIGHEST,
        )

    mine = own(R, s * R)
    gain_o[...] = mine[0:3]
    shift_o[...] = mine[3:6]
    dnb_o[...] = mine[8:9]
    step = lax.broadcasted_iota(jnp.int32, time_o.shape, 0)
    grad = jnp.zeros(time_o.shape, F32)
    for d in range(DOCS):
        grad = grad + jnp.where(step == timestep[d], mine[6 + d : 7 + d], 0.0)
    time_o[...] = grad
    wide = own(F, (s * F) % 512)
    row = lax.broadcasted_iota(jnp.int32, wide.shape, 0)
    upb_o[...] = jnp.sum(jnp.where(row == 9 + s * F // 512, wide, 0.0), axis=0, keepdims=True)


def last(v):
    S, Z, G = v["S"], v["Z"], v["G"]
    T, R, F, E = v["T"], v["R"], v["F"], v["encoder"].shape[0]
    FF = v["wup"].shape[1]
    chips = S // 2
    sds = jax.ShapeDtypeStruct
    V = pltpu.VMEM
    GM, ZM = (G, Z) if G > 1 else (1, 1)
    hidden_grad, encoder_grad, zfin, sums = remote_call(
        functools.partial(last_kernel, S, Z, G),
        "gradients_home",
        4,
        (
            v["info"], v["hidden_in"], v["vecs"], v["d_after"], v["x_all"], v["enc_all"], v["dqt"],
            v["dkv"].reshape(G, 8, Z, T, 128), v["dmem"],
            v["gproj"].reshape(512, 1536), v["gmem"].reshape(512, 1024),
            v["wout_grad"], v["cq_grad"], v["co_grad"], v["up_grad"], v["dn_grad"],
            v["small2"], v["small3"], v["upb_grad"],
        ),
        [sds((T, 512), F32), sds((E, 512), F32), sds((NC, R, 512), BF), sds((16, 512), F32)],
        [V((chips, R, 512), BF)] * 3 + [V((chips, R, FF), BF), V((chips, F, 512), BF)]
        + [
            V((2, Z, 8, T, 128), BF), V((8, T, 128), BF), V((GM, 8, ZM, T, 128), BF),
            V((8, T, 128), BF), V((8, HD, T), BF), V((8, E, 128), BF),
            V((512, 8 * T), BF), V((512, 8 * E), BF), V((8 * T, 256), BF),
            V((S, R, 256), BF), V((S, R, 256), BF), V((S, R, 128), BF), V((S, R, 128), BF),
            V((NC, R, 512), BF), V((2, NC, R, 512), BF),
            V((S, 16, 512), F32), V((Z, 16, 512), F32), V((16, 512), F32), V((16, 512), F32),
            DMA((5, chips)), DMA((5, chips)),
            DMA((2, Z, 8)), DMA((2, Z, 8)), DMA((G, 1)), DMA((G, 1)),
            DMA((8,)), DMA((8,)), DMA((8,)), DMA((8,)), DMA((8,)), DMA((8,)),
            DMA((S,)), DMA((S,)), DMA((S,)), DMA((S,)),
            DMA((2, NC)), DMA((2, NC)), DMA((2, NC)), DMA((NC,)),
            DMA((S,)), DMA((S,)), DMA((Z,)), DMA((Z,)),
        ],
        far=(7,) if G > 1 else (),
    )
    vmem = pl.BlockSpec(memory_space=pltpu.VMEM)
    smem = pl.BlockSpec(memory_space=pltpu.SMEM)
    steps = v["time_table"].shape[0]
    outs = [
        sds((T, 512), BF), sds((T, 512), F32), sds((E, 512), F32), sds((steps, R), F32), sds((3, R), F32),
        sds((3, R), F32), sds((R, 1536), F32), sds((R, 512), F32), sds((R, 512), F32), sds((R, 1024), F32),
        sds((R, 512), F32), sds((R, FF), F32), sds((1, F), F32), sds((F, 512), F32), sds((1, R), F32),
    ]
    res = pl.pallas_call(
        finish_kernel,
        out_shape=outs,
        in_specs=[smem, smem] + [vmem] * 5,
        out_specs=[vmem] * len(outs),
        compiler_params=pltpu.CompilerParams(vmem_limit_bytes=room()),
        name="outputs",
    )(v["info"], v["timestep"], zfin, sums, hidden_grad, encoder_grad, v["layer_out"])
    res = list(res)
    res[12] = res[12].reshape(F)
    res[14] = res[14].reshape(R)
    return tuple(res)


def shards(
    hidden_in, encoder, segment_ids, timestep, out_grad, time_table, norm_gain, norm_bias,
    self_proj, self_out, cross_query, cross_memory, cross_out, up_weight, up_bias, down_weight, down_bias,
):
    S, Z = lax.axis_size("shard"), lax.axis_size("seq")
    T, R, F = hidden_in.shape[0], self_proj.shape[0], up_bias.shape[0]
    G = S // 8
    info, x_all, kv, qt, mem, enc_all, vecs, upb, gout, gcq, gco, gup, gdn = gather_call(
        S,
        Z,
        (
            timestep, segment_ids.reshape(-1, 128), hidden_in, time_table, norm_gain, norm_bias,
            up_bias, down_bias, self_proj, cross_memory, encoder,
            self_out, cross_query, cross_out, up_weight, down_weight,
        ),
    )
    wout, wcq, wco = gout.reshape(512, 512), gcq.reshape(512, 512), gco.reshape(512, 512)
    wup, wdn = gup.reshape(512, -1), gdn.reshape(-1, 512)
    kv = kv.reshape(S * Z, T, 128)

    ot, of, lse = attend(Z, True, info, qt, kv)
    at, after, n2, cqt, mkv = middle(G, Z, info, ot, hidden_in, vecs, wout, wcq, mem)
    mkv = mkv.reshape(DOCS * ENC // T, T, 128)
    crt, crf, clse = attend(Z, False, info, cqt, mkv)
    layer_out, d_after2, co_grad, up_grad, dn_grad, small3, upb_grad, dct, gproj, gmem = feed(
        crt, after, vecs, upb, wco, wup, wdn, out_grad, self_proj, cross_memory
    )
    dcqt, dmkv = attend_back(Z, False, info, cqt, mkv, dct, crf, clse)
    d_after, cq_grad, wout_grad, small2, dat, dmem = middle_back(
        dcqt, after, d_after2, n2, at, vecs, wcq, wout, dmkv.reshape(G, 8, Z, -1, 128)
    )
    dqt, dkv = attend_back(Z, True, info, qt, kv, dat, of, lse)
    return last(locals())


def solution(mesh):
    return jax.shard_map(
        shards,
        mesh=mesh,
        in_specs=(
            P(("shard", "seq"), None),
            P(("shard", "seq"), None),
            P(),
            P(),
            P(("shard", "seq"), None),
            P(None, "shard"),
            P(None, "shard"),
            P(None, "shard"),
            P("shard", None),
            P("shard", None),
            P("shard", None),
            P("shard", None),
            P("shard", None),
            P("shard", None),
            P("shard"),
            P("shard", None),
            P("shard"),
        ),
        out_specs=(
            P(("shard", "seq"), None),
            P(("shard", "seq"), None),
            P(("shard", "seq"), None),
            P(None, "shard"),
            P(None, "shard"),
            P(None, "shard"),
            P("shard", None),
            P("shard", None),
            P("shard", None),
            P("shard", None),
            P("shard", None),
            P("shard", None),
            P("shard"),
            P("shard", None),
            P("shard"),
        ),
        check_vma=False,
    )
```
